32 devices in a mesh: seq: 4 (over y, x), dp: 8 (over z, core).
Axes of the slice: x: 2, y: 2, z: 4, core: 2. Of those that a mesh axis runs over, the one named last changes fastest.
Arguments:
- tokens: bfloat16 [16, 1024, 768], P('dp', 'seq'), may hold values from -6 to 6
- lengths: int32 [16], P('dp'), may hold values from 512 to 1024, as said below
- random_features: float32 [64, 256], replicated, may hold values from -6 to 6
- w_query: bfloat16 [768, 768], P(None, 'dp'), may hold values from -0.21875 to 0.21875
- w_key: bfloat16 [768, 768], P(None, 'dp'), may hold values from -0.21875 to 0.21875
- w_value: bfloat16 [768, 768], P(None, 'dp'), may hold values from -0.21875 to 0.21875
- w_output: bfloat16 [768, 768], P(None, 'dp'), may hold values from -3.5 to 3.5
- w_in: bfloat16 [768, 3072], P(None, 'dp'), may hold values from -0.21875 to 0.21875
- w_out: bfloat16 [3072, 768], P(None, 'dp'), may hold values from -0.109375 to 0.109375
- ln1_gain: bfloat16 [768], P('dp'), may hold values from 0.099609375 to 1.8984375
- ln1_bias: bfloat16 [768], P('dp'), may hold values from -3 to 3
- ln2_gain: bfloat16 [768], P('dp'), may hold values from 0.099609375 to 1.8984375
- ln2_bias: bfloat16 [768], P('dp'), may hold values from -3 to 3
- cotangent: bfloat16 [16, 1024, 768], P('dp', 'seq'), may hold values from -6 to 6
Outputs:
- layer_out: bfloat16 [16, 1024, 768], P('dp', 'seq')
- tokens_grad: float32 [16, 1024, 768], P('dp', 'seq')
- w_query_grad: float32 [768, 768], P(None, 'dp')
- w_key_grad: float32 [768, 768], P(None, 'dp')
- w_value_grad: float32 [768, 768], P(None, 'dp')
- w_output_grad: float32 [768, 768], P(None, 'dp')
- w_in_grad: float32 [768, 3072], P(None, 'dp')
- w_out_grad: float32 [3072, 768], P(None, 'dp')
- ln1_gain_grad: float32 [768], P('dp')
- ln1_bias_grad: float32 [768], P('dp')
- ln2_gain_grad: float32 [768], P('dp')
- ln2_bias_grad: float32 [768], P('dp')
The draws below stay inside these ranges and needn't reach their ends.
Inputs may be any that keep to these rules, and one draw needn't show every extreme that they name: `lengths`: every sequence holds between 512 and 1024 valid tokens at its start; both ends occur.
All inputs are finite; a program needn't handle non-finite values.
Results may differ from the reference program's by a relative error of at most 0.015.
The reference program's roundings to bfloat16 on the way count: a program that leaves them out, or rounds other values in their place, can miss the bound.
Values may be sent and summed in bfloat16 or wider, within the bound.
A program may use at most 192 MiB of HBM per device.

```python
from functools import partial
import jax
import jax.numpy as jnp
from jax import lax

D = 768
HEADS = 12
HEAD = 64
FF = 3072
FEAT = 256
L = 1024
BATCH = 16


def draw_lengths(key, part):
    values = jax.random.randint(key, (BATCH,), L // 2, L + 1)
    values = values.at[0].set(L)
    values = values.at[1].set(L // 2)
    return values.astype(jnp.int32)


def block_levels(stream_key, shape, cuts, low, high):
    level, own = 1.0, jax.random.fold_in(stream_key, 6)
    for axis_at, blocks in cuts:
        steps = jnp.exp(jax.random.uniform(jax.random.fold_in(own, axis_at), (blocks,), jnp.float32, low / len(cuts), high / len(cuts)))
        level = level * jnp.repeat(steps, shape[axis_at] // blocks).reshape([-1 if axis == axis_at else 1 for axis in range(len(shape))])
    return level


def normal_values(key, dims, deviation, bound, pieces=(), held_as=jnp.bfloat16):
    factor_of = block_levels(key, dims, pieces, -0.22, 0.18) if pieces else 1.0
    values = jax.random.normal(key, dims, jnp.float32) * deviation * factor_of
    return jnp.minimum(jnp.maximum(values, -bound), bound).astype(held_as)


def setup_inputs(seed: int = 0) -> dict:
    splits = jax.random.split(jax.random.key(seed), 15)
    return {
        "tokens": normal_values(splits[0], (BATCH, L, D), 1.0, 6.0, ((0, 8), (1, 4))),
        "lengths": draw_lengths(jax.random.fold_in(splits[14], 71), 0),
        "random_features": normal_values(splits[2], (HEAD, FEAT), 1.0, 6.0, (), jnp.float32),
        "w_query": normal_values(splits[3], (D, D), D ** -0.5, 0.21875, ((1, 8),)),
        "w_key": normal_values(splits[4], (D, D), D ** -0.5, 0.21875, ((1, 8),)),
        "w_value": normal_values(splits[5], (D, D), D ** -0.5, 0.21875, ((1, 8),)),
        "w_output": normal_values(splits[6], (D, D), 3 ** -0.5, 3.5, ((1, 8),)),
        "w_in": normal_values(splits[7], (D, FF), D ** -0.5, 0.21875, ((1, 8),)),
        "w_out": normal_values(splits[8], (FF, D), FF ** -0.5, 0.109375, ((1, 8),)),
        "ln1_gain": jnp.clip(1.0 + 0.18 * jax.random.normal(splits[9], (D,), jnp.float32), 0.099609375, 1.8984375).astype(jnp.bfloat16),
        "ln1_bias": normal_values(splits[10], (D,), 0.5, 3.0, ((0, 8),)),
        "ln2_gain": jnp.clip(1.0 + 0.18 * jax.random.normal(splits[11], (D,), jnp.float32), 0.099609375, 1.8984375).astype(jnp.bfloat16),
        "ln2_bias": normal_values(splits[12], (D,), 0.5, 3.0, ((0, 8),)),
        "cotangent": normal_values(splits[13], (BATCH, L, D), 1.0, 6.0, ((0, 8), (1, 4))),
    }


highest = lax.Precision.HIGHEST
norm_epsilon = 1e-12

@jax.custom_vjp
def low(v):
    return lax.optimization_barrier(v.astype(jnp.bfloat16)).astype(jnp.float32)

@jax.custom_vjp
def low_back(v):
    return v

def low_keep(v):
    return (low(v), None)

def low_pass(kept, grad):
    return (grad,)

def back_keep(v):
    return (v, None)

def back_low(kept, grad):
    return (low(grad),)
low.defvjp(low_keep, low_pass)
low_back.defvjp(back_keep, back_low)

def layer_norm(row_block, gain_vec, bias_vec):
    mean_val = lax.optimization_barrier(jnp.mean(row_block, -1, keepdims=True))
    centered = row_block - mean_val
    inv_std = lax.rsqrt(lax.optimization_barrier(jnp.mean(centered * centered, -1, keepdims=True)) + norm_epsilon)
    return centered * inv_std * gain_vec + bias_vec

def feature_map(projected, random_features):
    scaled = projected * HEAD ** (-0.25)
    projection = jnp.einsum('glhe,em->glhm', scaled, random_features, precision=highest)
    return jnp.exp(projection - 0.5 * lax.optimization_barrier(jnp.sum(scaled * scaled, -1, keepdims=True)))

def forward_pass(weights_f32, group_tokens, group_lengths, random_features):
    w_query, w_key, w_value, w_output, w_in, w_out, gain1, bias1, gain2, bias2 = weights_f32
    count = group_tokens.shape[0]
    positions = jnp.arange(L, dtype=jnp.int32)
    row_valid = (positions[None, :] < group_lengths[:, None]).astype(jnp.float32)

    def project(matrix):
        return low(low_back(jnp.einsum('gld,de->gle', group_tokens, matrix, precision=highest)))
    queries = project(w_query).reshape(count, L, HEADS, HEAD)
    key_proj = project(w_key).reshape(count, L, HEADS, HEAD)
    value_proj = project(w_value).reshape(count, L, HEADS, HEAD)
    q_feat = feature_map(queries, random_features)
    k_feat = feature_map(key_proj, random_features) * row_valid[:, :, None, None]
    key_state = jnp.einsum('glhm,glhe->ghme', k_feat, value_proj, precision=highest)
    key_total = lax.optimization_barrier(jnp.sum(k_feat, 1))
    numerator = jnp.einsum('glhm,ghme->glhe', q_feat, key_state, precision=highest)
    denominator = jnp.einsum('glhm,ghm->glh', q_feat, key_total, precision=highest)
    context = low(low_back(numerator / denominator[..., None])).reshape(count, L, D)
    attn_out = low_back(jnp.einsum('gld,de->gle', context, w_output, precision=highest))
    hidden = layer_norm(group_tokens + attn_out, gain1, bias1)
    pre_act = low_back(jnp.einsum('gld,df->glf', low(hidden), w_in, precision=highest))
    activated = low(jax.nn.gelu(pre_act, approximate=False))
    ffn_out = low_back(jnp.einsum('glf,fd->gld', activated, w_out, precision=highest))
    return layer_norm(hidden + ffn_out, gain2, bias2) * row_valid[:, :, None]

def reference(tokens, lengths, random_features, w_query, w_key, w_value, w_output, w_in, w_out, ln1_gain, ln1_bias, ln2_gain, ln2_bias, cotangent):
    weights_f32 = (w_query.astype(jnp.float32), w_key.astype(jnp.float32), w_value.astype(jnp.float32), w_output.astype(jnp.float32), w_in.astype(jnp.float32), w_out.astype(jnp.float32), ln1_gain.astype(jnp.float32), ln1_bias.astype(jnp.float32), ln2_gain.astype(jnp.float32), ln2_bias.astype(jnp.float32))
    group_count = BATCH // 4
    tok_groups = tokens.astype(jnp.float32).reshape(group_count, 4, L, D)
    cot_groups = cotangent.astype(jnp.float32).reshape(group_count, 4, L, D)
    len_groups = lengths.reshape(group_count, 4)

    def group_step(running, group_data):
        group_tokens, group_lengths, group_cot = group_data
        bound_forward = partial(forward_pass, group_lengths=group_lengths, random_features=random_features)
        layer_out, pullback = jax.vjp(bound_forward, weights_f32, group_tokens)
        weight_grads, token_grads = pullback(group_cot)
        running = jax.tree.map(jnp.add, running, weight_grads)
        return (running, (layer_out.astype(jnp.bfloat16), token_grads))
    zero_grads = tuple((jnp.zeros_like(item) for item in weights_f32))
    summed, (outputs, token_grads) = lax.scan(group_step, zero_grads, (tok_groups, len_groups, cot_groups))
    return (outputs.reshape(BATCH, L, D), token_grads.reshape(BATCH, L, D), summed[0], summed[1], summed[2], summed[3], summed[4], summed[5], summed[6], summed[7], summed[8], summed[9])
```

```python
import functools
from functools import partial

import jax
import jax.numpy as jnp
from jax import lax
from jax.experimental import pallas as pl
from jax.experimental.pallas import tpu as pltpu
from jax.sharding import PartitionSpec as P

MESH = pl.DeviceIdType.MESH
bf = jnp.bfloat16


def coords():
    s, d = lax.axis_index("seq"), lax.axis_index("dp")
    return s // 2, s % 2, d // 2, d % 2

def dev(y, x, z, c):
    return (y * 2 + x, z * 2 + c)

def entry_barrier(peers):
    sem = pltpu.get_barrier_semaphore()
    for p in peers:
        pl.semaphore_signal(sem, inc=1, device_id=p, device_id_type=MESH)
    pl.semaphore_wait(sem, len(peers))

def piece(g, ref, d, y, x):
    if g < 2:  return ref.at[y, d, x]
    if g == 2: return ref.at[d, y, x]
    return ref.at[y, x, d]
def lpiece(g, ref, y, x):
    return ref.at[y, x]
def shard(g, ref, d):
    if g < 2:  return ref.at[:, d]
    if g == 2: return ref.at[d]
    return ref.at[:, :, d]

def ag_kernel(nz, *refs):
    loc, out, sems = refs[:4], refs[4:8], refs[8:]
    zs, zr, xs, xr, ys, yr, ds_, dr, ss, sr, ls = sems
    y, x, z, c = coords()
    ynb, xnb, sib = dev(1 - y, x, z, c), dev(y, 1 - x, z, c), dev(y, x, z, 1 - c)
    zpeer = [dev(y, x, (z + k) % nz, c) for k in range(1, nz)]
    entry_barrier([ynb, xnb, sib] + zpeer)
    half = loc[0].shape[-1] // 2
    H = (pl.ds(0, half), pl.ds(half, half))
    me = z * 2 + c
    started = []
    def rc(src, dst, ssem, rsem, to):
        cp = pltpu.make_async_remote_copy(src_ref=src, dst_ref=dst, send_sem=ssem, recv_sem=rsem, device_id=to, device_id_type=MESH)
        return cp
    def go(cp):
        cp.start(); started.append(cp)
    def recv(dst, ssem, rsem, to):
        rc(dst, dst, ssem, rsem, to).wait_recv()
    G = range(4)
    for g in G:
        for k in range(1, nz):
            go(rc(lpiece(g, loc[g], y, x), piece(g, out[g], me, y, x), zs.at[g, k-1], zr.at[g, k-1], zpeer[k-1]))
        go(rc(loc[g], shard(g, out[g], me), ss.at[g, 0], sr.at[g, 0], sib))
    lc = []
    for g in G:
        cp = pltpu.make_async_copy(loc[g], shard(g, out[g], me), ls.at[g]); cp.start(); lc.append(cp)
    def st1(g):
        for k in range(1, nz):
            d = ((z + nz - k) % nz) * 2 + c
            p = piece(g, out[g], d, y, x)
            recv(p, zs.at[g, k-1], zr.at[g, k-1], zpeer[k-1])
            go(rc(p, p, xs.at[g, k-1], xr.at[g, k-1], xnb))
            go(rc(p, p, ys.at[g, k-1], yr.at[g, k-1], ynb))
    def st2(g):
        for k in range(1, nz):
            d = ((z + nz - k) % nz) * 2 + c
            p = piece(g, out[g], d, y, 1 - x)
            recv(p, xs.at[g, k-1], xr.at[g, k-1], xnb)
            pa = p.at[:, H[0]]
            go(rc(pa, pa, ds_.at[g, k-1, 0], dr.at[g, k-1, 0], ynb))
            p = piece(g, out[g], d, 1 - y, x)
            recv(p, ys.at[g, k-1], yr.at[g, k-1], ynb)
            pb = p.at[:, H[1]]
            go(rc(pb, pb, ds_.at[g, k-1, 1], dr.at[g, k-1, 1], xnb))
    def st3(g):
        for k in range(1, nz):
            d = ((z + nz - k) % nz) * 2 + c
            p = piece(g, out[g], d, 1 - y, 1 - x)
            pa, pb = p.at[:, H[0]], p.at[:, H[1]]
            recv(pa, ds_.at[g, k-1, 0], dr.at[g, k-1, 0], ynb)
            recv(pb, ds_.at[g, k-1, 1], dr.at[g, k-1, 1], xnb)
            sh = shard(g, out[g], d)
            go(rc(sh, sh, ss.at[g, k], sr.at[g, k], sib))
    for t in range(6):
        if t < 4: st1(t)
        if 0 <= t - 1 < 4: st2(t - 1)
        if 0 <= t - 2 < 4: st3(t - 2)
    for g in G:
        for k in range(nz):
            d = ((z + nz - k) % nz) * 2 + (1 - c)
            sh = shard(g, out[g], d)
            recv(sh, ss.at[g, k], sr.at[g, k], sib)
    for cp in lc: cp.wait()
    for cp in started: cp.wait_send()

def gather_weights(kv, qo, win, wout, dp):
    nz = dp // 2
    D = kv.shape[-1]
    a, b, c_ = kv.shape[2], win.shape[2], wout.shape[2]
    shp = [(2, dp, 2, a, D), (2, dp, 2, a, D), (dp, 2, 2, b, D), (2, 2, dp, c_, D)]
    S = pltpu.SemaphoreType.DMA
    n = nz - 1
    hb = pl.BlockSpec(memory_space=pl.ANY)
    return pl.pallas_call(
        functools.partial(ag_kernel, nz),
        out_shape=[jax.ShapeDtypeStruct(s, bf) for s in shp],
        in_specs=[hb] * 4, out_specs=[hb] * 4,
        scratch_shapes=[S((4, n)), S((4, n)), S((4, n)), S((4, n)), S((4, n)), S((4, n)), S((4, n, 2)), S((4, n, 2)), S((4, nz)), S((4, nz)), S((4,))],
        compiler_params=pltpu.CompilerParams(collective_id=1, has_side_effects=True),
    )(kv, qo, win, wout)

def pack(wq, wk, wv, wo, win, wout):
    D = wq.shape[0]
    sh = wq.shape[1]
    t = jnp.transpose
    kv = jnp.stack([t(wk), t(wv)]).reshape(2, 2, sh // 2, D)
    qo = jnp.stack([t(wq), t(wo)]).reshape(2, 2, sh // 2, D)
    wi = t(win).reshape(2, 2, win.shape[1] // 4, D)
    ff = wout.shape[0]
    wu = t(wout.reshape(ff // D, D, sh), (0, 2, 1)).reshape(2, 2, sh, D)
    return kv, qo, wi, wu


HEAD = 64


highest = lax.Precision.HIGHEST
norm_epsilon = 1e-12


def layer_norm(row_block, gain_vec, bias_vec):
    mean_val = jnp.mean(row_block, -1, keepdims=True)
    centered = row_block - mean_val
    inv_std = lax.rsqrt(jnp.mean(centered * centered, -1, keepdims=True) + norm_epsilon)
    normed = centered * inv_std
    return (normed * gain_vec + bias_vec, normed, inv_std)


def norm_back(grad_out, normed, inv_std, gain_vec):
    grad_normed = grad_out * gain_vec
    inner_term = (
        grad_normed
        - jnp.mean(grad_normed, -1, keepdims=True)
        - normed * jnp.mean(grad_normed * normed, -1, keepdims=True)
    )
    return (inv_std * inner_term, jnp.sum(grad_out * normed, 0), jnp.sum(grad_out, 0))


def row_product(left, right):
    return lax.dot_general(
        left, right, (((0,), (0,)), ((), ())), preferred_element_type=jnp.float32
    )


def feature_map(projected, random_features):
    scaled = projected.astype(jnp.float32) * HEAD ** (-0.25)
    projection = jnp.einsum("snhe,em->snhm", scaled, random_features, precision=highest)
    return (jnp.exp(projection - 0.5 * jnp.sum(scaled * scaled, -1, keepdims=True)), scaled)


def feature_back(grad_features, features, scaled, random_features):
    grad_proj = grad_features * features
    grad_scaled = jnp.einsum("snhm,em->snhe", grad_proj, random_features, precision=highest)
    grad_scaled = grad_scaled - scaled * jnp.sum(grad_proj, -1, keepdims=True)
    return grad_scaled * HEAD ** (-0.25)


def seq_sum(key_state, key_total):
    joined = lax.psum(jnp.concatenate([key_state, key_total[..., None]], -1), "seq")
    return (joined[..., :-1], joined[..., -1])


def mixer_forward(queries, key_proj, value_proj, key_mask, random_features, reducer):
    q_feat, q_scaled = feature_map(queries, random_features)
    k_feat, k_scaled = feature_map(key_proj, random_features)
    k_feat = k_feat * key_mask[:, :, None, None]
    key_state = jnp.einsum(
        "snhm,snhe->shme", k_feat, value_proj.astype(jnp.float32), precision=highest
    )
    key_total = jnp.sum(k_feat, 1)
    key_state, key_total = reducer(key_state, key_total)
    numerator = jnp.einsum("snhm,shme->snhe", q_feat, key_state, precision=highest)
    denominator = jnp.einsum("snhm,shm->snh", q_feat, key_total, precision=highest)
    context = numerator / denominator[..., None]
    return (
        context,
        (q_feat, q_scaled, k_feat, k_scaled, key_state, key_total, denominator, context),
    )


def mixer_backward(grad_context, value_proj, kept_mixer, random_features, reducer):
    q_feat, q_scaled, k_feat, k_scaled, key_state, key_total, denominator, context = kept_mixer
    grad_ctx = grad_context.astype(jnp.float32)
    grad_num = grad_ctx / denominator[..., None]
    grad_den = -jnp.sum(grad_ctx * context, -1) / denominator
    grad_qfeat = (
        jnp.einsum("snhe,shme->snhm", grad_num, key_state, precision=highest)
        + grad_den[..., None] * key_total[:, None]
    )
    grad_state = jnp.einsum("snhm,snhe->shme", q_feat, grad_num, precision=highest)
    grad_total = jnp.einsum("snhm,snh->shm", q_feat, grad_den, precision=highest)
    grad_state, grad_total = reducer(grad_state, grad_total)
    values_f32 = value_proj.astype(jnp.float32)
    grad_kfeat = (
        jnp.einsum("snhe,shme->snhm", values_f32, grad_state, precision=highest)
        + grad_total[:, None]
    )
    grad_values = jnp.einsum("snhm,shme->snhe", k_feat, grad_state, precision=highest)
    grad_queries = feature_back(grad_qfeat, q_feat, q_scaled, random_features)
    grad_keys = feature_back(grad_kfeat, k_feat, k_scaled, random_features)
    return (grad_queries, grad_keys, grad_values)


def shards(
    tokens,
    lengths,
    random_features,
    w_query,
    w_key,
    w_value,
    w_output,
    w_in,
    w_out,
    ln1_gain,
    ln1_bias,
    ln2_gain,
    ln2_bias,
    cotangent,
):
    seq_count, local_len, model_width = tokens.shape
    row_count = seq_count * local_len
    seq_parts = lax.axis_size("seq")
    heads_all = model_width // HEAD
    dp_size = lax.axis_size("dp")
    ff_width = w_in.shape[1] * dp_size
    if seq_parts == 4 and dp_size == 8 and w_query.shape[1] % 32 == 0:
        kv, qo, wi, wu = gather_weights(*pack(w_query, w_key, w_value, w_output, w_in, w_out), dp_size)
        square = (model_width, model_width)
        wk_full, wv_full = kv[0].reshape(square), kv[1].reshape(square)
        wq_full, wo_full = qo[0].reshape(square), qo[1].reshape(square)
        win_full = wi.reshape(ff_width, model_width)
        wout_full = jnp.transpose(wu.reshape(ff_width // model_width, *square), (1, 0, 2)).reshape(model_width, ff_width)
    else:
        wq_full, wk_full, wv_full, wo_full, win_full, wout_full = (
            lax.all_gather(w, "dp", axis=1, tiled=True).T
            for w in (w_query, w_key, w_value, w_output, w_in, w_out)
        )
    gain1, bias1, gain2, bias2 = lax.all_gather(
        jnp.stack([ln1_gain, ln1_bias, ln2_gain, ln2_bias]), "dp", axis=1, tiled=True
    )
    tok_rows = tokens.reshape(row_count, model_width)
    query_proj = lax.dot_general(tok_rows, wq_full, (((1,), (1,)), ((), ())), preferred_element_type=jnp.float32).astype(jnp.bfloat16)
    key_proj = lax.dot_general(tok_rows, wk_full, (((1,), (1,)), ((), ())), preferred_element_type=jnp.float32).astype(jnp.bfloat16)
    value_proj = lax.dot_general(tok_rows, wv_full, (((1,), (1,)), ((), ())), preferred_element_type=jnp.float32).astype(jnp.bfloat16)
    local_pos = lax.axis_index("seq") * local_len + jnp.arange(local_len, dtype=jnp.int32)
    row_valid = (local_pos[None, :] < lengths[:, None]).astype(jnp.float32)
    q_heads = query_proj.reshape(seq_count, local_len, heads_all, HEAD)
    k_heads = key_proj.reshape(seq_count, local_len, heads_all, HEAD)
    v_heads = value_proj.reshape(seq_count, local_len, heads_all, HEAD)
    context, kept_mixer = mixer_forward(q_heads, k_heads, v_heads, row_valid, random_features, seq_sum)
    ctx_rows = context.astype(jnp.bfloat16).reshape(row_count, model_width)
    attn_out = lax.dot_general(ctx_rows, wo_full, (((1,), (1,)), ((), ())), preferred_element_type=jnp.float32)
    resid1 = tok_rows.astype(jnp.float32) + attn_out
    hidden, normed1, inv1 = layer_norm(resid1, gain1.astype(jnp.float32), bias1.astype(jnp.float32))
    hidden_low = hidden.astype(jnp.bfloat16)
    pre_act = lax.dot_general(hidden_low, win_full, (((1,), (1,)), ((), ())), preferred_element_type=jnp.float32)
    activated, gelu_pull = jax.vjp(partial(jax.nn.gelu, approximate=False), pre_act)
    act_low = activated.astype(jnp.bfloat16)
    ffn_out = lax.dot_general(act_low, wout_full, (((1,), (1,)), ((), ())), preferred_element_type=jnp.float32)
    normed_out, normed2, inv2 = layer_norm(
        hidden + ffn_out, gain2.astype(jnp.float32), bias2.astype(jnp.float32)
    )
    valid_rows = row_valid.reshape(row_count, 1)
    layer_out = (
        (normed_out * valid_rows).astype(jnp.bfloat16).reshape(seq_count, local_len, model_width)
    )
    wq_back, wk_back, wv_back, wo_back, win_back, wout_back, gain1_back, gain2_back = (
        wq_full, wk_full, wv_full, wo_full, win_full, wout_full, gain1, gain2)
    grad_y = cotangent.reshape(row_count, model_width).astype(jnp.float32) * valid_rows
    grad_r2, grad_gain2, grad_bias2 = norm_back(
        grad_y, normed2, inv2, gain2_back.astype(jnp.float32)
    )
    grad_ffn = grad_r2.astype(jnp.bfloat16)
    grad_wout = row_product(act_low, grad_ffn)
    grad_act = lax.dot_general(
        grad_ffn, wout_back, (((1,), (0,)), ((), ())), preferred_element_type=jnp.float32
    )
    grad_pre = gelu_pull(grad_act)[0].astype(jnp.bfloat16)
    grad_win = row_product(hidden_low, grad_pre)
    grad_hidden = grad_r2 + lax.dot_general(
        grad_pre, win_back, (((1,), (0,)), ((), ())), preferred_element_type=jnp.float32
    )
    grad_r1, grad_gain1, grad_bias1 = norm_back(
        grad_hidden, normed1, inv1, gain1_back.astype(jnp.float32)
    )
    grad_attn = grad_r1.astype(jnp.bfloat16)
    grad_wo = row_product(ctx_rows, grad_attn)
    grad_ctx = lax.dot_general(
        grad_attn, wo_back, (((1,), (0,)), ((), ())), preferred_element_type=jnp.float32
    ).astype(jnp.bfloat16)
    grad_heads = grad_ctx.reshape(seq_count, local_len, heads_all, HEAD)
    grad_q, grad_k, grad_v = mixer_backward(grad_heads, v_heads, kept_mixer, random_features, seq_sum)
    grad_q_rows, grad_k_rows, grad_v_rows = (
        g.astype(jnp.bfloat16).reshape(row_count, model_width) for g in (grad_q, grad_k, grad_v)
    )
    grad_wq = row_product(tok_rows, grad_q_rows)
    grad_wk = row_product(tok_rows, grad_k_rows)
    grad_wv = row_product(tok_rows, grad_v_rows)
    contract_out = (((1,), (0,)), ((), ()))
    grad_tokens = grad_r1 + lax.dot_general(
        grad_q_rows, wq_back, contract_out, preferred_element_type=jnp.float32
    )
    grad_tokens = grad_tokens + lax.dot_general(
        grad_k_rows, wk_back, contract_out, preferred_element_type=jnp.float32
    )
    grad_tokens = grad_tokens + lax.dot_general(
        grad_v_rows, wv_back, contract_out, preferred_element_type=jnp.float32
    )
    (
        share_wq,
        share_wk,
        share_wv,
        share_wo,
        share_win,
        share_wout,
        share_g1,
        share_b1,
        share_g2,
        share_b2,
    ) = (
        lax.psum_scatter(grad_wq.astype(jnp.bfloat16), "dp", scatter_dimension=1, tiled=True),
        lax.psum_scatter(grad_wk.astype(jnp.bfloat16), "dp", scatter_dimension=1, tiled=True),
        lax.psum_scatter(grad_wv.astype(jnp.bfloat16), "dp", scatter_dimension=1, tiled=True),
        lax.psum_scatter(grad_wo.astype(jnp.bfloat16), "dp", scatter_dimension=1, tiled=True),
        lax.psum_scatter(grad_win.astype(jnp.bfloat16), "dp", scatter_dimension=1, tiled=True),
        lax.psum_scatter(grad_wout.astype(jnp.bfloat16), "dp", scatter_dimension=1, tiled=True),
        lax.psum_scatter(grad_gain1, "dp", scatter_dimension=0, tiled=True),
        lax.psum_scatter(grad_bias1, "dp", scatter_dimension=0, tiled=True),
        lax.psum_scatter(grad_gain2, "dp", scatter_dimension=0, tiled=True),
        lax.psum_scatter(grad_bias2, "dp", scatter_dimension=0, tiled=True),
    )
    (
        final_wq,
        final_wk,
        final_wv,
        final_wo,
        final_win,
        final_wout,
        final_g1,
        final_b1,
        final_g2,
        final_b2,
    ) = (
        lax.psum(share_wq.astype(jnp.bfloat16), "seq").astype(jnp.float32),
        lax.psum(share_wk.astype(jnp.bfloat16), "seq").astype(jnp.float32),
        lax.psum(share_wv.astype(jnp.bfloat16), "seq").astype(jnp.float32),
        lax.psum(share_wo.astype(jnp.bfloat16), "seq").astype(jnp.float32),
        lax.psum(share_win.astype(jnp.bfloat16), "seq").astype(jnp.float32),
        lax.psum(share_wout.astype(jnp.bfloat16), "seq").astype(jnp.float32),
        lax.psum(share_g1.astype(jnp.bfloat16), "seq").astype(jnp.float32),
        lax.psum(share_b1.astype(jnp.bfloat16), "seq").astype(jnp.float32),
        lax.psum(share_g2.astype(jnp.bfloat16), "seq").astype(jnp.float32),
        lax.psum(share_b2.astype(jnp.bfloat16), "seq").astype(jnp.float32),
    )
    return (
        layer_out,
        grad_tokens.reshape(seq_count, local_len, model_width),
        final_wq,
        final_wk,
        final_wv,
        final_wo,
        final_win,
        final_wout,
        final_g1,
        final_b1,
        final_g2,
        final_b2,
    )


def solution(mesh):
    in_specs = (
        P("dp", "seq", None),
        P("dp"),
        P(),
        P(None, "dp"),
        P(None, "dp"),
        P(None, "dp"),
        P(None, "dp"),
        P(None, "dp"),
        P(None, "dp"),
        P("dp"),
        P("dp"),
        P("dp"),
        P("dp"),
        P("dp", "seq", None),
    )
    out_specs = (
        P("dp", "seq", None),
        P("dp", "seq", None),
        P(None, "dp"),
        P(None, "dp"),
        P(None, "dp"),
        P(None, "dp"),
        P(None, "dp"),
        P(None, "dp"),
        P("dp"),
        P("dp"),
        P("dp"),
        P("dp"),
    )
    return jax.shard_map(shards, mesh=mesh, in_specs=in_specs, out_specs=out_specs, check_vma=False)
```

```python
import functools
from functools import partial

import jax
import jax.numpy as jnp
from jax import lax
from jax.experimental import pallas as pl
from jax.experimental.pallas import tpu as pltpu
from jax.sharding import PartitionSpec as P

MESH = pl.DeviceIdType.MESH
bf, f32 = jnp.bfloat16, jnp.float32
HEAD = 64
EPS = 1e-12
FWD_STATE = f32


def coords():
    s, d = lax.axis_index("seq"), lax.axis_index("dp")
    return s // 2, s % 2, d // 2, d % 2

def dev(y, x, z, c):
    return (y * 2 + x, z * 2 + c)

def entry_barrier(peers):
    sem = pltpu.get_barrier_semaphore()
    for p in peers:
        pl.semaphore_signal(sem, inc=1, device_id=p, device_id_type=MESH)
    pl.semaphore_wait(sem, len(peers))

def piece(g, ref, d, y, x):
    if g < 2:  return ref.at[y, d, x]
    if g == 2: return ref.at[d, y, x]
    return ref.at[y, x, d]
def lpiece(g, ref, y, x):
    return ref.at[y, x]
def shard(g, ref, d):
    if g < 2:  return ref.at[:, d]
    if g == 2: return ref.at[d]
    return ref.at[:, :, d]

def ag_kernel(nz, *refs):
    loc, out, sems = refs[:4], refs[4:8], refs[8:]
    zs, zr, xs, xr, ys, yr, ds_, dr, ss, sr, ls = sems
    y, x, z, c = coords()
    ynb, xnb, sib = dev(1 - y, x, z, c), dev(y, 1 - x, z, c), dev(y, x, z, 1 - c)
    zpeer = [dev(y, x, (z + k) % nz, c) for k in range(1, nz)]
    entry_barrier([ynb, xnb, sib] + zpeer)
    half = loc[0].shape[-1] // 2
    H = (pl.ds(0, half), pl.ds(half, half))
    me = z * 2 + c
    started = []
    def rc(src, dst, ssem, rsem, to):
        cp = pltpu.make_async_remote_copy(src_ref=src, dst_ref=dst, send_sem=ssem, recv_sem=rsem, device_id=to, device_id_type=MESH)
        return cp
    def go(cp):
        cp.start(); started.append(cp)
    def recv(dst, ssem, rsem, to):
        rc(dst, dst, ssem, rsem, to).wait_recv()
    G = range(4)
    for g in G:
        for k in range(1, nz):
            go(rc(lpiece(g, loc[g], y, x), piece(g, out[g], me, y, x), zs.at[g, k-1], zr.at[g, k-1], zpeer[k-1]))
        go(rc(loc[g], shard(g, out[g], me), ss.at[g, 0], sr.at[g, 0], sib))
    lc = []
    for g in G:
        cp = pltpu.make_async_copy(loc[g], shard(g, out[g], me), ls.at[g]); cp.start(); lc.append(cp)
    def st1(g):
        for k in range(1, nz):
            d = ((z + nz - k) % nz) * 2 + c
            p = piece(g, out[g], d, y, x)
            recv(p, zs.at[g, k-1], zr.at[g, k-1], zpeer[k-1])
            go(rc(p, p, xs.at[g, k-1], xr.at[g, k-1], xnb))
            go(rc(p, p, ys.at[g, k-1], yr.at[g, k-1], ynb))
    def st2(g):
        for k in range(1, nz):
            d = ((z + nz - k) % nz) * 2 + c
            p = piece(g, out[g], d, y, 1 - x)
            recv(p, xs.at[g, k-1], xr.at[g, k-1], xnb)
            pa = p.at[:, H[0]]
            go(rc(pa, pa, ds_.at[g, k-1, 0], dr.at[g, k-1, 0], ynb))
            p = piece(g, out[g], d, 1 - y, x)
            recv(p, ys.at[g, k-1], yr.at[g, k-1], ynb)
            pb = p.at[:, H[1]]
            go(rc(pb, pb, ds_.at[g, k-1, 1], dr.at[g, k-1, 1], xnb))
    def st3(g):
        for k in range(1, nz):
            d = ((z + nz - k) % nz) * 2 + c
            p = piece(g, out[g], d, 1 - y, 1 - x)
            pa, pb = p.at[:, H[0]], p.at[:, H[1]]
            recv(pa, ds_.at[g, k-1, 0], dr.at[g, k-1, 0], ynb)
            recv(pb, ds_.at[g, k-1, 1], dr.at[g, k-1, 1], xnb)
            sh = shard(g, out[g], d)
            go(rc(sh, sh, ss.at[g, k], sr.at[g, k], sib))
    for t in range(6):
        if t < 4: st1(t)
        if 0 <= t - 1 < 4: st2(t - 1)
        if 0 <= t - 2 < 4: st3(t - 2)
    for g in G:
        for k in range(nz):
            d = ((z + nz - k) % nz) * 2 + (1 - c)
            sh = shard(g, out[g], d)
            recv(sh, ss.at[g, k], sr.at[g, k], sib)
    for cp in lc: cp.wait()
    for cp in started: cp.wait_send()

def gather_weights(kv, qo, win, wout, dp):
    nz = dp // 2
    D = kv.shape[-1]
    a, b, c_ = kv.shape[2], win.shape[2], wout.shape[2]
    shp = [(2, dp, 2, a, D), (2, dp, 2, a, D), (dp, 2, 2, b, D), (2, 2, dp, c_, D)]
    S = pltpu.SemaphoreType.DMA
    n = nz - 1
    hb = pl.BlockSpec(memory_space=pl.ANY)
    return pl.pallas_call(
        functools.partial(ag_kernel, nz),
        out_shape=[jax.ShapeDtypeStruct(s, bf) for s in shp],
        in_specs=[hb] * 4, out_specs=[hb] * 4,
        scratch_shapes=[S((4, n)), S((4, n)), S((4, n)), S((4, n)), S((4, n)), S((4, n)), S((4, n, 2)), S((4, n, 2)), S((4, nz)), S((4, nz)), S((4,))],
        compiler_params=pltpu.CompilerParams(collective_id=1, has_side_effects=True),
    )(kv, qo, win, wout)

def pack(wq, wk, wv, wo, win, wout):
    D = wq.shape[0]
    sh = wq.shape[1]
    t = jnp.transpose
    kv = jnp.stack([t(wk), t(wv)]).reshape(2, 2, sh // 2, D)
    qo = jnp.stack([t(wq), t(wo)]).reshape(2, 2, sh // 2, D)
    wi = t(win).reshape(2, 2, win.shape[1] // 4, D)
    ff = wout.shape[0]
    wu = t(wout.reshape(ff // D, D, sh), (0, 2, 1)).reshape(2, 2, sh, D)
    return kv, qo, wi, wu


def nn(a, b): return lax.dot_general(a, b, (((1,), (0,)), ((), ())), preferred_element_type=f32)
def nt(a, b): return lax.dot_general(a, b, (((1,), (1,)), ((), ())), preferred_element_type=f32)
def tn(a, b): return lax.dot_general(a, b, (((0,), (0,)), ((), ())), preferred_element_type=f32)

def ds(i, n): return pl.ds(pl.multiple_of(i * n, n), n)

def project(tok, w, dst):
    D = tok.shape[1]
    for n in range(D // 256):
        o = nt(tok[...], w[n * 256:(n + 1) * 256, :]).astype(bf)
        dst[2 * n] = o[:, :128]
        dst[2 * n + 1] = o[:, 128:]

def features(x, wf):
    xf = x.astype(f32)
    sq = xf * xf
    hi = sq.astype(bf)
    lo = (sq - hi.astype(f32)).astype(bf)
    return jnp.exp(nn(jnp.concatenate([x, x, hi, lo], 1), wf[...]))

def pair_mask(m):
    r = lax.broadcasted_iota(jnp.int32, (128, 2 * m), 0) < HEAD
    c = lax.broadcasted_iota(jnp.int32, (128, 2 * m), 1) < m
    return (r == c)

def compact(st, m):
    return jnp.concatenate([st[:HEAD, :m], st[HEAD:, m:]], 0)

def key_side(kp, vp, wf, vm, kf, st, kt, nseq, loc):
    P_ = kp.shape[0]
    M = wf.shape[1] // 2
    def body(p, _):
        f = features(kp[p], wf) * jnp.concatenate([vm[...]] * (2 * M // 128), 1)
        fb = f.astype(bf)
        kf[p] = fb
        for b in range(nseq):
            rows = slice(b * loc, (b + 1) * loc)
            st[b, p] = compact(tn(vp[p, rows, :], fb[rows]), M)
            kt[b, p] = jnp.broadcast_to(jnp.sum(f[rows], 0, keepdims=True), (8, 2 * M))
        return 0
    lax.fori_loop(0, P_, body, 0)

def query_side(qp, wf, qf):
    def body(p, _):
        qf[p] = features(qp[p], wf).astype(bf)
        return 0
    lax.fori_loop(0, qp.shape[0], body, 0)

def build_right(st, kt, right, m):
    mask = pair_mask(m)
    nseq, P_ = st.shape[:2]
    for b in range(nseq):
        def body(p, _):
            c = st[b, p].astype(f32)
            s = jnp.where(mask, jnp.concatenate([c, c], 1), 0.0)
            t = jnp.where(mask, jnp.broadcast_to(kt[b, p][:1], (128, 2 * m)), 0.0)
            right[b, p] = jnp.concatenate([s, t], 0).astype(bf)
            return 0
        lax.fori_loop(0, P_, body, 0)

def mix_forward(qf, right, ctx, den, ctxb, nseq, loc):
    def body(p, _):
        for b in range(nseq):
            rows = slice(b * loc, (b + 1) * loc)
            o = nt(qf[p, rows, :], right[b, p])
            d = o[:, 128:]
            c = o[:, :128] / d
            ctx[p, rows, :] = c
            den[p, rows, :] = d
            ctxb[rows, ds(p, 128)] = c.astype(bf)
        return 0
    lax.fori_loop(0, qf.shape[0], body, 0)

def mean(a): return jnp.mean(a, -1, keepdims=True)

def attend_out(ctxb, wo, tok, vec, n1, inv1, hlow, resid):
    T, D = tok.shape
    for n in range(D // 256):
        resid[:, n * 256:(n + 1) * 256] = nt(ctxb[...], wo[n * 256:(n + 1) * 256, :])
    R = 64
    def body(i, _):
        r = ds(i, R)
        x = tok[r, :].astype(f32) + resid[r, :]
        cen = x - mean(x)
        inv = lax.rsqrt(mean(cen * cen) + EPS)
        n = cen * inv
        n1[r, :] = n
        inv1[r, :] = jnp.broadcast_to(inv, (R, 128))
        hlow[r, :] = (n * vec[0:1, :] + vec[1:2, :]).astype(bf)
        return 0
    lax.fori_loop(0, T // R, body, 0)

def ffn_chunk(j, hlow, win, wout, act, gp, acc, first):
    D = hlow.shape[1]
    C = act.shape[2]
    per = D // C
    pre = nt(hlow[...], win[ds(j, C), :])
    cdf = 0.5 * (1.0 + lax.erf(pre * 0.7071067811865476))
    a = (pre * cdf).astype(bf)
    act[j] = a
    gp[j] = (cdf + pre * (jnp.exp(-0.5 * pre * pre) * 0.3989422804014327)).astype(bf)
    o = nt(a, wout[j // per, :, ds(lax.rem(j, per), C)])
    if first: acc[...] = o
    else: acc[...] += o

def ffn_forward(hlow, win, wout, act, gp, acc):
    ffn_chunk(0, hlow, win, wout, act, gp, acc, True)
    def body(j, _):
        ffn_chunk(j, hlow, win, wout, act, gp, acc, False)
        return 0
    lax.fori_loop(1, act.shape[0], body, 0)

def fold8(a):
    return jnp.sum(a.reshape(a.shape[0] // 8, 8, a.shape[1]), 0)

def norm_pull(g, n, inv, gain):
    e = g * gain
    return inv * (e - mean(e) - n * mean(e * n))

def second_norm(acc, n1, vec, vm, cot, out, gr2, gffn, sums):
    T, D = acc.shape
    R = 64
    sums[0] = jnp.zeros((8, D), f32)
    sums[1] = jnp.zeros((8, D), f32)
    def body(i, _):
        r = ds(i, R)
        x = n1[r, :] * vec[0:1, :] + vec[1:2, :] + acc[r, :]
        cen = x - mean(x)
        inv = lax.rsqrt(mean(cen * cen) + EPS)
        n = cen * inv
        v = vm[r, :]
        vv = jnp.concatenate([v] * (D // 128), 1)
        out[r, :] = ((n * vec[2:3, :] + vec[3:4, :]) * vv).astype(bf)
        gy = cot[r, :].astype(f32) * vv
        sums[0] += fold8(gy * n)
        sums[1] += fold8(gy)
        g = norm_pull(gy, n, inv, vec[2:3, :])
        gr2[r, :] = g
        gffn[r, :] = g.astype(bf)
        return 0
    lax.fori_loop(0, T // R, body, 0)

def ffn_backward(j, gffn, gffn_t, hlow, win, wout, act, gp, gwin, gwout, gh, first):
    D = gffn.shape[1]
    C = act.shape[2]
    per = D // C
    jj, cc = j // per, lax.rem(j, per)
    ga = nn(gffn[...], wout[jj, :, ds(cc, C)])
    gpre = (ga * gp[j].astype(f32)).astype(bf)
    gwout[jj, :, ds(cc, C)] = nn(gffn_t[...], act[j]).astype(bf)
    gwin[ds(j, C), :] = tn(gpre, hlow[...]).astype(bf)
    o = nn(gpre, win[ds(j, C), :])
    if first: gh[...] = o
    else: gh[...] += o

def first_norm_back(gh, gr2, n1, inv1, vec, gr1, gattn, sums):
    T, D = gh.shape
    R = 64
    sums[2] = jnp.zeros((8, D), f32)
    sums[3] = jnp.zeros((8, D), f32)
    def body(i, _):
        r = ds(i, R)
        g = gr2[r, :] + gh[r, :]
        n = n1[r, :]
        sums[2] += fold8(g * n)
        sums[3] += fold8(g)
        o = norm_pull(g, n, inv1[r, :][:, :1], vec[0:1, :])
        gr1[r, :] = o
        gattn[r, :] = o.astype(bf)
        return 0
    lax.fori_loop(0, T // R, body, 0)

def weight_grad(gt, x, dst):
    D = x.shape[1]
    for n in range(D // 256):
        dst[n * 256:(n + 1) * 256, :] = nn(gt[n * 256:(n + 1) * 256, :], x[...]).astype(bf)

def weight_grad_pairs(gp_, x, dst):
    P_ = gp_.shape[0]
    for n in range(P_ // 2):
        g = jnp.concatenate([gp_[2 * n], gp_[2 * n + 1]], 1)
        dst[n * 256:(n + 1) * 256, :] = tn(g, x[...]).astype(bf)

def mix_back_query(gattn, wo, qp, qf, right, ctx, den, fbm, gst, gkt, gq, nseq, loc):
    M = qf.shape[2] // 2
    mask = pair_mask(M)
    def body(p, _):
        gc = nn(gattn[...], wo[:, ds(p, 128)]).astype(bf).astype(f32)
        gn = gc / den[p]
        t = -gn * ctx[p]
        g = jnp.concatenate([gn, t], 1).astype(bf)
        for b in range(nseq):
            rows = slice(b * loc, (b + 1) * loc)
            q = qf[p, rows, :]
            s = tn(g[rows], q)
            gst[b, p] = compact(s[:128], M)
            gkt[b, p] = jnp.broadcast_to(jnp.sum(jnp.where(mask, s[128:], 0.0), 0, keepdims=True), (8, 2 * M))
            pr = (nn(g[rows], right[b, p]) * q.astype(f32)).astype(bf)
            o = nn(pr, fbm[...])
            gq[p, rows, :] = (o[:, :128] - 0.125 * qp[p, rows, :].astype(f32) * o[:, 128:]).astype(bf)
        return 0
    lax.fori_loop(0, qf.shape[0], body, 0)

def mix_back_key(kp, vp, kf, gst, gkt, fbm, gk, gv, nseq, loc):
    M = kf.shape[2] // 2
    mask = pair_mask(M)
    def body(p, _):
        for b in range(nseq):
            rows = slice(b * loc, (b + 1) * loc)
            c = gst[b, p].astype(f32)
            s = jnp.where(mask, jnp.concatenate([c, c], 1), 0.0).astype(bf)
            k = kf[p, rows, :]
            pr = ((nn(vp[p, rows, :], s) + gkt[b, p][:1]) * k.astype(f32)).astype(bf)
            o = nn(pr, fbm[...])
            gk[p, rows, :] = (o[:, :128] - 0.125 * kp[p, rows, :].astype(f32) * o[:, 128:]).astype(bf)
            gv[p, rows, :] = nt(k, s).astype(bf)
        return 0
    lax.fori_loop(0, kf.shape[0], body, 0)

def join(g):
    return jnp.concatenate([g[i] for i in range(g.shape[0])], 1)

def token_grad(gr1, gq, gk, gv, wq, wk, wv, dst):
    D = gr1.shape[1]
    for n in range(D // 256):
        c = slice(n * 256, (n + 1) * 256)
        dst[:, c] = gr1[:, c] + (nn(join(gq), wq[:, c]) + nn(join(gk), wk[:, c]) + nn(join(gv), wv[:, c]))

def mixer_constants(rf):
    M = rf.shape[1]
    c = HEAD ** (-0.25)
    w = rf * c
    hi = w.astype(bf)
    lo = (w - hi.astype(f32)).astype(bf)
    z = jnp.zeros((HEAD, M), bf)
    def bd(a): return jnp.concatenate([jnp.concatenate([a, z], 1), jnp.concatenate([z, a], 1)], 0)
    s = jnp.full((HEAD, M), -0.0625, bf)
    wf = jnp.concatenate([bd(hi), bd(lo), bd(s), bd(s)], 0)
    fbm = jnp.concatenate([bd(hi), bd(jnp.ones((HEAD, M), bf))], 0).T
    return wf, fbm


class Reduce:
    def __init__(self, nz, grads, scratch, sems, fins):
        self.nz, self.grads, self.fins = nz, grads, fins
        G = len(grads)
        self.sib, self.a1, self.b1, self.a2, self.b2, self.tot, self.zrec = (scratch[i * G:(i + 1) * G] for i in range(7))
        self.sem = sems
        self.started = []
        y, x, z, c = self.pos = coords()
        self.ynb, self.xnb, self.sibdev = dev(1 - y, x, z, c), dev(y, 1 - x, z, c), dev(y, x, z, 1 - c)
        self.diag = dev(1 - y, 1 - x, z, c)
        self.zpeer = [dev(y, x, (z + k) % nz, c) for k in range(1, nz)]

    def peers(self):
        return [self.ynb, self.xnb, self.sibdev, self.diag] + self.zpeer

    def _cp(self, src, dst, g, i, to):
        s, r = self.sem
        return pltpu.make_async_remote_copy(src_ref=src, dst_ref=dst, send_sem=s.at[g, i], recv_sem=r.at[g, i], device_id=to, device_id_type=MESH)

    def _go(self, src, dst, g, i, to):
        cp = self._cp(src, dst, g, i, to)
        cp.start()
        self.started.append(cp)

    def _recv(self, dst, g, i, to):
        self._cp(dst, dst, g, i, to).wait_recv()

    def s0(self, g):
        y, x, z, c = self.pos
        for k in range(self.nz):
            self._go(shard(g, self.grads[g], k * 2 + 1 - c), self.sib[g].at[k], g, k, self.sibdev)

    def s1(self, g):
        y, x, z, c = self.pos
        nz, gr, sib = self.nz, self.grads[g], self.sib[g]
        half = gr.shape[-1] // 2
        A, B = pl.ds(0, half), pl.ds(half, half)
        for k in range(nz):
            self._recv(sib.at[k], g, k, self.sibdev)
        def body(i, _):
            k, q = i // 4, lax.rem(i, 4)
            qy, qx = q // 2, lax.rem(q, 2)
            sib[k, qy, qx] = (sib[k, qy, qx].astype(f32) + piece(g, gr, k * 2 + c, qy, qx)[...].astype(f32)).astype(bf)
            return 0
        lax.fori_loop(0, nz * 4, body, 0)
        self._go(sib.at[:, :, 1 - x, :, A], self.a1[g], g, nz, self.xnb)
        self._go(sib.at[:, 1 - y, :, :, B], self.b1[g], g, nz + 1, self.ynb)

    def s2(self, g):
        y, x, z, c = self.pos
        nz, sib = self.nz, self.sib[g]
        a1, b1 = self.a1[g], self.b1[g]
        half = a1.shape[-1]
        self._recv(a1, g, nz, self.xnb)
        self._recv(b1, g, nz + 1, self.ynb)
        def body(i, _):
            k, j = i // 2, lax.rem(i, 2)
            a1[k, j] = (a1[k, j].astype(f32) + sib[k, j, x, :, :half].astype(f32)).astype(bf)
            b1[k, j] = (b1[k, j].astype(f32) + sib[k, y, j, :, half:].astype(f32)).astype(bf)
            return 0
        lax.fori_loop(0, nz * 2, body, 0)
        self._go(a1.at[:, 1 - y], self.a2[g], g, nz + 2, self.ynb)
        self._go(b1.at[:, 1 - x], self.b2[g], g, nz + 3, self.xnb)

    def s3(self, g):
        y, x, z, c = self.pos
        nz = self.nz
        a1, b1, a2, b2, tot = self.a1[g], self.b1[g], self.a2[g], self.b2[g], self.tot[g]
        half = a1.shape[-1]
        self._recv(a2, g, nz + 2, self.ynb)
        self._recv(b2, g, nz + 3, self.xnb)
        def body(k, _):
            tot[k, :, :half] = (a1[k, y].astype(f32) + a2[k].astype(f32)).astype(bf)
            tot[k, :, half:] = (b1[k, x].astype(f32) + b2[k].astype(f32)).astype(bf)
            return 0
        lax.fori_loop(0, nz, body, 0)
        for k in range(1, nz):
            self._go(tot.at[(z + k) % nz], self.zrec[g].at[k - 1], g, nz + 3 + k, self.zpeer[k - 1])

    def s4(self, g):
        y, x, z, c = self.pos
        nz, zrec, fin = self.nz, self.zrec[g], self.fins[g]
        for k in range(1, nz):
            self._recv(zrec.at[k - 1], g, nz + 3 + k, self.zpeer[k - 1])
        t = self.tot[g][z].astype(f32)
        for k in range(1, nz):
            t = t + zrec[k - 1].astype(f32)
        mine = fin.at[y, x]
        fin[y, x] = t.astype(bf)
        for i, to in enumerate((self.xnb, self.ynb, self.diag)):
            self._go(mine, mine, g, 2 * nz + 3 + i, to)

    def s5(self, g):
        y, x, z, c = self.pos
        nz, fin = self.nz, self.fins[g]
        for i, (py, px, to) in enumerate(((y, 1 - x, self.xnb), (1 - y, x, self.ynb), (1 - y, 1 - x, self.diag))):
            self._recv(fin.at[py, px], g, 2 * nz + 3 + i, to)

    def finish(self):
        for cp in self.started:
            cp.wait_send()

def grad_shapes(dp, D, a, b, c_):
    return [(2, dp, 2, a, D), (2, dp, 2, a, D), (dp, 2, 2, b, D), (2, 2, dp, c_, D)]

def reduce_scratch(dp, D, a, b, c_):
    nz, h = dp // 2, D // 2
    rows = (a, a, b, c_)
    out = []
    for shp in (lambda r: (nz, 2, 2, r, D), lambda r: (nz, 2, r, h), lambda r: (nz, 2, r, h), lambda r: (nz, r, h),
                lambda r: (nz, r, h), lambda r: (nz, r, D), lambda r: (nz - 1, r, D)):
        out += [pltpu.VMEM(shp(r), bf) for r in rows]
    return out

def rs_kernel(nz, *refs):
    grads, fins = refs[:4], refs[4:8]
    scratch, sems = refs[8:8 + 28], refs[36:38]
    R = Reduce(nz, grads, scratch, sems, fins)
    entry_barrier(R.peers())
    for g in range(4): R.s0(g)
    stages = (R.s1, R.s2, R.s3, R.s4, R.s5)
    for t in range(4 + len(stages) - 1):
        for i, st in enumerate(stages):
            if 0 <= t - i < 4: st(t - i)
    R.finish()

def reduce_grads(grads, dp):
    D = grads[0].shape[-1]
    a, b, c_ = grads[0].shape[3], grads[2].shape[3], grads[3].shape[3]
    VM = pl.BlockSpec(memory_space=pltpu.VMEM)
    S = pltpu.SemaphoreType.DMA
    nz = dp // 2
    return pl.pallas_call(
        functools.partial(rs_kernel, nz),
        out_shape=[jax.ShapeDtypeStruct((2, 2, r, D), bf) for r in (a, a, b, c_)],
        in_specs=[VM] * 4, out_specs=[VM] * 4,
        scratch_shapes=reduce_scratch(dp, D, a, b, c_) + [S((4, 2 * nz + 6)), S((4, 2 * nz + 6))],
        compiler_params=pltpu.CompilerParams(collective_id=2, has_side_effects=True, vmem_limit_bytes=67043328),
    )(*grads)

def state_kernel(cid_dtype, st, kt, sto, kto, sb, srec, krec, ks, sems, semr):
    y, x, z, c = coords()
    peers = [dev(y, 1 - x, z, c), dev(1 - y, x, z, c), dev(1 - y, 1 - x, z, c)]
    sid = [y * 2 + 1 - x, (1 - y) * 2 + x, (1 - y) * 2 + 1 - x]
    me = y * 2 + x
    entry_barrier(peers)
    sb[...] = st[...].astype(cid_dtype)
    def cp(src, dst, i, k):
        return pltpu.make_async_remote_copy(src_ref=src, dst_ref=dst, send_sem=sems.at[i, k], recv_sem=semr.at[i, k], device_id=peers[k], device_id_type=MESH)
    out = []
    for k in range(3):
        a = cp(sb.at[sid[k]], srec.at[k], 0, k); a.start()
        b = cp(kt.at[sid[k]], krec.at[k], 1, k); b.start()
        out += [a, b]
    for k in range(3):
        cp(srec.at[k], srec.at[k], 0, k).wait_recv()
        cp(krec.at[k], krec.at[k], 1, k).wait_recv()
    t, u = st[me], kt[me]
    for k in range(3):
        t = t + srec[k].astype(f32)
        u = u + krec[k]
    sto[me] = t.astype(cid_dtype)
    kto[me] = u
    for k in range(3):
        a = cp(sto.at[me], sto.at[me], 2, k); a.start()
        b = cp(kto.at[me], kto.at[me], 3, k); b.start()
        out += [a, b]
    for k in range(3):
        cp(sto.at[sid[k]], sto.at[sid[k]], 2, k).wait_recv()
        cp(kto.at[sid[k]], kto.at[sid[k]], 3, k).wait_recv()
    for a in out: a.wait_send()

def sum_state(st, kt, cid, dtype):
    ns, P_, _, M = st.shape
    n = ns * P_ // 4
    st4, kt4 = st.reshape(4, n, 128, M), kt.reshape(4, n, 8, 2 * M)
    VM = pl.BlockSpec(memory_space=pltpu.VMEM)
    S = pltpu.SemaphoreType.DMA
    sto, kto = pl.pallas_call(
        functools.partial(state_kernel, dtype),
        out_shape=[jax.ShapeDtypeStruct(st4.shape, dtype), jax.ShapeDtypeStruct(kt4.shape, f32)],
        in_specs=[VM] * 2, out_specs=[VM] * 2,
        scratch_shapes=[pltpu.VMEM(st4.shape, dtype), pltpu.VMEM((3, n, 128, M), dtype), pltpu.VMEM((3, n, 8, 2 * M), f32), pltpu.VMEM((8, 128), f32), S((4, 3)), S((4, 3))],
        compiler_params=pltpu.CompilerParams(collective_id=cid, has_side_effects=True, vmem_limit_bytes=33554432),
    )(st4, kt4)
    return sto.reshape(st.shape), kto.reshape(kt.shape)


VM = pl.BlockSpec(memory_space=pltpu.VMEM)
ALLV = 67043328
COLS = 256


def call(body, ins, outs, scratch=(), name=None):
    return pl.pallas_call(
        body,
        out_shape=[jax.ShapeDtypeStruct(s, d) for s, d in outs],
        in_specs=[VM] * len(ins),
        out_specs=[VM] * len(outs),
        scratch_shapes=list(scratch),
        name=name,
        compiler_params=pltpu.CompilerParams(vmem_limit_bytes=ALLV),
    )(*ins)


def key_query_kernel(ns, loc, tok, kvw, qow, wf, vm, kp, vp, qp, kf, qf, st, kt):
    project(tok, kvw.at[0], kp)
    project(tok, kvw.at[1], vp)
    project(tok, qow.at[0], qp)
    key_side(kp, vp, wf, vm, kf, st, kt, ns, loc)
    query_side(qp, wf, qf)


def forward_kernel(ns, loc, tok, cot, qow, win, wout, vec, vm, qf, st, kt, ctx, den, ctxb, right, n1, inv1, hlow, act, gp, out, gr2, gffn, sums, acc):
    build_right(st, kt, right, qf.shape[2] // 2)
    mix_forward(qf, right, ctx, den, ctxb, ns, loc)
    attend_out(ctxb, qow.at[1], tok, vec, n1, inv1, hlow, acc)
    ffn_forward(hlow, win, wout, act, gp, acc)
    second_norm(acc, n1, vec, vm, cot, out, gr2, gffn, sums)


def backward_kernel(ns, loc, gffn, gr2, hlow, win, wout, act, gp, n1, inv1, vec, qow, ctxb, ctx, den, qp, qf, right, fbm, tok, gwin, gwout, gqo, gr1, gq, gst, gkt, sums, gh, gattn, tr):
    tr[...] = gffn[...].T
    ffn_backward(0, gffn, tr, hlow, win, wout, act, gp, gwin, gwout, gh, True)

    def body(j, _):
        ffn_backward(j, gffn, tr, hlow, win, wout, act, gp, gwin, gwout, gh, False)
        return 0

    lax.fori_loop(1, act.shape[0], body, 0)
    first_norm_back(gh, gr2, n1, inv1, vec, gr1, gattn, sums)
    tr[...] = gattn[...].T
    weight_grad(tr, ctxb, gqo.at[1])
    mix_back_query(gattn, qow.at[1], qp, qf, right, ctx, den, fbm, gst, gkt, gq, ns, loc)
    weight_grad_pairs(gq, tok, gqo.at[0])


def last_kernel(ns, loc, kp, vp, kf, gst, gkt, fbm, gr1, gq, kvw, qow, tok, gkv, tg, gk, gv):
    mix_back_key(kp, vp, kf, gst, gkt, fbm, gk, gv, ns, loc)
    weight_grad_pairs(gk, tok, gkv.at[0])
    weight_grad_pairs(gv, tok, gkv.at[1])
    token_grad(gr1, gq, gk, gv, qow.at[0], kvw.at[0], kvw.at[1], tg)


def shards(tokens, lengths, random_features, w_query, w_key, w_value, w_output, w_in, w_out, ln1_gain, ln1_bias, ln2_gain, ln2_bias, cotangent):
    ns, loc, D = tokens.shape
    T = ns * loc
    dp, parts = lax.axis_size("dp"), lax.axis_size("seq")
    part = w_query.shape[1]
    FF = w_out.shape[0]
    M = random_features.shape[1]
    P_ = D // 128
    fast = parts == 4 and dp == 8 and part % 32 == 0 and D == part * dp
    wf, fbm = mixer_constants(random_features)
    pos = lax.axis_index("seq") * loc + jnp.arange(loc, dtype=jnp.int32)
    valid = (pos[None, :] < lengths[:, None]).astype(f32).reshape(T, 1)
    vm = jnp.broadcast_to(valid, (T, 128))
    tok, cot = tokens.reshape(T, D), cotangent.reshape(T, D)
    vec = lax.all_gather(jnp.stack([ln1_gain, ln1_bias, ln2_gain, ln2_bias]), "dp", axis=1, tiled=True)
    vec = jnp.pad(vec.astype(f32), ((0, 4), (0, 0)))
    if fast:
        kvw, qow, win, wout = gather_weights(*pack(w_query, w_key, w_value, w_output, w_in, w_out), dp)
    else:
        def full(w):
            return lax.all_gather(w, "dp", axis=1, tiled=True).T
        kvw, qow = jnp.stack([full(w_key), full(w_value)]), jnp.stack([full(w_query), full(w_output)])
        win = full(w_in)
        wout = jnp.transpose(full(w_out).reshape(D, FF // D, D), (1, 0, 2))
    kvw, qow, win, wout = kvw.reshape(2, D, D), qow.reshape(2, D, D), win.reshape(FF, D), wout.reshape(FF // D, D, D)
    pm, pf, stt, ktt = (P_, T, 128), (P_, T, 2 * M), (ns, P_, 128, M), (ns, P_, 8, 2 * M)
    kp, vp, qp, kf, qf, st, kt = call(
        partial(key_query_kernel, ns, loc), (tok, kvw, qow, wf, vm),
        [(pm, bf)] * 3 + [(pf, bf)] * 2 + [(stt, f32), (ktt, f32)], name="key_query")
    if fast:
        st, kt = sum_state(st, kt, 3, FWD_STATE)
    else:
        st, kt = lax.psum((st, kt), "seq")
    ch = (FF // COLS, T, COLS)
    ctx, den, ctxb, right, n1, inv1, hlow, act, gp, out, gr2, gffn, sums = call(
        partial(forward_kernel, ns, loc), (tok, cot, qow, win, wout, vec, vm, qf, st, kt),
        [(pm, f32), (pm, f32), ((T, D), bf), ((ns, P_, 256, 2 * M), bf), ((T, D), f32), ((T, 128), f32), ((T, D), bf), (ch, bf), (ch, bf), ((T, D), bf), ((T, D), f32), ((T, D), bf), ((4, 8, D), f32)],
        [pltpu.VMEM((T, D), f32)], name="forward")
    gwin, gwout, gqo, gr1, gq, gst, gkt, sums2 = call(
        partial(backward_kernel, ns, loc), (gffn, gr2, hlow, win, wout, act, gp, n1, inv1, vec, qow, ctxb, ctx, den, qp, qf, right, fbm, tok),
        [((FF, D), bf), ((FF // D, D, D), bf), ((2, D, D), bf), ((T, D), f32), (pm, bf), (stt, f32), (ktt, f32), ((4, 8, D), f32)],
        [pltpu.VMEM((T, D), f32), pltpu.VMEM((T, D), bf), pltpu.VMEM((D, T), bf)], name="backward")
    if fast:
        gst, gkt = sum_state(gst, gkt, 4, bf)
    else:
        gst, gkt = lax.psum((gst, gkt), "seq")
    gkv, tg = call(
        partial(last_kernel, ns, loc), (kp, vp, kf, gst, gkt, fbm, gr1, gq, kvw, qow, tok),
        [((2, D, D), bf), ((T, D), f32)], [pltpu.VMEM(pm, bf), pltpu.VMEM(pm, bf)], name="last")
    small = jnp.sum(jnp.concatenate([sums2[2:], sums[:2]]), 1)
    small = lax.psum(small, ("seq", "dp"))
    small = lax.dynamic_slice_in_dim(small, lax.axis_index("dp") * part, part, 1)
    if fast:
        shp = grad_shapes(dp, D, part // 2, FF // dp // 4, part)
        kvg, qog, wig, wug = reduce_grads([g.reshape(s) for g, s in zip((gkv, gqo, gwin, gwout), shp)], dp)
        wk_g, wv_g, wq_g, wo_g = kvg[0].reshape(part, D).T, kvg[1].reshape(part, D).T, qog[0].reshape(part, D).T, qog[1].reshape(part, D).T
        wi_g = wig.reshape(FF // dp, D).T
        wu_g = jnp.transpose(wug.reshape(FF // D, part, D), (0, 2, 1)).reshape(FF, part)
        grads = (wq_g, wk_g, wv_g, wo_g, wi_g, wu_g)
    else:
        whole = (gqo[0].T, gkv[0].T, gkv[1].T, gqo[1].T, gwin.T, jnp.transpose(gwout, (0, 2, 1)).reshape(FF, D))
        grads = tuple(lax.psum(lax.psum_scatter(g, "dp", scatter_dimension=1, tiled=True), "seq") for g in whole)
    return (out.reshape(tokens.shape), tg.reshape(tokens.shape), *(g.astype(f32) for g in grads), small[0], small[1], small[2], small[3])


def solution(mesh):
    rows, cols, vecs = P("dp", "seq", None), P(None, "dp"), P("dp")
    return jax.shard_map(
        shards,
        mesh=mesh,
        in_specs=(rows, vecs, P(), *([cols] * 6), *([vecs] * 4), rows),
        out_specs=(rows, rows, *([cols] * 6), *([vecs] * 4)),
        check_vma=False,
    )
```

```python
import functools
from functools import partial

import jax
import jax.numpy as jnp
from jax import lax
from jax.experimental import pallas as pl
from jax.experimental.pallas import tpu as pltpu
from jax.sharding import PartitionSpec as P

MESH = pl.DeviceIdType.MESH
bf, f32 = jnp.bfloat16, jnp.float32
HEAD = 64
EPS = 1e-12


def coords():
    s, d = lax.axis_index("seq"), lax.axis_index("dp")
    return s // 2, s % 2, d // 2, d % 2

def dev(y, x, z, c):
    return (y * 2 + x, z * 2 + c)

def entry_barrier(peers):
    sem = pltpu.get_barrier_semaphore()
    for p in peers:
        pl.semaphore_signal(sem, inc=1, device_id=p, device_id_type=MESH)
    pl.semaphore_wait(sem, len(peers))

GROUPS = ((0, 0), (1, 0), (2, 0), (2, 1), (3, 0), (3, 1))
NAMES = ("kv", "qo", "wi0", "wi1", "wu0", "wu1")
ZFIRST = (2,)
EARLY = 4
NG = len(GROUPS)

def some(g, r):
    return pl.ds(GROUPS[g][1] * r, r)
def piece(g, ref, d, y, x, r):
    i = GROUPS[g][0]
    if i < 2:  return ref.at[y, d, x]
    if i == 2: return ref.at[d, y, x, some(g, r)]
    return ref.at[y, x, d, some(g, r)]
def lpiece(g, ref, y, x, r):
    return ref.at[y, x, some(g, r)]
def local_rows(g, ref, r):
    return ref.at[:, :, some(g, r)]
def shard(g, ref, d, r):
    i = GROUPS[g][0]
    if i < 2:  return ref.at[:, d]
    if i == 2: return ref.at[d, :, :, some(g, r)]
    return ref.at[:, :, d, some(g, r)]

class Gather:
    def __init__(self, nz, loc, out, sems, r):
        self.nz, self.sems, self.r = nz, sems, r
        self.loc, self.out = [loc[i] for i, _ in GROUPS], [out[i] for i, _ in GROUPS]
        y, x, z, c = self.pos = coords()
        dp = nz * 2
        self.ynb, self.xnb, self.sib = dev(1 - y, x, z, c), dev(y, 1 - x, z, c), dev(y, x, z, 1 - c)
        self.zpeer = [dev(y, x, (z + k) % nz, c) for k in range(1, nz)]
        self.me = z * 2 + c
        self.dpeer = [dev(y, x, (self.me + k) % dp // 2, (self.me + k) % 2) for k in range(1, dp)]
        self.started = []
        half = loc[3].shape[-1] // 2
        self.H = (pl.ds(0, half), pl.ds(half, half))

    def _rc(self, src, dst, ssem, rsem, to):
        return pltpu.make_async_remote_copy(src_ref=src, dst_ref=dst, send_sem=ssem, recv_sem=rsem, device_id=to, device_id_type=MESH)

    def _go(self, *a):
        cp = self._rc(*a)
        cp.start()
        self.started.append(cp)

    def _recv(self, dst, ssem, rsem, to):
        self._rc(dst, dst, ssem, rsem, to).wait_recv()

    def _local(self, g):
        return pltpu.make_async_copy(local_rows(g, self.loc[g], self.r), shard(g, self.out[g], self.me, self.r), self.sems[10].at[g])

    def _own(self, g):
        ss, sr = self.sems[8:10]
        self._go(local_rows(g, self.loc[g], self.r), shard(g, self.out[g], self.me, self.r), ss.at[g, 0], sr.at[g, 0], self.sib)
        self._local(g).start()

    def _vlocal(self, vloc, vout):
        return pltpu.make_async_copy(vloc, vout.at[self.me], self.sems[10].at[NG])

    def start(self, wz, vloc, vout):
        zs, zr, vs, vr = *self.sems[:2], *self.sems[11:13]
        y, x, z, c = self.pos
        for g in range(EARLY):
            for k in range(1, self.nz):
                self._go(lpiece(g, self.loc[g], y, x, self.r), piece(g, self.out[g], self.me, y, x, self.r), zs.at[g, k-1], zr.at[g, k-1], self.zpeer[k-1])
            self._own(g)
        for k in range(1, self.nz):
            self._go(self.loc[EARLY].at[y, x], wz.at[k - 1], zs.at[EARLY, k-1], zr.at[EARLY, k-1], self.zpeer[k-1])
        for k in range(1, self.nz * 2):
            self._go(vloc, vout.at[self.me], vs.at[k - 1], vr.at[k - 1], self.dpeer[k - 1])
        self._vlocal(vloc, vout).start()

    def _wz_local(self, wz, g, k):
        y, x, z, c = self.pos
        return pltpu.make_async_copy(wz.at[k - 1, some(g, self.r)], piece(g, self.out[g], self._from(k, c), y, x, self.r), self.sems[0].at[g, k - 1])

    def relay(self, wz):
        xs, xr, ys, yr = self.sems[2:6]
        y, x, z, c = self.pos
        for g in range(EARLY, NG):
            for k in range(1, self.nz):
                p, src = piece(g, self.out[g], self._from(k, c), y, x, self.r), wz.at[k - 1, some(g, self.r)]
                self._go(src, p, xs.at[g, k-1], xr.at[g, k-1], self.xnb)
                self._go(src, p, ys.at[g, k-1], yr.at[g, k-1], self.ynb)
        for g in range(EARLY, NG):
            for k in range(1, self.nz): self._wz_local(wz, g, k).start()
            self._own(g)

    def stage(self, g, i):
        (None, self.st1, self.st2, self.st3, self.done)[i](g)

    def _from(self, k, c):
        return ((self.pos[2] + self.nz - k) % self.nz) * 2 + c

    def st1(self, g):
        zs, zr, xs, xr, ys, yr = self.sems[:6]
        y, x, z, c = self.pos
        for k in range(1, self.nz):
            p = piece(g, self.out[g], self._from(k, c), y, x, self.r)
            self._recv(p, zs.at[g, k-1], zr.at[g, k-1], self.zpeer[k-1])
            self._go(p, p, xs.at[g, k-1], xr.at[g, k-1], self.xnb)
            self._go(p, p, ys.at[g, k-1], yr.at[g, k-1], self.ynb)

    def st2(self, g):
        xs, xr, ys, yr, ds_, dr = self.sems[2:8]
        y, x, z, c = self.pos
        for k in range(1, self.nz):
            d = self._from(k, c)
            p = piece(g, self.out[g], d, y, 1 - x, self.r)
            self._recv(p, xs.at[g, k-1], xr.at[g, k-1], self.xnb)
            pa = p.at[:, self.H[0]]
            self._go(pa, pa, ds_.at[g, k-1, 0], dr.at[g, k-1, 0], self.ynb)
            p = piece(g, self.out[g], d, 1 - y, x, self.r)
            self._recv(p, ys.at[g, k-1], yr.at[g, k-1], self.ynb)
            pb = p.at[:, self.H[1]]
            self._go(pb, pb, ds_.at[g, k-1, 1], dr.at[g, k-1, 1], self.xnb)

    def st3(self, g):
        ds_, dr, ss, sr = self.sems[6:10]
        y, x, z, c = self.pos
        for k in range(1, self.nz):
            d = self._from(k, c)
            p = piece(g, self.out[g], d, 1 - y, 1 - x, self.r)
            pa, pb = p.at[:, self.H[0]], p.at[:, self.H[1]]
            self._recv(pa, ds_.at[g, k-1, 0], dr.at[g, k-1, 0], self.ynb)
            self._recv(pb, ds_.at[g, k-1, 1], dr.at[g, k-1, 1], self.xnb)
            sh = shard(g, self.out[g], d, self.r)
            self._go(sh, sh, ss.at[g, k], sr.at[g, k], self.sib)

    def done(self, g):
        ss, sr = self.sems[8:10]
        for k in range(self.nz):
            self._recv(shard(g, self.out[g], self._from(k, 1 - self.pos[3]), self.r), ss.at[g, k], sr.at[g, k], self.sib)
        self._local(g).wait()

    def end(self, wz, vloc, vout):
        zs, zr, vs, vr = *self.sems[:2], *self.sems[11:13]
        dp = self.nz * 2
        for k in range(1, self.nz):
            self._recv(wz.at[k - 1], zs.at[EARLY, k-1], zr.at[EARLY, k-1], self.zpeer[k-1])
        for k in range(1, dp):
            self._recv(vout.at[(self.me + dp - k) % dp], vs.at[k - 1], vr.at[k - 1], self.dpeer[k - 1])
        self._vlocal(vloc, vout).wait()
        self.finish()

    def finish(self):
        for cp in self.started:
            cp.wait_send()

def gather_sems(dp):
    nz = dp // 2
    n = nz - 1
    S = pltpu.SemaphoreType.DMA
    return [S((NG, n)) for _ in range(6)] + [S((NG, n, 2)), S((NG, n, 2)), S((NG, nz)), S((NG, nz)), S((NG + 1,)), S((dp - 1,)), S((dp - 1,))]

def pack(wq, wk, wv, wo, win, wout):
    D = wq.shape[0]
    sh = wq.shape[1]
    t = jnp.transpose
    kv = jnp.stack([t(wk), t(wv)]).reshape(2, 2, sh // 2, D)
    qo = jnp.stack([t(wq), t(wo)]).reshape(2, 2, sh // 2, D)
    wi = t(win).reshape(2, 2, win.shape[1] // 4, D)
    ff = wout.shape[0]
    wu = t(wout.reshape(ff // D, D, sh), (0, 2, 1)).reshape(2, 2, sh, D)
    return kv, qo, wi, wu


def nn(a, b): return lax.dot_general(a, b, (((1,), (0,)), ((), ())), preferred_element_type=f32)
def nt(a, b): return lax.dot_general(a, b, (((1,), (1,)), ((), ())), preferred_element_type=f32)
def tn(a, b): return lax.dot_general(a, b, (((0,), (0,)), ((), ())), preferred_element_type=f32)

def ds(i, n): return pl.ds(pl.multiple_of(i * n, n), n)

def mat(w):
    return w[...].reshape(-1, w.shape[-1])

def project(tok, w, dst):
    D = tok.shape[1]
    v = mat(w)
    for n in range(D // 256):
        o = nt(tok[...], v[n * 256:(n + 1) * 256, :]).astype(bf)
        dst[2 * n] = o[:, :128]
        dst[2 * n + 1] = o[:, 128:]

def features(x, wf):
    xf = x.astype(f32)
    sq = xf * xf
    hi = sq.astype(bf)
    lo = (sq - hi.astype(f32)).astype(bf)
    return jnp.exp(nn(jnp.concatenate([x, x, hi, lo], 1), wf[...]))

def pair_mask(m):
    r = lax.broadcasted_iota(jnp.int32, (128, 2 * m), 0) < HEAD
    c = lax.broadcasted_iota(jnp.int32, (128, 2 * m), 1) < m
    return (r == c)

def compact(st, m):
    return jnp.concatenate([st[:HEAD, :m], st[HEAD:, m:]], 0)

def key_side(kp, vp, wf, vm, kf, st, kt, nseq, loc):
    P_ = kp.shape[0]
    M = wf.shape[1] // 2
    def body(p, _):
        f = features(kp[p], wf) * jnp.concatenate([vm[...]] * (2 * M // 128), 1)
        fb = f.astype(bf)
        kf[p] = fb
        for b in range(nseq):
            rows = slice(b * loc, (b + 1) * loc)
            st[b, p] = compact(tn(vp[p, rows, :], fb[rows]), M)
            kt[b, p] = jnp.broadcast_to(jnp.sum(f[rows], 0, keepdims=True), (8, 2 * M))
        return 0
    lax.fori_loop(0, P_, body, 0)

def query_side(qp, wf, qf):
    def body(p, _):
        qf[p] = features(qp[p], wf).astype(bf)
        return 0
    lax.fori_loop(0, qp.shape[0], body, 0)

def build_right(st, kt, right, m):
    mask = pair_mask(m)
    nseq, P_ = right.shape[:2]
    for b in range(nseq):
        def body(p, _):
            c = st[b, p].astype(f32)
            s = jnp.where(mask, jnp.concatenate([c, c], 1), 0.0)
            t = jnp.where(mask, jnp.broadcast_to(kt[b, p][:1], (128, 2 * m)), 0.0)
            right[b, p] = jnp.concatenate([s, t], 0).astype(bf)
            return 0
        lax.fori_loop(0, P_, body, 0)

def mix_forward(qf, right, ctx, den, ctxb, nseq, loc):
    def body(p, _):
        for b in range(nseq):
            rows = slice(b * loc, (b + 1) * loc)
            o = nt(qf[p, rows, :], right[b, p])
            d = o[:, 128:]
            c = o[:, :128] / d
            ctx[p, rows, :] = c
            den[p, rows, :] = d
            ctxb[rows, ds(p, 128)] = c.astype(bf)
        return 0
    lax.fori_loop(0, qf.shape[0], body, 0)

def mean(a): return jnp.mean(a, -1, keepdims=True)

def attend_out(ctxb, wo, tok, n1, inv1, resid):
    T, D = tok.shape
    v = mat(wo)
    for n in range(D // 256):
        resid[:, n * 256:(n + 1) * 256] = nt(ctxb[...], v[n * 256:(n + 1) * 256, :])
    R = 64
    def body(i, _):
        r = ds(i, R)
        x = tok[r, :].astype(f32) + resid[r, :]
        cen = x - mean(x)
        inv = lax.rsqrt(mean(cen * cen) + EPS)
        n1[r, :] = cen * inv
        inv1[r, :] = jnp.broadcast_to(inv, (R, 128))
        return 0
    lax.fori_loop(0, T // R, body, 0)

def ffn_chunk(j, hlow, win, act, gp):
    C = act.shape[2]
    pre = nt(hlow[...], win[ds(j, C), :])
    cdf = 0.5 * (1.0 + lax.erf(pre * 0.7071067811865476))
    act[j] = (pre * cdf).astype(bf)
    gp[j] = (cdf + pre * (jnp.exp(-0.5 * pre * pre) * 0.3989422804014327)).astype(bf)

def out_columns(wout, j, C):
    per = wout.shape[-1] // C
    jj, cc = j // per, ds(lax.rem(j, per), C)
    if len(wout.shape) == 3:
        return wout[jj, :, cc]
    return wout[jj // 2, lax.rem(jj, 2), :, :, cc].reshape(-1, C)

def ffn_output(j, act, wout, acc, first):
    o = nt(act[j], out_columns(wout, j, act.shape[2]))
    if first: acc[...] = o
    else: acc[...] += o

def hidden_rows(n1, vec, hlow):
    R = 64
    def body(i, _):
        r = ds(i, R)
        hlow[r, :] = (n1[r, :] * vec[0:1, :] + vec[1:2, :]).astype(bf)
        return 0
    lax.fori_loop(0, n1.shape[0] // R, body, 0)

def fold8(a):
    return jnp.sum(a.reshape(a.shape[0] // 8, 8, a.shape[1]), 0)

def norm_pull(g, n, inv, gain):
    e = g * gain
    return inv * (e - mean(e) - n * mean(e * n))

def second_norm(acc, n1, vec, vm, cot, out, gr2, gffn, sums):
    T, D = acc.shape
    R = 64
    sums[0] = jnp.zeros((8, D), f32)
    sums[1] = jnp.zeros((8, D), f32)
    def body(i, _):
        r = ds(i, R)
        x = n1[r, :] * vec[0:1, :] + vec[1:2, :] + acc[r, :]
        cen = x - mean(x)
        inv = lax.rsqrt(mean(cen * cen) + EPS)
        n = cen * inv
        v = vm[r, :]
        vv = jnp.concatenate([v] * (D // 128), 1)
        out[r, :] = ((n * vec[2:3, :] + vec[3:4, :]) * vv).astype(bf)
        gy = cot[r, :].astype(f32) * vv
        sums[0] += fold8(gy * n)
        sums[1] += fold8(gy)
        g = norm_pull(gy, n, inv, vec[2:3, :])
        gr2[r, :] = g
        gffn[r, :] = g.astype(bf)
        return 0
    lax.fori_loop(0, T // R, body, 0)

def ffn_out_grad(j, gffn_t, act, gwout):
    C = act.shape[2]
    per = gwout.shape[-1] // C
    o = nn(gffn_t[...], act[j]).astype(bf)
    jj, cc = j // per, ds(lax.rem(j, per), C)
    if len(gwout.shape) == 3:
        gwout[jj, :, cc] = o
    else:
        gwout[jj // 2, lax.rem(jj, 2), :, :, cc] = o.reshape(gwout.shape[2], gwout.shape[3], C)

def ffn_backward(j, gffn, hlow, win, wout, gp, gwin, gh, first):
    C = gp.shape[2]
    ga = nn(gffn[...], out_columns(wout, j, C))
    gpre = (ga * gp[j].astype(f32)).astype(bf)
    gwin[ds(j, C), :] = tn(gpre, hlow[...]).astype(bf)
    o = nn(gpre, win[ds(j, C), :])
    if first: gh[...] = o
    else: gh[...] += o

def first_norm_back(gh, gr2, n1, inv1, vec, gr1, gattn, sums):
    T, D = gh.shape
    R = 64
    sums[2] = jnp.zeros((8, D), f32)
    sums[3] = jnp.zeros((8, D), f32)
    def body(i, _):
        r = ds(i, R)
        g = gr2[r, :] + gh[r, :]
        n = n1[r, :]
        sums[2] += fold8(g * n)
        sums[3] += fold8(g)
        o = norm_pull(g, n, inv1[r, :][:, :1], vec[0:1, :])
        gr1[r, :] = o
        gattn[r, :] = o.astype(bf)
        return 0
    lax.fori_loop(0, T // R, body, 0)

def put_units(dst, n, o):
    dp, _, a, _ = dst.shape
    for u in range(dp):
        i = n * dp + u
        dst[i // 2, i % 2] = o[u * a:(u + 1) * a].astype(bf)

def weight_grad_units(gt, x, dst):
    h = gt.shape[0] // 2
    for n in range(2):
        put_units(dst, n, nn(gt[n * h:(n + 1) * h, :], x[...]))

def weight_grad_pairs_units(gp_, x, dst):
    h = gp_.shape[0] // 2
    for n in range(2):
        g = jnp.concatenate([gp_[n * h + i] for i in range(h)], 1)
        put_units(dst, n, tn(g, x[...]))

def weight_grad(gt, x, dst):
    D = x.shape[1]
    for n in range(D // 256):
        dst[n * 256:(n + 1) * 256, :] = nn(gt[n * 256:(n + 1) * 256, :], x[...]).astype(bf)

def weight_grad_pairs(gp_, x, dst):
    P_ = gp_.shape[0]
    for n in range(P_ // 2):
        g = jnp.concatenate([gp_[2 * n], gp_[2 * n + 1]], 1)
        dst[n * 256:(n + 1) * 256, :] = tn(g, x[...]).astype(bf)

def mix_back_query(gattn, wo, qp, qf, right, ctx, den, fbm, gst, gkt, gq, nseq, loc):
    M = qf.shape[2] // 2
    mask = pair_mask(M)
    def body(p, _):
        gc = nn(gattn[...], wo[:, ds(p, 128)]).astype(bf).astype(f32)
        gn = gc / den[p]
        t = -gn * ctx[p]
        g = jnp.concatenate([gn, t], 1).astype(bf)
        for b in range(nseq):
            rows = slice(b * loc, (b + 1) * loc)
            q = qf[p, rows, :]
            s = tn(g[rows], q)
            gst[b, p] = compact(s[:128], M)
            gkt[b, p] = jnp.broadcast_to(jnp.sum(jnp.where(mask, s[128:], 0.0), 0, keepdims=True), (8, 2 * M))
            pr = (nn(g[rows], right[b, p]) * q.astype(f32)).astype(bf)
            o = nn(pr, fbm[...])
            gq[p, rows, :] = (o[:, :128] - 0.125 * qp[p, rows, :].astype(f32) * o[:, 128:]).astype(bf)
        return 0
    lax.fori_loop(0, qf.shape[0], body, 0)

def mix_back_key(kp, vp, kf, gst, gkt, fbm, gk, gv, nseq, loc):
    M = kf.shape[2] // 2
    mask = pair_mask(M)
    def body(p, _):
        for b in range(nseq):
            rows = slice(b * loc, (b + 1) * loc)
            c = gst[b, p].astype(f32)
            s = jnp.where(mask, jnp.concatenate([c, c], 1), 0.0).astype(bf)
            k = kf[p, rows, :]
            pr = ((nn(vp[p, rows, :], s) + gkt[b, p][:1]) * k.astype(f32)).astype(bf)
            o = nn(pr, fbm[...])
            gk[p, rows, :] = (o[:, :128] - 0.125 * kp[p, rows, :].astype(f32) * o[:, 128:]).astype(bf)
            gv[p, rows, :] = nt(k, s).astype(bf)
        return 0
    lax.fori_loop(0, kf.shape[0], body, 0)

def join(g):
    return jnp.concatenate([g[i] for i in range(g.shape[0])], 1)

def token_grad(gr1, gq, gk, gv, wq, wk, wv, dst):
    D = gr1.shape[1]
    for n in range(D // 256):
        c = slice(n * 256, (n + 1) * 256)
        dst[:, c] = gr1[:, c] + (nn(join(gq), wq[:, c]) + nn(join(gk), wk[:, c]) + nn(join(gv), wv[:, c]))

def token_grad_query(gq, wq, dst):
    D = dst.shape[1]
    for n in range(D // 256):
        c = slice(n * 256, (n + 1) * 256)
        dst[:, c] += nn(join(gq), wq[:, c])

def token_grad_keys(gk, gv, wk, wv, dst):
    D = dst.shape[1]
    for n in range(D // 256):
        c = slice(n * 256, (n + 1) * 256)
        dst[:, c] += nn(join(gk), wk[:, c]) + nn(join(gv), wv[:, c])

def split_features(rf):
    w = rf * HEAD ** (-0.25)
    hi = w.astype(bf)
    lo = (w - hi.astype(f32)).astype(bf)
    z = jnp.zeros(rf.shape, bf)
    def bd(a): return jnp.concatenate([jnp.concatenate([a, z], 1), jnp.concatenate([z, a], 1)], 0)
    return hi, lo, bd

def feature_matrix(rf):
    hi, lo, bd = split_features(rf)
    s = bd(jnp.full(rf.shape, -0.0625, bf))
    return jnp.concatenate([bd(hi), bd(lo), s, s], 0)

def feature_pull(rf):
    hi, lo, bd = split_features(rf)
    return jnp.concatenate([bd(hi), bd(jnp.ones(rf.shape, bf))], 0).T


class Reduce:
    def __init__(self, nz, grads, own, scratch, sems, own_sem, fins, r):
        self.nz, self.own, self.own_sem, self.sem, self.r, self.sc = nz, own, own_sem, sems, r, scratch
        self.grads = [grads[i] for i, _ in GROUPS]
        if fins is not None:
            self.fins = [local_rows(g, fins[GROUPS[g][0]], r) for g in range(NG)]
            self.h = fins[0].shape[-1] // 2
        else:
            self.h = grads[3].shape[-1] // 2
        self.started = []
        y, x, z, c = self.pos = coords()
        self.ynb, self.xnb, self.sibdev = dev(1 - y, x, z, c), dev(y, 1 - x, z, c), dev(y, x, z, 1 - c)
        self.zpeer = [dev(y, x, (z + k) % nz, c) for k in range(1, nz)]
        self.A, self.B = pl.ds(0, self.h), pl.ds(self.h, self.h)

    def _cp(self, src, dst, g, i, to):
        s, r = self.sem
        return pltpu.make_async_remote_copy(src_ref=src, dst_ref=dst, send_sem=s.at[g, i], recv_sem=r.at[g, i], device_id=to, device_id_type=MESH)

    def _go(self, src, dst, g, i, to):
        cp = self._cp(src, dst, g, i, to)
        cp.start()
        self.started.append(cp)

    def _recv(self, dst, g, i, to):
        self._cp(dst, dst, g, i, to).wait_recv()

    def stage(self, g, i):
        late = g in ZFIRST
        (self.s0, self.z1 if late else self.s1, self.z2 if late else self.s2, self.z3 if late else self.s3, self.z4 if late else self.s4, self.s5, self.s6)[i](g)

    def s0(self, g):
        c = self.pos[3]
        sib = self.sc[g][0]
        for k in range(self.nz):
            self._go(shard(g, self.grads[g], k * 2 + 1 - c, self.r), sib.at[k], g, k, self.sibdev)
        if self.own[g] is not None:
            for k in range(self.nz):
                self._own(g, k).start()

    def _own(self, g, k):
        c = self.pos[3]
        return pltpu.make_async_copy(shard(g, self.grads[g], k * 2 + c, self.r), self.own[g].at[k], self.own_sem.at[g, k])

    def _pair(self, g):
        c = self.pos[3]
        sib, own, gr = self.sc[g][0], self.own[g], self.grads[g]
        for k in range(self.nz):
            self._recv(sib.at[k], g, k, self.sibdev)
            if own is not None:
                self._own(g, k).wait()
        def body(i, _):
            k, q = i // 4, lax.rem(i, 4)
            qy, qx = q // 2, lax.rem(q, 2)
            mine = piece(g, gr, k * 2 + c, qy, qx, self.r) if own is None else own.at[k, qy, qx]
            sib[k, qy, qx] = (sib[k, qy, qx].astype(f32) + mine[...].astype(f32)).astype(bf)
            return 0
        lax.fori_loop(0, self.nz * 4, body, 0)

    def s1(self, g):
        y, x, z, c = self.pos
        sib, a1, b1 = self.sc[g][:3]
        self._pair(g)
        self._go(sib.at[:, :, 1 - x, :, self.A], a1, g, self.nz, self.xnb)
        self._go(sib.at[:, 1 - y, :, :, self.B], b1, g, self.nz + 1, self.ynb)

    def recv1(self, g):
        a1, b1 = self.sc[g][1:3]
        self._recv(a1, g, self.nz, self.xnb)
        self._recv(b1, g, self.nz + 1, self.ynb)

    def s2(self, g):
        y, x, z, c = self.pos
        nz, h = self.nz, self.h
        sib, a1, b1, a2, b2 = self.sc[g][:5]
        if g < EARLY:
            self.recv1(g)
        def body(i, _):
            k, j = i // 2, lax.rem(i, 2)
            a1[k, j] = (a1[k, j].astype(f32) + sib[k, j, x, :, :h].astype(f32)).astype(bf)
            b1[k, j] = (b1[k, j].astype(f32) + sib[k, y, j, :, h:].astype(f32)).astype(bf)
            return 0
        lax.fori_loop(0, nz * 2, body, 0)
        self._go(a1.at[:, 1 - y], a2, g, nz + 2, self.ynb)
        self._go(b1.at[:, 1 - x], b2, g, nz + 3, self.xnb)

    def s3(self, g):
        y, x, z, c = self.pos
        nz, h = self.nz, self.h
        a1, b1, a2, b2, tot, zrec = self.sc[g][1:]
        self._recv(a2, g, nz + 2, self.ynb)
        self._recv(b2, g, nz + 3, self.xnb)
        def body(k, _):
            tot[k, :, :h] = (a1[k, y].astype(f32) + a2[k].astype(f32)).astype(bf)
            tot[k, :, h:] = (b1[k, x].astype(f32) + b2[k].astype(f32)).astype(bf)
            return 0
        lax.fori_loop(0, nz, body, 0)
        for k in range(1, nz):
            self._go(tot.at[(z + k) % nz], zrec.at[k - 1], g, nz + 3 + k, self.zpeer[k - 1])

    def s4(self, g):
        y, x, z, c = self.pos
        nz, fin = self.nz, self.fins[g]
        tot, zrec = self.sc[g][5:]
        for k in range(1, nz):
            self._recv(zrec.at[k - 1], g, nz + 3 + k, self.zpeer[k - 1])
        t = tot[z].astype(f32)
        for k in range(1, nz):
            t = t + zrec[k - 1].astype(f32)
        fin[y, x] = t.astype(bf)
        self._spread(g)

    def z1(self, g):
        z = self.pos[2]
        sib, zrec = self.sc[g][0], self.sc[g][6]
        self._pair(g)
        for k in range(1, self.nz):
            self._go(sib.at[(z + k) % self.nz], zrec.at[k - 1], g, self.nz + 3 + k, self.zpeer[k - 1])

    def z2(self, g):
        y, x, z, c = self.pos
        nz = self.nz
        sib, a1, b1, a2, b2, tot, zrec = self.sc[g]
        for k in range(1, nz):
            self._recv(zrec.at[k - 1], g, nz + 3 + k, self.zpeer[k - 1])
        def body(i, _):
            j, l = i // 2, lax.rem(i, 2)
            t = sib[z, j, l].astype(f32)
            for k in range(1, nz):
                t = t + zrec[k - 1, j, l].astype(f32)
            tot[j, l] = t.astype(bf)
            return 0
        lax.fori_loop(0, 4, body, 0)
        self._go(tot.at[:, 1 - x, :, self.A], a1, g, nz, self.xnb)
        self._go(tot.at[1 - y, :, :, self.B], b1, g, nz + 1, self.ynb)

    def z3(self, g):
        y, x, z, c = self.pos
        nz, h = self.nz, self.h
        sib, a1, b1, a2, b2, tot, zrec = self.sc[g]
        self._recv(a1, g, nz, self.xnb)
        self._recv(b1, g, nz + 1, self.ynb)
        for j in range(2):
            a1[j] = (a1[j].astype(f32) + tot[j, x, :, :h].astype(f32)).astype(bf)
            b1[j] = (b1[j].astype(f32) + tot[y, j, :, h:].astype(f32)).astype(bf)
        self._go(a1.at[1 - y], a2, g, nz + 2, self.ynb)
        self._go(b1.at[1 - x], b2, g, nz + 3, self.xnb)

    def z4(self, g):
        y, x, z, c = self.pos
        nz, h, fin = self.nz, self.h, self.fins[g]
        a1, b1, a2, b2 = self.sc[g][1:5]
        self._recv(a2, g, nz + 2, self.ynb)
        self._recv(b2, g, nz + 3, self.xnb)
        fin[y, x, :, :h] = (a1[y].astype(f32) + a2[...].astype(f32)).astype(bf)
        fin[y, x, :, h:] = (b1[x].astype(f32) + b2[...].astype(f32)).astype(bf)
        self._spread(g)

    def _spread(self, g):
        y, x, z, c = self.pos
        a, b = self.fins[g].at[y, x, :, self.A], self.fins[g].at[y, x, :, self.B]
        self._go(a, a, g, 2 * self.nz + 3, self.xnb)
        self._go(b, b, g, 2 * self.nz + 4, self.ynb)

    def s5(self, g):
        y, x, z, c = self.pos
        nz, fin = self.nz, self.fins[g]
        self._recv(fin.at[y, 1 - x, :, self.A], g, 2 * nz + 3, self.xnb)
        self._recv(fin.at[1 - y, x, :, self.B], g, 2 * nz + 4, self.ynb)
        a, b = fin.at[y, :, :, self.A], fin.at[:, x, :, self.B]
        self._go(a, a, g, 2 * nz + 5, self.ynb)
        self._go(b, b, g, 2 * nz + 6, self.xnb)

    def s6(self, g):
        y, x, z, c = self.pos
        nz, fin = self.nz, self.fins[g]
        self._recv(fin.at[1 - y, :, :, self.A], g, 2 * nz + 5, self.ynb)
        self._recv(fin.at[:, 1 - x, :, self.B], g, 2 * nz + 6, self.xnb)

    def finish(self):
        for cp in self.started:
            cp.wait_send()

def grad_shapes(dp, D, a, b, c_):
    return [(2, dp, 2, a, D), (2, dp, 2, a, D), (dp, 2, 2, b, D), (2, 2, dp, c_, D)]

def reduce_shapes(nz, D, r, g):
    h = D // 2
    if g in ZFIRST:
        return (nz, 2, 2, r, D), (2, r, h), (2, r, h), (r, h), (r, h), (2, 2, r, D), (nz - 1, 2, 2, r, D)
    return (nz, 2, 2, r, D), (nz, 2, r, h), (nz, 2, r, h), (nz, r, h), (nz, r, h), (nz, r, D), (nz - 1, r, D)

class SmallSum:
    def __init__(self, nz, src, dst, first, second, sems):
        self.dp, self.src, self.dst, self.first, self.second, self.sem = nz * 2, src, dst, first, second, sems
        y, x, z, c = coords()
        self.me, self.seq, dp = z * 2 + c, y * 2 + x, nz * 2
        self.dpeer = [dev(y, x, (self.me + k) % dp // 2, (self.me + k) % 2) for k in range(1, dp)]
        self.speer = [dev(y, 1 - x, z, c), dev(1 - y, x, z, c), dev(1 - y, 1 - x, z, c)]
        self.sid = [y * 2 + 1 - x, (1 - y) * 2 + x, (1 - y) * 2 + 1 - x]
        self.started = []

    def peers(self):
        return self.dpeer + self.speer

    def _cp(self, src, dst, i, to):
        s, r = self.sem
        return pltpu.make_async_remote_copy(src_ref=src, dst_ref=dst, send_sem=s.at[i], recv_sem=r.at[i], device_id=to, device_id_type=MESH)

    def _go(self, *a):
        cp = self._cp(*a)
        cp.start()
        self.started.append(cp)

    def t0(self):
        for k in range(1, self.dp):
            self._go(self.src.at[(self.me + k) % self.dp], self.first.at[k - 1], k - 1, self.dpeer[k - 1])

    def t1(self):
        t = self.src[self.me]
        for k in range(1, self.dp):
            self._cp(self.first.at[k - 1], self.first.at[k - 1], k - 1, self.dpeer[k - 1]).wait_recv()
            t = t + self.first[k - 1]
        self.second[self.seq] = t
        for i in range(3):
            self._go(self.second.at[self.seq], self.second.at[self.seq], self.dp - 1 + i, self.speer[i])

    def t2(self):
        for i in range(3):
            self._cp(self.second.at[self.sid[i]], self.second.at[self.sid[i]], self.dp - 1 + i, self.speer[i]).wait_recv()
        self.dst[...] = (self.second[0] + self.second[1]) + (self.second[2] + self.second[3])

    def finish(self):
        for cp in self.started:
            cp.wait_send()

def small_scratch(dp):
    S = pltpu.SemaphoreType.DMA
    return [pltpu.VMEM((dp - 1, 8, 128), f32), pltpu.VMEM((4, 8, 128), f32), S((dp + 2,)), S((dp + 2,))]

class StateSum:
    def __init__(self, st, kt, sto, kto, sb, srec, krec, sems):
        self.st, self.kt, self.sto, self.kto, self.srec, self.krec, self.sem = st, kt, sto, kto, srec, krec, sems
        self.sb = st if sb is None else sb
        y, x, z, c = coords()
        self.peers = [dev(y, 1 - x, z, c), dev(1 - y, x, z, c), dev(1 - y, 1 - x, z, c)]
        self.sid = [y * 2 + 1 - x, (1 - y) * 2 + x, (1 - y) * 2 + 1 - x]
        self.me = y * 2 + x
        self.started = []

    def _cp(self, src, dst, i, k):
        s, r = self.sem
        return pltpu.make_async_remote_copy(src_ref=src, dst_ref=dst, send_sem=s.at[i, k], recv_sem=r.at[i, k], device_id=self.peers[k], device_id_type=MESH)

    def _go(self, *a):
        cp = self._cp(*a)
        cp.start()
        self.started.append(cp)

    def _recv(self, dst, i, k):
        self._cp(dst, dst, i, k).wait_recv()

    def start(self):
        if self.sb is not self.st:
            self.sb[...] = self.st[...].astype(self.sb.dtype)
        for k in range(3):
            self._go(self.sb.at[self.sid[k]], self.srec.at[k], 0, k)
            self._go(self.kt.at[self.sid[k]], self.krec.at[k], 1, k)

    def stage(self, i):
        (self.start, self.mid, self.end)[i]()

    def mid(self):
        me = self.me
        t, u = self.st[me], self.kt[me]
        for k in range(3):
            self._recv(self.srec.at[k], 0, k)
            self._recv(self.krec.at[k], 1, k)
            t = t + self.srec[k].astype(f32)
            u = u + self.krec[k]
        self.sto[me] = t.astype(self.sto.dtype)
        self.kto[me] = u
        for k in range(3):
            self._go(self.sto.at[me], self.sto.at[me], 2, k)
            self._go(self.kto.at[me], self.kto.at[me], 3, k)

    def end(self):
        for k in range(3):
            self._recv(self.sto.at[self.sid[k]], 2, k)
            self._recv(self.kto.at[self.sid[k]], 3, k)

    def finish(self):
        for cp in self.started:
            cp.wait_send()

class Flat:
    def __init__(self, ref, pairs):
        self.ref, self.pairs = ref, pairs

    def _at(self, i):
        f = i[0] * self.pairs + i[1]
        return (f // self.ref.shape[1], f % self.ref.shape[1])

    def __getitem__(self, i):
        return self.ref[self._at(i)]

    def __setitem__(self, i, v):
        self.ref[self._at(i)] = v

class FlatRow:
    def __init__(self, ref, pairs, n):
        self.ref, self.pairs, self.n = ref, pairs, n

    def _at(self, i):
        f = i[0] * self.pairs + i[1]
        return (f // self.n, pl.ds(f % self.n, 1), slice(None))

    def __getitem__(self, i):
        return self.ref[self._at(i)]

    def __setitem__(self, i, v):
        self.ref[self._at(i)] = v[:1]

def state_scratch(n, M, dtype):
    S = pltpu.SemaphoreType.DMA
    sb = [] if dtype == f32 else [pltpu.VMEM((4, n, 128, M), dtype)]
    return sb + [pltpu.VMEM((3, n, 128, M), dtype), pltpu.VMEM((3, 8, 2 * M), f32), S((4, 3)), S((4, 3))]

VM = pl.BlockSpec(memory_space=pltpu.VMEM)
ALLV = 67043328
COLS = 256


def call(body, ins, outs, scratch=(), name=None):
    return pl.pallas_call(
        body,
        out_shape=[jax.ShapeDtypeStruct(s, d) for s, d in outs],
        in_specs=[VM] * len(ins),
        out_specs=[VM] * len(outs),
        scratch_shapes=list(scratch),
        name=name,
        compiler_params=pltpu.CompilerParams(vmem_limit_bytes=ALLV),
    )(*ins)


def key_query_kernel(ns, loc, tok, kvw, qow, wf, vm, kp, vp, qp, kf, qf, st, kt):
    project(tok, kvw.at[0], kp)
    project(tok, kvw.at[1], vp)
    project(tok, qow.at[0], qp)
    key_side(kp, vp, wf, vm, kf, st, kt, ns, loc)
    query_side(qp, wf, qf)


def mix_kernel(ns, loc, tok, qow, qf, st, kt, ctx, den, ctxb, right, n1, inv1, resid):
    build_right(st, kt, right, qf.shape[2] // 2)
    mix_forward(qf, right, ctx, den, ctxb, ns, loc)
    attend_out(ctxb, qow.at[1], tok, n1, inv1, resid)


KEPT = 11
HEAD_ORDER = (
    "kv.1", "kv.2", "qo.1", "kv.3", "wi0.1", "kv.4", "qo.2", "pk", "wi1.1", "ks", "qo.3", "s.0",
    "wi0.2", "s.1", "wi0.3", "qo.4", "pq", "qs", "s.2", "wi1.2", "mx", "wi1.3", "wi0.4", "at",
    "wi1.4",
)


def run_order(order, compute, stage, state):
    for op in order:
        if op in compute:
            compute[op]()
        else:
            name, i = op.split(".")
            if name == "s":
                state(int(i))
            else:
                stage(NAMES.index(name), int(i))


def head_kernel(ns, loc, nz, *refs):
    local, (vloc, tok, rf, vm), refs = refs[:4], refs[4:8], refs[8:]
    whole, wz, vout, kept, refs = (*refs[:3], None), refs[3], refs[4], refs[5:5 + KEPT], refs[5 + KEPT:]
    sems, (kvs, qos, lsem), here, ksem, refs = refs[:13], refs[13:16], refs[16:16 + KEPT], refs[16 + KEPT], refs[17 + KEPT:]
    st, kt, sto, kto, sb, srec, krec, ss, sr, resid, wf = refs
    kp, vp, qp, kf, qf, ctx, den, ctxb, right, n1, inv1 = here
    P_, M = qf.shape[0], qf.shape[2] // 2
    n = ns * P_ // 4

    def keep(i):
        return pltpu.make_async_copy(here[i], kept[i], ksem.at[i])

    def load(i, dst):
        return pltpu.make_async_copy(whole[i], dst, lsem.at[i])
    G = Gather(nz, local, whole, sems, local[0].shape[2])
    S = StateSum(st, kt, sto, kto, sb, srec, krec, (ss, sr))
    entry_barrier([G.ynb, S.peers[0], S.peers[2]] + G.dpeer)
    G.start(wz, vloc, vout)
    wf[...] = feature_matrix(rf[...])

    def key_values():
        load(0, kvs).start()
        load(0, kvs).wait()
        project(tok, kvs.at[0], kp)
        project(tok, kvs.at[1], vp)
        for i in (0, 1): keep(i).start()

    def keys():
        kt[...] = jnp.zeros_like(kt)
        key_side(kp, vp, wf, vm, kf, Flat(st, P_), FlatRow(kt, P_, n), ns, loc)
        keep(3).start()

    def queries():
        load(1, qos).start()
        load(1, qos).wait()
        project(tok, qos.at[0], qp)
        keep(2).start()

    def query_features():
        query_side(qp, wf, qf)
        keep(4).start()

    def mix():
        build_right(Flat(sto, P_), FlatRow(kto, P_, n), right, M)
        mix_forward(qf, right, ctx, den, ctxb, ns, loc)
        for i in (5, 6, 7, 8): keep(i).start()

    def attend():
        attend_out(ctxb, qos.at[1], tok, n1, inv1, resid)
        for i in (9, 10): keep(i).start()
    run_order(HEAD_ORDER, {"pk": key_values, "ks": keys, "pq": queries, "qs": query_features, "mx": mix, "at": attend}, G.stage, S.stage)
    S.finish()
    G.end(wz, vloc, vout)
    for i in range(KEPT): keep(i).wait()


def head(ns, loc, dp, packed, vloc, tok, rf, vm):
    T, D = tok.shape
    nz = dp // 2
    M = rf.shape[1]
    P_ = D // 128
    shp = grad_shapes(dp, D, packed[0].shape[2], packed[2].shape[2], packed[3].shape[2])
    n = ns * P_ // 4
    pm, pf = (P_, T, 128), (P_, T, 2 * M)
    kept = [(pm, bf)] * 3 + [(pf, bf)] * 2 + [(pm, f32)] * 2 + [((T, D), bf), ((ns, P_, 256, 2 * M), bf), ((T, D), f32), ((T, 128), f32)]
    S = pltpu.SemaphoreType.DMA
    hb = pl.BlockSpec(memory_space=pl.ANY)
    scratch = gather_sems(dp) + [pltpu.VMEM(shp[0], bf), pltpu.VMEM(shp[1], bf), S((2,))] + [pltpu.VMEM(a, t) for a, t in kept] + [S((KEPT,))]
    scratch += [pltpu.VMEM((4, n, 128, M), f32), pltpu.VMEM((4, 8, 2 * M), f32), pltpu.VMEM((4, n, 128, M), bf), pltpu.VMEM((4, 8, 2 * M), f32)]
    scratch += state_scratch(n, M, bf) + [pltpu.VMEM((T, D), f32), pltpu.VMEM((8 * HEAD, 2 * M), bf)]
    return pl.pallas_call(
        partial(head_kernel, ns, loc, nz),
        out_shape=[jax.ShapeDtypeStruct(a, bf) for a in shp[:3]] + [jax.ShapeDtypeStruct((nz - 1, packed[3].shape[2], D), bf), jax.ShapeDtypeStruct((dp,) + vloc.shape, f32)] + [jax.ShapeDtypeStruct(a, t) for a, t in kept],
        in_specs=[hb] * 5 + [VM] * 3, out_specs=[hb] * (5 + KEPT),
        scratch_shapes=scratch,
        name="head",
        compiler_params=pltpu.CompilerParams(collective_id=1, has_side_effects=True, vmem_limit_bytes=ALLV),
    )(*packed, vloc, tok, rf, vm)


def ffn_kernel(nz, *refs):
    (vec, *given, win), wout, refs = refs[:6], refs[6:8 if nz else 7], refs[8 if nz else 7:]
    (gr1, gattn, sums, outh, gwin), refs = refs[:5], refs[5:]
    gwout, refs = refs[:6 if nz else 1], refs[6 if nz else 1:]
    (wi, wu, gwi, gwu, act, gp, hlow, acc, gr2, gffn, tr, n1, inv1, vm, cot, out, lsem, ssem, gsem), sems = refs[:19], refs[19:]
    sibs, sems = (sems[:2], sems[2:]) if nz else ((), sems)
    J, _, C = act.shape

    def rows(j): return ds(j, C)
    def load(j):
        return pltpu.make_async_copy(win.at[rows(j)], wi.at[rows(j)], lsem.at[j])
    def store(j):
        return pltpu.make_async_copy(gwi.at[rows(j)], gwin.at[rows(j)], ssem.at[j])
    def start_load(j, _):
        load(j).start()
        return 0
    def forward(j, _):
        load(j).wait()
        ffn_chunk(j, hlow, wi, act, gp)
        return 0
    def output(j, _):
        ffn_output(j, act, wu, acc, False)
        return 0
    def out_grad(j, _):
        ffn_out_grad(j, tr, act, gwu)
        return 0
    def backward(j, first):
        ffn_backward(j, gffn, hlow, wi, wu, gp, gwi, acc, first)
        store(j).start()
        return 0
    def some_backward(lo, hi):
        lax.fori_loop(lo, hi, lambda j, _: backward(j, False), 0)
    def end_store(j, _):
        store(j).wait()
        return 0
    here = [pltpu.make_async_copy(a, b, gsem.at[i]) for i, (a, b) in enumerate(zip(given, (n1, inv1, vm, cot)))]
    done_out = pltpu.make_async_copy(out, outh, gsem.at[4])

    def begin():
        for cp in here: cp.start()
        lax.fori_loop(0, J, start_load, 0)
        for cp in here: cp.wait()
        hidden_rows(n1, vec, hlow)
    if nz:
        wz, loc = wout
        r = loc.shape[2] // 2
        G = Gather(nz, (None, None, None, loc), (None, None, None, wu), sems[2:], r)
        entry_barrier([G.ynb, G.xnb, G.sib])
        G.relay(wz)
        begin()
        lax.fori_loop(0, J // 2, forward, 0)
        G.st2(EARLY)
        lax.fori_loop(J // 2, J - J // 6, forward, 0)
        G.st2(EARLY + 1)
        for g in (EARLY, EARLY + 1):
            for k in range(1, nz): G._wz_local(wz, g, k).wait()
        G.st3(EARLY)
        lax.fori_loop(J - J // 6, J, forward, 0)
        G.st3(EARLY + 1)
        G.done(EARLY)
        G.done(EARLY + 1)
    else:
        whole = pltpu.make_async_copy(wout[0], wu, ssem.at[0])
        whole.start()
        begin()
        lax.fori_loop(0, J, forward, 0)
        whole.wait()
    ffn_output(0, act, wu, acc, True)
    lax.fori_loop(1, J, output, 0)
    second_norm(acc, n1, vec, vm, cot, out, gr2, gffn, sums)
    done_out.start()
    tr[...] = gffn[...].T
    lax.fori_loop(0, J, out_grad, 0)
    if nz:
        sc = [()] * EARLY + [(sibs[0], *gwout[1:3]), (sibs[1], *gwout[4:])]
        kept = [pltpu.make_async_copy(sibs[i], gwout[3 * i], gsem.at[5 + i]) for i in range(2)]
        R = Reduce(nz, (None, None, None, gwu), (None,) * NG, sc, sems[:2], None, None, r)
        R.s0(EARLY)
        R.s0(EARLY + 1)
        backward(0, True)
        some_backward(1, J // 4)
        R.s1(EARLY)
        kept[0].start()
        some_backward(J // 4, J // 2)
        R.s1(EARLY + 1)
        kept[1].start()
        some_backward(J // 2, J)
    else:
        backward(0, True)
        some_backward(1, J)
    first_norm_back(acc, gr2, n1, inv1, vec, gr1, gattn, sums)
    if nz:
        for g in (EARLY, EARLY + 1): R.recv1(g)
        G.finish()
        R.finish()
        for cp in kept: cp.wait()
    done_out.wait()
    lax.fori_loop(0, J, end_store, 0)
    if not nz:
        cp = pltpu.make_async_copy(gwu, gwout[0], lsem.at[0])
        cp.start()
        cp.wait()


def ffn(n1, inv1, vec, vm, cot, win, wout, dp=0):
    T, D = n1.shape
    FF = win.shape[0]
    J = FF // COLS
    nz = dp // 2
    hb = pl.BlockSpec(memory_space=pl.ANY)
    S = pltpu.SemaphoreType.DMA
    ws, us, ch = (FF, D), (FF // D, D, D), (J, T, COLS)
    gs = (2, 2, dp, D // dp, D) if dp else us
    part_sums = [a for g in (EARLY, EARLY + 1) for a in reduce_shapes(nz, D, D // dp // 2, g)[:3]] if dp else [us]
    outs = [((T, D), f32), ((T, D), bf), ((4, 8, D), f32), ((T, D), bf), (ws, bf)] + [(a, bf) for a in part_sums]
    scratch = [(ws, bf), (gs, bf), (ws, bf), (gs, bf), (ch, bf), (ch, bf), ((T, D), bf), ((T, D), f32), ((T, D), f32), ((T, D), bf), ((D, T), bf)]
    scratch += [(n1.shape, f32), (inv1.shape, f32), (vm.shape, f32), ((T, D), bf), ((T, D), bf)]
    sems = [pltpu.VMEM(part_sums[0], bf)] * 2 + [S((NG, 2 * nz + 7)), S((NG, 2 * nz + 7))] + gather_sems(dp) if dp else []
    remote = dict(collective_id=3, has_side_effects=True) if dp else {}
    return pl.pallas_call(
        partial(ffn_kernel, nz),
        out_shape=[jax.ShapeDtypeStruct(a, t) for a, t in outs],
        in_specs=[VM] + [hb] * (5 + len(wout)), out_specs=[VM] * 3 + [hb] * 2 + ([hb, VM, VM] * 2 if dp else [hb]),
        scratch_shapes=[pltpu.VMEM(a, t) for a, t in scratch] + [S((J,)), S((J,)), S((7,))] + sems,
        name="ffn",
        compiler_params=pltpu.CompilerParams(vmem_limit_bytes=ALLV, **remote),
    )(vec, n1, inv1, vm, cot, win, *wout)


def mix_back_kernel(ns, loc, gattn, qow, ctxb, ctx, den, qp, qf, right, fbm, tok, gqo, gq, gst, gkt, tr):
    tr[...] = gattn[...].T
    weight_grad(tr, ctxb, gqo.at[1])
    mix_back_query(gattn, qow.at[1], qp, qf, right, ctx, den, fbm, gst, gkt, gq, ns, loc)
    weight_grad_pairs(gq, tok, gqo.at[0])


LATE = 11
TAIL_ORDER = (
    "wu1.2", "mq", "s.0", "gq", "wi0.0", "wo", "wu1.3", "wu0.2", "wi1.0", "wi0.1", "qo.0", "tq",
    "s.1", "wi1.1", "qo.1", "s.2", "mk", "wu0.3", "gkv", "kv.0", "wi1.2", "qo.2", "kv.1", "wi0.2",
    "wi1.3", "wu0.4", "qo.3", "kv.2", "wi1.4", "wu1.4", "wi0.3", "kv.3", "wu0.5", "qo.4", "wu1.5", "wi0.4",
    "wi1.5", "wi0.5", "wu0.6", "wu1.6", "kv.4", "qo.5", "wi1.6", "tk", "kv.5", "wi0.6", "kv.6", "qo.6",
)


def tail_kernel(ns, loc, nz, *refs):
    (gattn, ctxb, small, rf), refs = refs[:4], refs[4:]
    (gwin, gr1, *part_sums), refs = refs[:8], refs[8:]
    late, refs = refs[:LATE], refs[LATE:]
    tg, fins, sout, refs = refs[0], refs[1:5], refs[5], refs[6:]
    there, lsem, refs = refs[:LATE], refs[LATE], refs[LATE + 1:]
    (gkv, gqo, *own, gq, gk, gv, tr, gst, gkt, sto, kto), refs = refs[:12], refs[12:]
    (sb, srec, krec, ss, sr), refs = refs[:5], refs[5:]
    scratch, refs = [refs[g * 7:(g + 1) * 7] for g in range(NG)], refs[7 * NG:]
    rsend, rrecv, osem, sfirst, ssecond, qsend, qrecv, fbm = refs
    qow, qp, qf, right, ctx, den, tok, kp, vp, kf, kvw = there
    P_ = gq.shape[0]
    n = ns * P_ // 4

    def load(i):
        return pltpu.make_async_copy(late[i], there[i], lsem.at[i])
    grl = pltpu.make_async_copy(gr1, tg, lsem.at[LATE])
    early = [pltpu.make_async_copy(part_sums[i], scratch[EARLY + i // 3][i % 3], lsem.at[LATE + 1 + i]) for i in range(6)]
    for cp in early: cp.start()
    for i in range(LATE): load(i).start()
    grl.start()
    R = Reduce(nz, (gkv, gqo, gwin, None), (None, None, *own, None, None), scratch, (rsend, rrecv), osem, fins, gkv.shape[3])
    Q = SmallSum(nz, small, sout, sfirst, ssecond, (qsend, qrecv))
    S = StateSum(gst, gkt, sto, kto, sb, srec, krec, (ss, sr))
    entry_barrier(S.peers + Q.dpeer)
    Q.t0()
    fbm[...] = feature_pull(rf[...])
    wait_for = iter(range(LATE))

    def need(n):
        for _ in range(n): load(next(wait_for)).wait()

    def output_grad():
        tr[...] = gattn[...].T
        weight_grad_units(tr, ctxb, gqo.at[1])

    def mix_query():
        need(7)
        gkt[...] = jnp.zeros_like(gkt)
        mix_back_query(gattn, qow.at[1], qp, qf, right, ctx, den, fbm, Flat(gst, P_), FlatRow(gkt, P_, n), gq, ns, loc)

    def query_token():
        grl.wait()
        token_grad_query(gq, qow.at[0], tg)

    def mix_key():
        need(4)
        mix_back_key(kp, vp, kf, Flat(sto, P_), FlatRow(kto, P_, n), fbm, gk, gv, ns, loc)

    def key_grads():
        weight_grad_pairs_units(gk, tok, gkv.at[0])
        weight_grad_pairs_units(gv, tok, gkv.at[1])
        Q.t1()
    compute = {
        "wo": output_grad, "mq": mix_query, "gq": lambda: weight_grad_pairs_units(gq, tok, gqo.at[0]), "tq": query_token, "mk": mix_key,
        "gkv": key_grads, "tk": lambda: token_grad_keys(gk, gv, kvw.at[0], kvw.at[1], tg),
    }

    def stage(g, i):
        if g >= EARLY and i == 2:
            for cp in early[(g - EARLY) * 3:(g - EARLY) * 3 + 3]: cp.wait()
        R.stage(g, i)
    run_order(TAIL_ORDER, compute, stage, S.stage)
    Q.t2()
    S.finish()
    Q.finish()
    R.finish()


def tail(ns, loc, dp, gattn, ctxb, small, rf, gwin, gr1, part_sums, late):
    T, D = gattn.shape
    nz = dp // 2
    qf = late[2]
    P_, M = qf.shape[0], qf.shape[2] // 2
    part, ff = D // dp, gwin.shape[0]
    rows = (part // 2, part // 2, ff // dp // 4, part)
    shp = grad_shapes(dp, D, rows[0], rows[2], rows[3])
    n = ns * P_ // 4
    S = pltpu.SemaphoreType.DMA
    pm = pltpu.VMEM((P_, T, 128), bf)
    scratch = [pltpu.VMEM(a.shape, a.dtype) for a in late] + [S((LATE + 7,))]
    scratch += [pltpu.VMEM(shp[0], bf), pltpu.VMEM(shp[1], bf)] + [pltpu.VMEM((nz, 2, 2, rows[0], D), bf)] * 2
    scratch += [pm, pm, pm, pltpu.VMEM((D, T), bf), pltpu.VMEM((4, n, 128, M), f32), pltpu.VMEM((4, 8, 2 * M), f32)]
    scratch += [pltpu.VMEM((4, n, 128, M), bf), pltpu.VMEM((4, 8, 2 * M), f32)] + state_scratch(n, M, bf)
    scratch += [pltpu.VMEM(a, bf) for g in range(NG) for a in reduce_shapes(nz, D, rows[0], g)] + [S((NG, 2 * nz + 7)), S((NG, 2 * nz + 7)), S((NG, nz))] + small_scratch(dp) + [pltpu.VMEM((2 * M, 4 * HEAD), bf)]
    hb = pl.BlockSpec(memory_space=pl.ANY)
    return pl.pallas_call(
        partial(tail_kernel, ns, loc, nz),
        out_shape=[jax.ShapeDtypeStruct((T, D), f32)] + [jax.ShapeDtypeStruct((2, 2, r, D), bf) for r in rows] + [jax.ShapeDtypeStruct(small.shape[1:], f32)],
        in_specs=[VM] * 4 + [hb] * (8 + LATE), out_specs=[VM] * 6,
        scratch_shapes=scratch,
        name="tail",
        compiler_params=pltpu.CompilerParams(collective_id=2, has_side_effects=True, vmem_limit_bytes=ALLV),
    )(gattn, ctxb, small, rf, gwin.reshape(shp[2]), gr1, *part_sums, *late)


def last_kernel(ns, loc, kp, vp, kf, gst, gkt, fbm, gr1, gq, kvw, qow, tok, gkv, tg, gk, gv):
    mix_back_key(kp, vp, kf, gst, gkt, fbm, gk, gv, ns, loc)
    weight_grad_pairs(gk, tok, gkv.at[0])
    weight_grad_pairs(gv, tok, gkv.at[1])
    token_grad(gr1, gq, gk, gv, qow.at[0], kvw.at[0], kvw.at[1], tg)


def shards(tokens, lengths, random_features, w_query, w_key, w_value, w_output, w_in, w_out, ln1_gain, ln1_bias, ln2_gain, ln2_bias, cotangent):
    ns, loc, D = tokens.shape
    T = ns * loc
    dp, parts = lax.axis_size("dp"), lax.axis_size("seq")
    part = w_query.shape[1]
    FF = w_out.shape[0]
    M = random_features.shape[1]
    P_ = D // 128
    fast = parts == 4 and dp == 8 and part % 32 == 0 and D == part * dp and part <= 128 and ns * P_ % 4 == 0 and ns * P_ <= 32 and FF == 4 * D
    pos = lax.axis_index("seq") * loc + jnp.arange(loc, dtype=jnp.int32)
    valid = (pos[None, :] < lengths[:, None]).astype(f32).reshape(T, 1)
    vm = jnp.broadcast_to(valid, (T, 128))
    tok, cot = tokens.reshape(T, D), cotangent.reshape(T, D)
    vloc = jnp.stack([ln1_gain, ln1_bias, ln2_gain, ln2_bias]).astype(f32)
    pm, pf, stt, ktt = (P_, T, 128), (P_, T, 2 * M), (ns, P_, 128, M), (ns, P_, 8, 2 * M)
    if fast:
        vloc = jnp.pad(vloc, ((0, 4), (0, 128 - part)))
        packed = pack(w_query, w_key, w_value, w_output, w_in, w_out)
        kvw, qow, win, wz, vec, *kept = head(ns, loc, dp, packed, vloc, tok, random_features, vm)
        wout = wz, packed[3]
        kp, vp, qp, kf, qf, ctx, den, ctxb, right, n1, inv1 = kept
        vec = jnp.transpose(vec[:, :, :part], (1, 0, 2)).reshape(8, D)
    else:
        vec = jnp.pad(lax.all_gather(vloc, "dp", axis=1, tiled=True), ((0, 4), (0, 0)))
        def full(w):
            return lax.all_gather(w, "dp", axis=1, tiled=True).T
        kvw, qow = jnp.stack([full(w_key), full(w_value)]), jnp.stack([full(w_query), full(w_output)])
        win = full(w_in)
        wout = (jnp.transpose(full(w_out).reshape(D, FF // D, D), (1, 0, 2)),)
    kvw, qow, win = kvw.reshape(2, D, D), qow.reshape(2, D, D), win.reshape(FF, D)
    if not fast:
        wf, fbm = feature_matrix(random_features), feature_pull(random_features)
        kp, vp, qp, kf, qf, st, kt = call(
            partial(key_query_kernel, ns, loc), (tok, kvw, qow, wf, vm),
            [(pm, bf)] * 3 + [(pf, bf)] * 2 + [(stt, f32), (ktt, f32)], name="key_query")
        st, kt = lax.psum((st, kt), "seq")
        ctx, den, ctxb, right, n1, inv1 = call(
            partial(mix_kernel, ns, loc), (tok, qow, qf, st, kt),
            [(pm, f32), (pm, f32), ((T, D), bf), ((ns, P_, 256, 2 * M), bf), ((T, D), f32), ((T, 128), f32)],
            [pltpu.VMEM((T, D), f32)], name="mix")
    gr1, gattn, sums, out, gwin, *gwout = ffn(n1, inv1, vec, vm, cot, win, wout, dp if fast else 0)
    small = jnp.sum(jnp.concatenate([sums[2:], sums[:2]]), 1)
    if fast:
        small = jnp.transpose(jnp.pad(small.reshape(4, dp, part), ((0, 4), (0, 0), (0, 128 - part))), (1, 0, 2))
        tg, kvg, qog, wig, wug, small = tail(ns, loc, dp, gattn, ctxb, small, random_features, gwin, gr1, gwout, (qow, qp, qf, right, ctx, den, tok, kp, vp, kf, kvw))
        small = small[:, :part]
        wk_g, wv_g, wq_g, wo_g = kvg[0].reshape(part, D).T, kvg[1].reshape(part, D).T, qog[0].reshape(part, D).T, qog[1].reshape(part, D).T
        wi_g = wig.reshape(FF // dp, D).T
        wu_g = jnp.transpose(wug.reshape(FF // D, part, D), (0, 2, 1)).reshape(FF, part)
        grads = (wq_g, wk_g, wv_g, wo_g, wi_g, wu_g)
    else:
        gqo, gq, gst, gkt = call(
            partial(mix_back_kernel, ns, loc), (gattn, qow, ctxb, ctx, den, qp, qf, right, fbm, tok),
            [((2, D, D), bf), (pm, bf), (stt, f32), (ktt, f32)], [pltpu.VMEM((D, T), bf)], name="mix_back")
        gst, gkt = lax.psum((gst, gkt), "seq")
        gkv, tg = call(
            partial(last_kernel, ns, loc), (kp, vp, kf, gst, gkt, fbm, gr1, gq, kvw, qow, tok),
            [((2, D, D), bf), ((T, D), f32)], [pltpu.VMEM(pm, bf), pltpu.VMEM(pm, bf)], name="last")
        small = lax.psum(small, ("seq", "dp"))
        small = lax.dynamic_slice_in_dim(small, lax.axis_index("dp") * part, part, 1)
        whole = (gqo[0].T, gkv[0].T, gkv[1].T, gqo[1].T, gwin.T, jnp.transpose(gwout[0], (0, 2, 1)).reshape(FF, D))
        grads = tuple(lax.psum(lax.psum_scatter(g, "dp", scatter_dimension=1, tiled=True), "seq") for g in whole)
    return (out.reshape(tokens.shape), tg.reshape(tokens.shape), *(g.astype(f32) for g in grads), small[0], small[1], small[2], small[3])


def solution(mesh):
    rows, cols, vecs = P("dp", "seq", None), P(None, "dp"), P("dp")
    return jax.shard_map(
        shards,
        mesh=mesh,
        in_specs=(rows, vecs, P(), *([cols] * 6), *([vecs] * 4), rows),
        out_specs=(rows, rows, *([cols] * 6), *([vecs] * 4)),
        check_vma=False,
    )
```

```python
import functools
from functools import partial

import jax
import jax.numpy as jnp
from jax import lax
from jax.experimental import pallas as pl
from jax.experimental.pallas import tpu as pltpu
from jax.sharding import PartitionSpec as P

MESH = pl.DeviceIdType.MESH
bf, f32 = jnp.bfloat16, jnp.float32
HEAD = 64
EPS = 1e-12


def coords():
    s, d = lax.axis_index("seq"), lax.axis_index("dp")
    return s // 2, s % 2, d // 2, d % 2

def dev(y, x, z, c):
    return (y * 2 + x, z * 2 + c)

def entry_barrier(peers):
    sem = pltpu.get_barrier_semaphore()
    for p in peers:
        pl.semaphore_signal(sem, inc=1, device_id=p, device_id_type=MESH)
    pl.semaphore_wait(sem, len(peers))

GROUPS = ((0, 0), (1, 0), (2, 0), (2, 1), (3, 0), (3, 1))
NAMES = ("kv", "qo", "wi0", "wi1", "wu0", "wu1")
ZFIRST = (2,)
EARLY = 4
NG = len(GROUPS)

def some(g, r):
    return pl.ds(GROUPS[g][1] * r, r)
def piece(g, ref, d, y, x, r):
    i = GROUPS[g][0]
    if i < 2:  return ref.at[y, d, x]
    if i == 2: return ref.at[d, y, x, some(g, r)]
    return ref.at[y, x, d, some(g, r)]
def lpiece(g, ref, y, x, r):
    return ref.at[y, x, some(g, r)]
def local_rows(g, ref, r):
    return ref.at[:, :, some(g, r)]
def shard(g, ref, d, r):
    i = GROUPS[g][0]
    if i < 2:  return ref.at[:, d]
    if i == 2: return ref.at[d, :, :, some(g, r)]
    return ref.at[:, :, d, some(g, r)]

class Gather:
    def __init__(self, nz, loc, out, sems, r):
        self.nz, self.sems, self.r = nz, sems, r
        self.loc, self.out = [loc[i] for i, _ in GROUPS], [out[i] for i, _ in GROUPS]
        y, x, z, c = self.pos = coords()
        dp = nz * 2
        self.ynb, self.xnb, self.sib = dev(1 - y, x, z, c), dev(y, 1 - x, z, c), dev(y, x, z, 1 - c)
        self.zpeer = [dev(y, x, (z + k) % nz, c) for k in range(1, nz)]
        self.me = z * 2 + c
        self.dpeer = [dev(y, x, (self.me + k) % dp // 2, (self.me + k) % 2) for k in range(1, dp)]
        self.started = []
        half = loc[3].shape[-1] // 2
        self.H = (pl.ds(0, half), pl.ds(half, half))

    def _rc(self, src, dst, ssem, rsem, to):
        return pltpu.make_async_remote_copy(src_ref=src, dst_ref=dst, send_sem=ssem, recv_sem=rsem, device_id=to, device_id_type=MESH)

    def _go(self, *a):
        cp = self._rc(*a)
        cp.start()
        self.started.append(cp)

    def _recv(self, dst, ssem, rsem, to):
        self._rc(dst, dst, ssem, rsem, to).wait_recv()

    def _local(self, g):
        return pltpu.make_async_copy(local_rows(g, self.loc[g], self.r), shard(g, self.out[g], self.me, self.r), self.sems[10].at[g])

    def _own(self, g):
        ss, sr = self.sems[8:10]
        self._go(local_rows(g, self.loc[g], self.r), shard(g, self.out[g], self.me, self.r), ss.at[g, 0], sr.at[g, 0], self.sib)
        self._local(g).start()

    def _vlocal(self, vloc, vout):
        return pltpu.make_async_copy(vloc, vout.at[self.me], self.sems[10].at[NG])

    def start(self, wz, vloc, vout):
        zs, zr, vs, vr = *self.sems[:2], *self.sems[11:13]
        y, x, z, c = self.pos
        for g in range(EARLY):
            for k in range(1, self.nz):
                self._go(lpiece(g, self.loc[g], y, x, self.r), piece(g, self.out[g], self.me, y, x, self.r), zs.at[g, k-1], zr.at[g, k-1], self.zpeer[k-1])
            self._own(g)
        for k in range(1, self.nz):
            self._go(self.loc[EARLY].at[y, x], wz.at[k - 1], zs.at[EARLY, k-1], zr.at[EARLY, k-1], self.zpeer[k-1])
        for k in range(1, self.nz * 2):
            self._go(vloc, vout.at[self.me], vs.at[k - 1], vr.at[k - 1], self.dpeer[k - 1])
        self._vlocal(vloc, vout).start()

    def _wz_local(self, wz, g, k):
        y, x, z, c = self.pos
        return pltpu.make_async_copy(wz.at[k - 1, some(g, self.r)], piece(g, self.out[g], self._from(k, c), y, x, self.r), self.sems[0].at[g, k - 1])

    def relay(self, wz):
        xs, xr, ys, yr = self.sems[2:6]
        y, x, z, c = self.pos
        for g in range(EARLY, NG):
            for k in range(1, self.nz):
                p, src = piece(g, self.out[g], self._from(k, c), y, x, self.r), wz.at[k - 1, some(g, self.r)]
                self._go(src, p, xs.at[g, k-1], xr.at[g, k-1], self.xnb)
                self._go(src, p, ys.at[g, k-1], yr.at[g, k-1], self.ynb)
        for g in range(EARLY, NG):
            for k in range(1, self.nz): self._wz_local(wz, g, k).start()
            self._own(g)

    def stage(self, g, i):
        (None, self.st1, self.st2, self.st3, self.done)[i](g)

    def _from(self, k, c):
        return ((self.pos[2] + self.nz - k) % self.nz) * 2 + c

    def st1(self, g):
        zs, zr, xs, xr, ys, yr = self.sems[:6]
        y, x, z, c = self.pos
        for k in range(1, self.nz):
            p = piece(g, self.out[g], self._from(k, c), y, x, self.r)
            self._recv(p, zs.at[g, k-1], zr.at[g, k-1], self.zpeer[k-1])
            self._go(p, p, xs.at[g, k-1], xr.at[g, k-1], self.xnb)
            self._go(p, p, ys.at[g, k-1], yr.at[g, k-1], self.ynb)

    def st2(self, g):
        xs, xr, ys, yr, ds_, dr = self.sems[2:8]
        y, x, z, c = self.pos
        for k in range(1, self.nz):
            d = self._from(k, c)
            p = piece(g, self.out[g], d, y, 1 - x, self.r)
            self._recv(p, xs.at[g, k-1], xr.at[g, k-1], self.xnb)
            pa = p.at[:, self.H[0]]
            self._go(pa, pa, ds_.at[g, k-1, 0], dr.at[g, k-1, 0], self.ynb)
            p = piece(g, self.out[g], d, 1 - y, x, self.r)
            self._recv(p, ys.at[g, k-1], yr.at[g, k-1], self.ynb)
            pb = p.at[:, self.H[1]]
            self._go(pb, pb, ds_.at[g, k-1, 1], dr.at[g, k-1, 1], self.xnb)

    def st3(self, g):
        ds_, dr, ss, sr = self.sems[6:10]
        y, x, z, c = self.pos
        for k in range(1, self.nz):
            d = self._from(k, c)
            p = piece(g, self.out[g], d, 1 - y, 1 - x, self.r)
            pa, pb = p.at[:, self.H[0]], p.at[:, self.H[1]]
            self._recv(pa, ds_.at[g, k-1, 0], dr.at[g, k-1, 0], self.ynb)
            self._recv(pb, ds_.at[g, k-1, 1], dr.at[g, k-1, 1], self.xnb)
            sh = shard(g, self.out[g], d, self.r)
            self._go(sh, sh, ss.at[g, k], sr.at[g, k], self.sib)

    def done(self, g):
        ss, sr = self.sems[8:10]
        for k in range(self.nz):
            self._recv(shard(g, self.out[g], self._from(k, 1 - self.pos[3]), self.r), ss.at[g, k], sr.at[g, k], self.sib)
        self._local(g).wait()

    def end(self, wz, vloc, vout):
        zs, zr, vs, vr = *self.sems[:2], *self.sems[11:13]
        dp = self.nz * 2
        for k in range(1, self.nz):
            self._recv(wz.at[k - 1], zs.at[EARLY, k-1], zr.at[EARLY, k-1], self.zpeer[k-1])
        for k in range(1, dp):
            self._recv(vout.at[(self.me + dp - k) % dp], vs.at[k - 1], vr.at[k - 1], self.dpeer[k - 1])
        self._vlocal(vloc, vout).wait()
        self.finish()

    def finish(self):
        for cp in self.started:
            cp.wait_send()

def gather_sems(dp):
    nz = dp // 2
    n = nz - 1
    S = pltpu.SemaphoreType.DMA
    return [S((NG, n)) for _ in range(6)] + [S((NG, n, 2)), S((NG, n, 2)), S((NG, nz)), S((NG, nz)), S((NG + 1,)), S((dp - 1,)), S((dp - 1,))]

def pack(wq, wk, wv, wo, win, wout):
    D = wq.shape[0]
    sh = wq.shape[1]
    t = jnp.transpose
    kv = jnp.stack([t(wk), t(wv)]).reshape(2, 2, sh // 2, D)
    qo = jnp.stack([t(wq), t(wo)]).reshape(2, 2, sh // 2, D)
    wi = t(win).reshape(2, 2, win.shape[1] // 4, D)
    ff = wout.shape[0]
    wu = t(wout.reshape(ff // D, D, sh), (0, 2, 1)).reshape(2, 2, sh, D)
    return kv, qo, wi, wu


def nn(a, b): return lax.dot_general(a, b, (((1,), (0,)), ((), ())), preferred_element_type=f32)
def nt(a, b): return lax.dot_general(a, b, (((1,), (1,)), ((), ())), preferred_element_type=f32)
def tn(a, b): return lax.dot_general(a, b, (((0,), (0,)), ((), ())), preferred_element_type=f32)

def ds(i, n): return pl.ds(pl.multiple_of(i * n, n), n)

def mat(w):
    return w[...].reshape(-1, w.shape[-1])

def project(tok, w, dst):
    D = tok.shape[1]
    v = mat(w)
    for n in range(D // 256):
        o = nt(tok[...], v[n * 256:(n + 1) * 256, :]).astype(bf)
        dst[2 * n] = o[:, :128]
        dst[2 * n + 1] = o[:, 128:]

def features(x, wf):
    xf = x.astype(f32)
    sq = xf * xf
    hi = sq.astype(bf)
    lo = (sq - hi.astype(f32)).astype(bf)
    return jnp.exp(nn(jnp.concatenate([x, x, hi, lo], 1), wf[...]))

def pair_mask(m):
    r = lax.broadcasted_iota(jnp.int32, (128, 2 * m), 0) < HEAD
    c = lax.broadcasted_iota(jnp.int32, (128, 2 * m), 1) < m
    return (r == c)

def compact(st, m):
    return jnp.concatenate([st[:HEAD, :m], st[HEAD:, m:]], 0)

def key_side(kp, vp, wf, vm, kf, st, kt, nseq, loc):
    P_ = kp.shape[0]
    M = wf.shape[1] // 2
    def body(p, _):
        f = features(kp[p], wf) * jnp.concatenate([vm[...]] * (2 * M // 128), 1)
        fb = f.astype(bf)
        kf[p] = fb
        for b in range(nseq):
            rows = slice(b * loc, (b + 1) * loc)
            st[b, p] = compact(tn(vp[p, rows, :], fb[rows]), M)
            kt[b, p] = jnp.broadcast_to(jnp.sum(f[rows], 0, keepdims=True), (8, 2 * M))
        return 0
    lax.fori_loop(0, P_, body, 0)

def query_side(qp, wf, qf):
    def body(p, _):
        qf[p] = features(qp[p], wf).astype(bf)
        return 0
    lax.fori_loop(0, qp.shape[0], body, 0)

def build_right(st, kt, right, m):
    mask = pair_mask(m)
    nseq, P_ = right.shape[:2]
    for b in range(nseq):
        def body(p, _):
            c = st[b, p].astype(f32)
            s = jnp.where(mask, jnp.concatenate([c, c], 1), 0.0)
            t = jnp.where(mask, jnp.broadcast_to(kt[b, p][:1], (128, 2 * m)), 0.0)
            right[b, p] = jnp.concatenate([s, t], 0).astype(bf)
            return 0
        lax.fori_loop(0, P_, body, 0)

def mix_forward(qf, right, ctx, den, ctxb, nseq, loc):
    def body(p, _):
        for b in range(nseq):
            rows = slice(b * loc, (b + 1) * loc)
            o = nt(qf[p, rows, :], right[b, p])
            d = o[:, 128:]
            c = o[:, :128] / d
            ctx[p, rows, :] = c
            den[p, rows, :] = d
            ctxb[rows, ds(p, 128)] = c.astype(bf)
        return 0
    lax.fori_loop(0, qf.shape[0], body, 0)

def mean(a): return jnp.mean(a, -1, keepdims=True)

def attend_out(ctxb, wo, tok, n1, inv1, resid):
    T, D = tok.shape
    v = mat(wo)
    for n in range(D // 256):
        resid[:, n * 256:(n + 1) * 256] = nt(ctxb[...], v[n * 256:(n + 1) * 256, :])
    R = 64
    def body(i, _):
        r = ds(i, R)
        x = tok[r, :].astype(f32) + resid[r, :]
        cen = x - mean(x)
        inv = lax.rsqrt(mean(cen * cen) + EPS)
        n1[r, :] = cen * inv
        inv1[r, :] = jnp.broadcast_to(inv, (R, 128))
        return 0
    lax.fori_loop(0, T // R, body, 0)

def ffn_chunk(j, hlow, win, act, gp):
    C = act.shape[2]
    pre = nt(hlow[...], win[ds(j, C), :])
    cdf = 0.5 * (1.0 + lax.erf(pre * 0.7071067811865476))
    act[j] = (pre * cdf).astype(bf)
    gp[j] = (cdf + pre * (jnp.exp(-0.5 * pre * pre) * 0.3989422804014327)).astype(bf)

def out_columns(wout, j, C):
    per = wout.shape[-1] // C
    jj, cc = j // per, ds(lax.rem(j, per), C)
    if len(wout.shape) == 3:
        return wout[jj, :, cc]
    return wout[jj // 2, lax.rem(jj, 2), :, :, cc].reshape(-1, C)

def ffn_output(j, act, wout, acc, first):
    o = nt(act[j], out_columns(wout, j, act.shape[2]))
    if first: acc[...] = o
    else: acc[...] += o

def hidden_rows(n1, vec, hlow):
    R = 64
    def body(i, _):
        r = ds(i, R)
        hlow[r, :] = (n1[r, :] * vec[0:1, :] + vec[1:2, :]).astype(bf)
        return 0
    lax.fori_loop(0, n1.shape[0] // R, body, 0)

def fold8(a):
    return jnp.sum(a.reshape(a.shape[0] // 8, 8, a.shape[1]), 0)

def norm_pull(g, n, inv, gain):
    e = g * gain
    return inv * (e - mean(e) - n * mean(e * n))

def second_norm(acc, n1, vec, vm, cot, out, gr2, gffn, sums):
    T, D = acc.shape
    R = 64
    sums[0] = jnp.zeros((8, D), f32)
    sums[1] = jnp.zeros((8, D), f32)
    def body(i, _):
        r = ds(i, R)
        x = n1[r, :] * vec[0:1, :] + vec[1:2, :] + acc[r, :]
        cen = x - mean(x)
        inv = lax.rsqrt(mean(cen * cen) + EPS)
        n = cen * inv
        v = vm[r, :]
        vv = jnp.concatenate([v] * (D // 128), 1)
        out[r, :] = ((n * vec[2:3, :] + vec[3:4, :]) * vv).astype(bf)
        gy = cot[r, :].astype(f32) * vv
        sums[0] += fold8(gy * n)
        sums[1] += fold8(gy)
        g = norm_pull(gy, n, inv, vec[2:3, :])
        gr2[r, :] = g
        gffn[r, :] = g.astype(bf)
        return 0
    lax.fori_loop(0, T // R, body, 0)

def ffn_out_grad(j, gffn_t, act, gwout):
    C = act.shape[2]
    per = gwout.shape[-1] // C
    o = nn(gffn_t[...], act[j]).astype(bf)
    jj, cc = j // per, ds(lax.rem(j, per), C)
    if len(gwout.shape) == 3:
        gwout[jj, :, cc] = o
    else:
        gwout[jj // 2, lax.rem(jj, 2), :, :, cc] = o.reshape(gwout.shape[2], gwout.shape[3], C)

def ffn_backward(j, gffn, hlow, win, wout, gp, gwin, gh, first):
    C = gp.shape[2]
    ga = nn(gffn[...], out_columns(wout, j, C))
    gpre = (ga * gp[j].astype(f32)).astype(bf)
    gwin[ds(j, C), :] = tn(gpre, hlow[...]).astype(bf)
    o = nn(gpre, win[ds(j, C), :])
    if first: gh[...] = o
    else: gh[...] += o

def first_norm_back(gh, gr2, n1, inv1, vec, gr1, gattn, sums):
    T, D = gh.shape
    R = 64
    sums[2] = jnp.zeros((8, D), f32)
    sums[3] = jnp.zeros((8, D), f32)
    def body(i, _):
        r = ds(i, R)
        g = gr2[r, :] + gh[r, :]
        n = n1[r, :]
        sums[2] += fold8(g * n)
        sums[3] += fold8(g)
        o = norm_pull(g, n, inv1[r, :][:, :1], vec[0:1, :])
        gr1[r, :] = o
        gattn[r, :] = o.astype(bf)
        return 0
    lax.fori_loop(0, T // R, body, 0)

def put_units(dst, n, o):
    dp, _, a, _ = dst.shape
    for u in range(dp):
        i = n * dp + u
        dst[i // 2, i % 2] = o[u * a:(u + 1) * a].astype(bf)

def weight_grad_units(gt, x, dst):
    h = gt.shape[0] // 2
    for n in range(2):
        put_units(dst, n, nn(gt[n * h:(n + 1) * h, :], x[...]))

def weight_grad_pairs_units(gp_, x, dst):
    h = gp_.shape[0] // 2
    for n in range(2):
        g = jnp.concatenate([gp_[n * h + i] for i in range(h)], 1)
        put_units(dst, n, tn(g, x[...]))

def weight_grad(gt, x, dst):
    D = x.shape[1]
    for n in range(D // 256):
        dst[n * 256:(n + 1) * 256, :] = nn(gt[n * 256:(n + 1) * 256, :], x[...]).astype(bf)

def weight_grad_pairs(gp_, x, dst):
    P_ = gp_.shape[0]
    for n in range(P_ // 2):
        g = jnp.concatenate([gp_[2 * n], gp_[2 * n + 1]], 1)
        dst[n * 256:(n + 1) * 256, :] = tn(g, x[...]).astype(bf)

def mix_back_query(gattn, wo, qp, qf, right, ctx, den, fbm, gst, gkt, gq, nseq, loc):
    M = qf.shape[2] // 2
    mask = pair_mask(M)
    def body(p, _):
        gc = nn(gattn[...], wo[:, ds(p, 128)]).astype(bf).astype(f32)
        gn = gc / den[p]
        t = -gn * ctx[p]
        g = jnp.concatenate([gn, t], 1).astype(bf)
        for b in range(nseq):
            rows = slice(b * loc, (b + 1) * loc)
            q = qf[p, rows, :]
            s = tn(g[rows], q)
            gst[b, p] = compact(s[:128], M)
            gkt[b, p] = jnp.broadcast_to(jnp.sum(jnp.where(mask, s[128:], 0.0), 0, keepdims=True), (8, 2 * M))
            pr = (nn(g[rows], right[b, p]) * q.astype(f32)).astype(bf)
            o = nn(pr, fbm[...])
            gq[p, rows, :] = (o[:, :128] - 0.125 * qp[p, rows, :].astype(f32) * o[:, 128:]).astype(bf)
        return 0
    lax.fori_loop(0, qf.shape[0], body, 0)

def mix_back_key(kp, vp, kf, gst, gkt, fbm, gk, gv, nseq, loc):
    M = kf.shape[2] // 2
    mask = pair_mask(M)
    def body(p, _):
        for b in range(nseq):
            rows = slice(b * loc, (b + 1) * loc)
            c = gst[b, p].astype(f32)
            s = jnp.where(mask, jnp.concatenate([c, c], 1), 0.0).astype(bf)
            k = kf[p, rows, :]
            pr = ((nn(vp[p, rows, :], s) + gkt[b, p][:1]) * k.astype(f32)).astype(bf)
            o = nn(pr, fbm[...])
            gk[p, rows, :] = (o[:, :128] - 0.125 * kp[p, rows, :].astype(f32) * o[:, 128:]).astype(bf)
            gv[p, rows, :] = nt(k, s).astype(bf)
        return 0
    lax.fori_loop(0, kf.shape[0], body, 0)

def join(g):
    return jnp.concatenate([g[i] for i in range(g.shape[0])], 1)

def token_grad(gr1, gq, gk, gv, wq, wk, wv, dst):
    D = gr1.shape[1]
    for n in range(D // 256):
        c = slice(n * 256, (n + 1) * 256)
        dst[:, c] = gr1[:, c] + (nn(join(gq), wq[:, c]) + nn(join(gk), wk[:, c]) + nn(join(gv), wv[:, c]))

def token_grad_query(gq, wq, dst):
    D = dst.shape[1]
    for n in range(D // 256):
        c = slice(n * 256, (n + 1) * 256)
        dst[:, c] += nn(join(gq), wq[:, c])

def token_grad_keys(gk, gv, wk, wv, dst):
    D = dst.shape[1]
    for n in range(D // 256):
        c = slice(n * 256, (n + 1) * 256)
        dst[:, c] += nn(join(gk), wk[:, c]) + nn(join(gv), wv[:, c])

def split_features(rf):
    w = rf * HEAD ** (-0.25)
    hi = w.astype(bf)
    lo = (w - hi.astype(f32)).astype(bf)
    z = jnp.zeros(rf.shape, bf)
    def bd(a): return jnp.concatenate([jnp.concatenate([a, z], 1), jnp.concatenate([z, a], 1)], 0)
    return hi, lo, bd

def feature_matrix(rf):
    hi, lo, bd = split_features(rf)
    s = bd(jnp.full(rf.shape, -0.0625, bf))
    return jnp.concatenate([bd(hi), bd(lo), s, s], 0)

def feature_pull(rf):
    hi, lo, bd = split_features(rf)
    return jnp.concatenate([bd(hi), bd(jnp.ones(rf.shape, bf))], 0).T


class Reduce:
    def __init__(self, nz, grads, own, scratch, sems, own_sem, fins, r):
        self.nz, self.own, self.own_sem, self.sem, self.r, self.sc = nz, own, own_sem, sems, r, scratch
        self.grads = [grads[i] for i, _ in GROUPS]
        if fins is not None:
            self.fins = [local_rows(g, fins[GROUPS[g][0]], r) for g in range(NG)]
            self.h = fins[0].shape[-1] // 2
        else:
            self.h = grads[3].shape[-1] // 2
        self.started = []
        y, x, z, c = self.pos = coords()
        self.ynb, self.xnb, self.sibdev = dev(1 - y, x, z, c), dev(y, 1 - x, z, c), dev(y, x, z, 1 - c)
        self.zpeer = [dev(y, x, (z + k) % nz, c) for k in range(1, nz)]
        self.A, self.B = pl.ds(0, self.h), pl.ds(self.h, self.h)

    def _cp(self, src, dst, g, i, to):
        s, r = self.sem
        return pltpu.make_async_remote_copy(src_ref=src, dst_ref=dst, send_sem=s.at[g, i], recv_sem=r.at[g, i], device_id=to, device_id_type=MESH)

    def _go(self, src, dst, g, i, to):
        cp = self._cp(src, dst, g, i, to)
        cp.start()
        self.started.append(cp)

    def _recv(self, dst, g, i, to):
        self._cp(dst, dst, g, i, to).wait_recv()

    def stage(self, g, i):
        late = g in ZFIRST
        (self.s0, self.z1 if late else self.s1, self.z2 if late else self.s2, self.z3 if late else self.s3, self.z4 if late else self.s4, self.s5, self.s6)[i](g)

    def s0(self, g):
        c = self.pos[3]
        sib = self.sc[g][0]
        for k in range(self.nz):
            self._go(shard(g, self.grads[g], k * 2 + 1 - c, self.r), sib.at[k], g, k, self.sibdev)
        if self.own[g] is not None:
            for k in range(self.nz):
                self._own(g, k).start()

    def _own(self, g, k):
        c = self.pos[3]
        return pltpu.make_async_copy(shard(g, self.grads[g], k * 2 + c, self.r), self.own[g].at[k], self.own_sem.at[g, k])

    def _pair(self, g):
        c = self.pos[3]
        sib, own, gr = self.sc[g][0], self.own[g], self.grads[g]
        for k in range(self.nz):
            self._recv(sib.at[k], g, k, self.sibdev)
            if own is not None:
                self._own(g, k).wait()
        def body(i, _):
            k, q = i // 4, lax.rem(i, 4)
            qy, qx = q // 2, lax.rem(q, 2)
            mine = piece(g, gr, k * 2 + c, qy, qx, self.r) if own is None else own.at[k, qy, qx]
            sib[k, qy, qx] = (sib[k, qy, qx].astype(f32) + mine[...].astype(f32)).astype(bf)
            return 0
        lax.fori_loop(0, self.nz * 4, body, 0)

    def s1(self, g):
        y, x, z, c = self.pos
        sib, a1, b1 = self.sc[g][:3]
        self._pair(g)
        self._go(sib.at[:, :, 1 - x, :, self.A], a1, g, self.nz, self.xnb)
        self._go(sib.at[:, 1 - y, :, :, self.B], b1, g, self.nz + 1, self.ynb)

    def recv1(self, g):
        a1, b1 = self.sc[g][1:3]
        self._recv(a1, g, self.nz, self.xnb)
        self._recv(b1, g, self.nz + 1, self.ynb)

    def s2(self, g):
        y, x, z, c = self.pos
        nz, h = self.nz, self.h
        sib, a1, b1, a2, b2 = self.sc[g][:5]
        if g < EARLY:
            self.recv1(g)
        def body(i, _):
            k, j = i // 2, lax.rem(i, 2)
            a1[k, j] = (a1[k, j].astype(f32) + sib[k, j, x, :, :h].astype(f32)).astype(bf)
            b1[k, j] = (b1[k, j].astype(f32) + sib[k, y, j, :, h:].astype(f32)).astype(bf)
            return 0
        lax.fori_loop(0, nz * 2, body, 0)
        self._go(a1.at[:, 1 - y], a2, g, nz + 2, self.ynb)
        self._go(b1.at[:, 1 - x], b2, g, nz + 3, self.xnb)

    def s3(self, g):
        y, x, z, c = self.pos
        nz, h = self.nz, self.h
        a1, b1, a2, b2, tot, zrec = self.sc[g][1:]
        self._recv(a2, g, nz + 2, self.ynb)
        self._recv(b2, g, nz + 3, self.xnb)
        def body(k, _):
            tot[k, :, :h] = (a1[k, y].astype(f32) + a2[k].astype(f32)).astype(bf)
            tot[k, :, h:] = (b1[k, x].astype(f32) + b2[k].astype(f32)).astype(bf)
            return 0
        lax.fori_loop(0, nz, body, 0)
        for k in range(1, nz):
            self._go(tot.at[(z + k) % nz], zrec.at[k - 1], g, nz + 3 + k, self.zpeer[k - 1])

    def s4(self, g):
        y, x, z, c = self.pos
        nz, fin = self.nz, self.fins[g]
        tot, zrec = self.sc[g][5:]
        for k in range(1, nz):
            self._recv(zrec.at[k - 1], g, nz + 3 + k, self.zpeer[k - 1])
        t = tot[z].astype(f32)
        for k in range(1, nz):
            t = t + zrec[k - 1].astype(f32)
        fin[y, x] = t.astype(bf)
        self._spread(g)

    def z1(self, g):
        z = self.pos[2]
        sib, zrec = self.sc[g][0], self.sc[g][6]
        self._pair(g)
        for k in range(1, self.nz):
            self._go(sib.at[(z + k) % self.nz], zrec.at[k - 1], g, self.nz + 3 + k, self.zpeer[k - 1])

    def z2(self, g):
        y, x, z, c = self.pos
        nz = self.nz
        sib, a1, b1, a2, b2, tot, zrec = self.sc[g]
        for k in range(1, nz):
            self._recv(zrec.at[k - 1], g, nz + 3 + k, self.zpeer[k - 1])
        def body(i, _):
            j, l = i // 2, lax.rem(i, 2)
            t = sib[z, j, l].astype(f32)
            for k in range(1, nz):
                t = t + zrec[k - 1, j, l].astype(f32)
            tot[j, l] = t.astype(bf)
            return 0
        lax.fori_loop(0, 4, body, 0)
        self._go(tot.at[:, 1 - x, :, self.A], a1, g, nz, self.xnb)
        self._go(tot.at[1 - y, :, :, self.B], b1, g, nz + 1, self.ynb)

    def z3(self, g):
        y, x, z, c = self.pos
        nz, h = self.nz, self.h
        sib, a1, b1, a2, b2, tot, zrec = self.sc[g]
        self._recv(a1, g, nz, self.xnb)
        self._recv(b1, g, nz + 1, self.ynb)
        for j in range(2):
            a1[j] = (a1[j].astype(f32) + tot[j, x, :, :h].astype(f32)).astype(bf)
            b1[j] = (b1[j].astype(f32) + tot[y, j, :, h:].astype(f32)).astype(bf)
        self._go(a1.at[1 - y], a2, g, nz + 2, self.ynb)
        self._go(b1.at[1 - x], b2, g, nz + 3, self.xnb)

    def z4(self, g):
        y, x, z, c = self.pos
        nz, h, fin = self.nz, self.h, self.fins[g]
        a1, b1, a2, b2 = self.sc[g][1:5]
        self._recv(a2, g, nz + 2, self.ynb)
        self._recv(b2, g, nz + 3, self.xnb)
        fin[y, x, :, :h] = (a1[y].astype(f32) + a2[...].astype(f32)).astype(bf)
        fin[y, x, :, h:] = (b1[x].astype(f32) + b2[...].astype(f32)).astype(bf)
        self._spread(g)

    def _spread(self, g):
        y, x, z, c = self.pos
        a, b = self.fins[g].at[y, x, :, self.A], self.fins[g].at[y, x, :, self.B]
        self._go(a, a, g, 2 * self.nz + 3, self.xnb)
        self._go(b, b, g, 2 * self.nz + 4, self.ynb)

    def s5(self, g):
        y, x, z, c = self.pos
        nz, fin = self.nz, self.fins[g]
        self._recv(fin.at[y, 1 - x, :, self.A], g, 2 * nz + 3, self.xnb)
        self._recv(fin.at[1 - y, x, :, self.B], g, 2 * nz + 4, self.ynb)
        a, b = fin.at[y, :, :, self.A], fin.at[:, x, :, self.B]
        self._go(a, a, g, 2 * nz + 5, self.ynb)
        self._go(b, b, g, 2 * nz + 6, self.xnb)

    def s6(self, g):
        y, x, z, c = self.pos
        nz, fin = self.nz, self.fins[g]
        self._recv(fin.at[1 - y, :, :, self.A], g, 2 * nz + 5, self.ynb)
        self._recv(fin.at[:, 1 - x, :, self.B], g, 2 * nz + 6, self.xnb)

    def finish(self):
        for cp in self.started:
            cp.wait_send()

def grad_shapes(dp, D, a, b, c_):
    return [(2, dp, 2, a, D), (2, dp, 2, a, D), (dp, 2, 2, b, D), (2, 2, dp, c_, D)]

def reduce_shapes(nz, D, r, g):
    h = D // 2
    if g in ZFIRST:
        return (nz, 2, 2, r, D), (2, r, h), (2, r, h), (r, h), (r, h), (2, 2, r, D), (nz - 1, 2, 2, r, D)
    return (nz, 2, 2, r, D), (nz, 2, r, h), (nz, 2, r, h), (nz, r, h), (nz, r, h), (nz, r, D), (nz - 1, r, D)

class SmallSum:
    def __init__(self, nz, src, dst, first, second, sems):
        self.dp, self.src, self.dst, self.first, self.second, self.sem = nz * 2, src, dst, first, second, sems
        y, x, z, c = coords()
        self.me, self.seq, dp = z * 2 + c, y * 2 + x, nz * 2
        self.dpeer = [dev(y, x, (self.me + k) % dp // 2, (self.me + k) % 2) for k in range(1, dp)]
        self.speer = [dev(y, 1 - x, z, c), dev(1 - y, x, z, c), dev(1 - y, 1 - x, z, c)]
        self.sid = [y * 2 + 1 - x, (1 - y) * 2 + x, (1 - y) * 2 + 1 - x]
        self.started = []

    def peers(self):
        return self.dpeer + self.speer

    def _cp(self, src, dst, i, to):
        s, r = self.sem
        return pltpu.make_async_remote_copy(src_ref=src, dst_ref=dst, send_sem=s.at[i], recv_sem=r.at[i], device_id=to, device_id_type=MESH)

    def _go(self, *a):
        cp = self._cp(*a)
        cp.start()
        self.started.append(cp)

    def t0(self):
        for k in range(1, self.dp):
            self._go(self.src, self.first.at[k - 1], k - 1, self.dpeer[k - 1])

    def t1(self):
        t = self.src[...]
        for k in range(1, self.dp):
            self._cp(self.first.at[k - 1], self.first.at[k - 1], k - 1, self.dpeer[k - 1]).wait_recv()
            t = t + self.first[k - 1]
        self.second[self.seq] = t
        for i in range(3):
            self._go(self.second.at[self.seq], self.second.at[self.seq], self.dp - 1 + i, self.speer[i])

    def t2(self):
        for i in range(3):
            self._cp(self.second.at[self.sid[i]], self.second.at[self.sid[i]], self.dp - 1 + i, self.speer[i]).wait_recv()
        self.dst[...] = (self.second[0] + self.second[1]) + (self.second[2] + self.second[3])

    def finish(self):
        for cp in self.started:
            cp.wait_send()

def small_scratch(dp, D):
    S = pltpu.SemaphoreType.DMA
    return [pltpu.VMEM((dp - 1, 8, D), f32), pltpu.VMEM((4, 8, D), f32), S((dp + 2,)), S((dp + 2,)), pltpu.VMEM((8, D), f32)]

class StateSum:
    def __init__(self, st, kt, sto, kto, sb, srec, krec, sems):
        self.st, self.kt, self.sto, self.kto, self.srec, self.krec, self.sem = st, kt, sto, kto, srec, krec, sems
        self.sb = st if sb is None else sb
        y, x, z, c = coords()
        self.peers = [dev(y, 1 - x, z, c), dev(1 - y, x, z, c), dev(1 - y, 1 - x, z, c)]
        self.sid = [y * 2 + 1 - x, (1 - y) * 2 + x, (1 - y) * 2 + 1 - x]
        self.me = y * 2 + x
        self.started = []

    def _cp(self, src, dst, i, k):
        s, r = self.sem
        return pltpu.make_async_remote_copy(src_ref=src, dst_ref=dst, send_sem=s.at[i, k], recv_sem=r.at[i, k], device_id=self.peers[k], device_id_type=MESH)

    def _go(self, *a):
        cp = self._cp(*a)
        cp.start()
        self.started.append(cp)

    def _recv(self, dst, i, k):
        self._cp(dst, dst, i, k).wait_recv()

    def start(self):
        if self.sb is not self.st:
            self.sb[...] = self.st[...].astype(self.sb.dtype)
        for k in range(3):
            self._go(self.sb.at[self.sid[k]], self.srec.at[k], 0, k)
            self._go(self.kt.at[self.sid[k]], self.krec.at[k], 1, k)

    def stage(self, i):
        (self.start, self.mid, self.end)[i]()

    def mid(self):
        me = self.me
        t, u = self.st[me], self.kt[me]
        for k in range(3):
            self._recv(self.srec.at[k], 0, k)
            self._recv(self.krec.at[k], 1, k)
            t = t + self.srec[k].astype(f32)
            u = u + self.krec[k]
        self.sto[me] = t.astype(self.sto.dtype)
        self.kto[me] = u
        for k in range(3):
            self._go(self.sto.at[me], self.sto.at[me], 2, k)
            self._go(self.kto.at[me], self.kto.at[me], 3, k)

    def end(self):
        for k in range(3):
            self._recv(self.sto.at[self.sid[k]], 2, k)
            self._recv(self.kto.at[self.sid[k]], 3, k)

    def finish(self):
        for cp in self.started:
            cp.wait_send()

class Flat:
    def __init__(self, ref, pairs):
        self.ref, self.pairs = ref, pairs

    def _at(self, i):
        f = i[0] * self.pairs + i[1]
        return (f // self.ref.shape[1], f % self.ref.shape[1])

    def __getitem__(self, i):
        return self.ref[self._at(i)]

    def __setitem__(self, i, v):
        self.ref[self._at(i)] = v

class FlatRow:
    def __init__(self, ref, pairs, n):
        self.ref, self.pairs, self.n = ref, pairs, n

    def _at(self, i):
        f = i[0] * self.pairs + i[1]
        return (f // self.n, pl.ds(f % self.n, 1), slice(None))

    def __getitem__(self, i):
        return self.ref[self._at(i)]

    def __setitem__(self, i, v):
        self.ref[self._at(i)] = v[:1]

def state_scratch(n, M, dtype):
    S = pltpu.SemaphoreType.DMA
    sb = [] if dtype == f32 else [pltpu.VMEM((4, n, 128, M), dtype)]
    return sb + [pltpu.VMEM((3, n, 128, M), dtype), pltpu.VMEM((3, 8, 2 * M), f32), S((4, 3)), S((4, 3))]

VM = pl.BlockSpec(memory_space=pltpu.VMEM)
ALLV = 67043328
COLS = 256


def call(body, ins, outs, scratch=(), name=None):
    return pl.pallas_call(
        body,
        out_shape=[jax.ShapeDtypeStruct(s, d) for s, d in outs],
        in_specs=[VM] * len(ins),
        out_specs=[VM] * len(outs),
        scratch_shapes=list(scratch),
        name=name,
        compiler_params=pltpu.CompilerParams(vmem_limit_bytes=ALLV),
    )(*ins)


def key_query_kernel(ns, loc, tok, kvw, qow, wf, vm, kp, vp, qp, kf, qf, st, kt):
    project(tok, kvw.at[0], kp)
    project(tok, kvw.at[1], vp)
    project(tok, qow.at[0], qp)
    key_side(kp, vp, wf, vm, kf, st, kt, ns, loc)
    query_side(qp, wf, qf)


def mix_kernel(ns, loc, tok, qow, qf, st, kt, ctx, den, ctxb, right, n1, inv1, resid):
    build_right(st, kt, right, qf.shape[2] // 2)
    mix_forward(qf, right, ctx, den, ctxb, ns, loc)
    attend_out(ctxb, qow.at[1], tok, n1, inv1, resid)


KEPT = 11
HEAD_ORDER = (
    "kv.1", "kv.2", "qo.1", "kv.3", "wi0.1", "kv.4", "qo.2", "pk", "wi1.1", "ks", "qo.3", "s.0",
    "wi0.2", "s.1", "wi0.3", "qo.4", "pq", "qs", "s.2", "wi1.2", "mx", "wi1.3", "wi0.4", "at",
    "wi1.4",
)


def run_order(order, compute, stage, state):
    for op in order:
        if op in compute:
            compute[op]()
        else:
            name, i = op.split(".")
            if name == "s":
                state(int(i))
            else:
                stage(NAMES.index(name), int(i))


def head_kernel(ns, loc, nz, *refs):
    local, (vloc, tok, rf, vm), refs = refs[:4], refs[4:8], refs[8:]
    whole, wz, vout, kept, refs = (*refs[:3], None), refs[3], refs[4], refs[5:5 + KEPT], refs[5 + KEPT:]
    sems, (kvs, qos, lsem), here, ksem, refs = refs[:13], refs[13:16], refs[16:16 + KEPT], refs[16 + KEPT], refs[17 + KEPT:]
    st, kt, sto, kto, sb, srec, krec, ss, sr, resid, wf = refs
    kp, vp, qp, kf, qf, ctx, den, ctxb, right, n1, inv1 = here
    P_, M = qf.shape[0], qf.shape[2] // 2
    n = ns * P_ // 4

    def keep(i):
        return pltpu.make_async_copy(here[i], kept[i], ksem.at[i])

    def load(i, dst):
        return pltpu.make_async_copy(whole[i], dst, lsem.at[i])
    G = Gather(nz, local, whole, sems, local[0].shape[2])
    S = StateSum(st, kt, sto, kto, sb, srec, krec, (ss, sr))
    entry_barrier([G.ynb, S.peers[0], S.peers[2]] + G.dpeer)
    G.start(wz, vloc, vout)
    wf[...] = feature_matrix(rf[...])

    def key_values():
        load(0, kvs).start()
        load(0, kvs).wait()
        project(tok, kvs.at[0], kp)
        project(tok, kvs.at[1], vp)
        for i in (0, 1): keep(i).start()

    def keys():
        kt[...] = jnp.zeros_like(kt)
        key_side(kp, vp, wf, vm, kf, Flat(st, P_), FlatRow(kt, P_, n), ns, loc)
        keep(3).start()

    def queries():
        load(1, qos).start()
        load(1, qos).wait()
        project(tok, qos.at[0], qp)
        keep(2).start()

    def query_features():
        query_side(qp, wf, qf)
        keep(4).start()

    def mix():
        build_right(Flat(sto, P_), FlatRow(kto, P_, n), right, M)
        mix_forward(qf, right, ctx, den, ctxb, ns, loc)
        for i in (5, 6, 7, 8): keep(i).start()

    def attend():
        attend_out(ctxb, qos.at[1], tok, n1, inv1, resid)
        for i in (9, 10): keep(i).start()
    run_order(HEAD_ORDER, {"pk": key_values, "ks": keys, "pq": queries, "qs": query_features, "mx": mix, "at": attend}, G.stage, S.stage)
    S.finish()
    G.end(wz, vloc, vout)
    for i in range(KEPT): keep(i).wait()


def head(ns, loc, dp, packed, vloc, tok, rf, vm):
    T, D = tok.shape
    nz = dp // 2
    M = rf.shape[1]
    P_ = D // 128
    shp = grad_shapes(dp, D, packed[0].shape[2], packed[2].shape[2], packed[3].shape[2])
    n = ns * P_ // 4
    pm, pf = (P_, T, 128), (P_, T, 2 * M)
    kept = [(pm, bf)] * 3 + [(pf, bf)] * 2 + [(pm, f32)] * 2 + [((T, D), bf), ((ns, P_, 256, 2 * M), bf), ((T, D), f32), ((T, 128), f32)]
    S = pltpu.SemaphoreType.DMA
    hb = pl.BlockSpec(memory_space=pl.ANY)
    scratch = gather_sems(dp) + [pltpu.VMEM(shp[0], bf), pltpu.VMEM(shp[1], bf), S((2,))] + [pltpu.VMEM(a, t) for a, t in kept] + [S((KEPT,))]
    scratch += [pltpu.VMEM((4, n, 128, M), f32), pltpu.VMEM((4, 8, 2 * M), f32), pltpu.VMEM((4, n, 128, M), bf), pltpu.VMEM((4, 8, 2 * M), f32)]
    scratch += state_scratch(n, M, bf) + [pltpu.VMEM((T, D), f32), pltpu.VMEM((8 * HEAD, 2 * M), bf)]
    return pl.pallas_call(
        partial(head_kernel, ns, loc, nz),
        out_shape=[jax.ShapeDtypeStruct(a, bf) for a in shp[:3]] + [jax.ShapeDtypeStruct((nz - 1, packed[3].shape[2], D), bf), jax.ShapeDtypeStruct((dp,) + vloc.shape, f32)] + [jax.ShapeDtypeStruct(a, t) for a, t in kept],
        in_specs=[hb] * 5 + [VM] * 3, out_specs=[hb] * (5 + KEPT),
        scratch_shapes=scratch,
        name="head",
        compiler_params=pltpu.CompilerParams(collective_id=1, has_side_effects=True, vmem_limit_bytes=ALLV),
    )(*packed, vloc, tok, rf, vm)


def ffn_kernel(nz, part, *refs):
    (shards_, *given, win), wout, refs = refs[:6], refs[6:8 if nz else 7], refs[8 if nz else 7:]
    (gr1, gattn, sums, outh, gwin), refs = refs[:5], refs[5:]
    gwout, refs = refs[:6 if nz else 1], refs[6 if nz else 1:]
    (wi, wu, gwi, gwu, act, gp, hlow, acc, gr2, gffn, tr, n1, inv1, vm, cot, out, lsem, ssem, gsem), sems = refs[:19], refs[19:]
    vec, sems = sems[0], sems[1:]
    sibs, sems = (sems[:2], sems[2:]) if nz else ((), sems)
    J, _, C = act.shape

    def rows(j): return ds(j, C)
    def load(j):
        return pltpu.make_async_copy(win.at[rows(j)], wi.at[rows(j)], lsem.at[j])
    def store(j):
        return pltpu.make_async_copy(gwi.at[rows(j)], gwin.at[rows(j)], ssem.at[j])
    def start_load(j, _):
        load(j).start()
        return 0
    def forward(j, _):
        load(j).wait()
        ffn_chunk(j, hlow, wi, act, gp)
        return 0
    def output(j, _):
        ffn_output(j, act, wu, acc, False)
        return 0
    def out_grad(j, _):
        ffn_out_grad(j, tr, act, gwu)
        return 0
    def backward(j, first):
        ffn_backward(j, gffn, hlow, wi, wu, gp, gwi, acc, first)
        store(j).start()
        return 0
    def some_backward(lo, hi):
        lax.fori_loop(lo, hi, lambda j, _: backward(j, False), 0)
    def end_store(j, _):
        store(j).wait()
        return 0
    here = [pltpu.make_async_copy(a, b, gsem.at[i]) for i, (a, b) in enumerate(zip(given, (n1, inv1, vm, cot)))]
    done_out = pltpu.make_async_copy(out, outh, gsem.at[4])

    def begin():
        for cp in here: cp.start()
        lax.fori_loop(0, J, start_load, 0)
        vec[...] = jnp.concatenate([shards_[d][:, :part] for d in range(shards_.shape[0])], 1)
        for cp in here: cp.wait()
        hidden_rows(n1, vec, hlow)
    if nz:
        wz, loc = wout
        r = loc.shape[2] // 2
        G = Gather(nz, (None, None, None, loc), (None, None, None, wu), sems[2:], r)
        entry_barrier([G.ynb, G.xnb, G.sib])
        G.relay(wz)
        begin()
        lax.fori_loop(0, J // 2, forward, 0)
        G.st2(EARLY)
        lax.fori_loop(J // 2, J - J // 6, forward, 0)
        G.st2(EARLY + 1)
        for g in (EARLY, EARLY + 1):
            for k in range(1, nz): G._wz_local(wz, g, k).wait()
        G.st3(EARLY)
        lax.fori_loop(J - J // 6, J, forward, 0)
        G.st3(EARLY + 1)
        G.done(EARLY)
        G.done(EARLY + 1)
    else:
        whole = pltpu.make_async_copy(wout[0], wu, ssem.at[0])
        whole.start()
        begin()
        lax.fori_loop(0, J, forward, 0)
        whole.wait()
    ffn_output(0, act, wu, acc, True)
    lax.fori_loop(1, J, output, 0)
    second_norm(acc, n1, vec, vm, cot, out, gr2, gffn, sums)
    done_out.start()
    tr[...] = gffn[...].T
    lax.fori_loop(0, J, out_grad, 0)
    if nz:
        sc = [()] * EARLY + [(sibs[0], *gwout[1:3]), (sibs[1], *gwout[4:])]
        kept = [pltpu.make_async_copy(sibs[i], gwout[3 * i], gsem.at[5 + i]) for i in range(2)]
        R = Reduce(nz, (None, None, None, gwu), (None,) * NG, sc, sems[:2], None, None, r)
        R.s0(EARLY)
        R.s0(EARLY + 1)
        backward(0, True)
        some_backward(1, J // 4)
        R.s1(EARLY)
        kept[0].start()
        some_backward(J // 4, J // 2)
        R.s1(EARLY + 1)
        kept[1].start()
        some_backward(J // 2, J)
    else:
        backward(0, True)
        some_backward(1, J)
    first_norm_back(acc, gr2, n1, inv1, vec, gr1, gattn, sums)
    if nz:
        for g in (EARLY, EARLY + 1): R.recv1(g)
        G.finish()
        R.finish()
        for cp in kept: cp.wait()
    done_out.wait()
    lax.fori_loop(0, J, end_store, 0)
    if not nz:
        cp = pltpu.make_async_copy(gwu, gwout[0], lsem.at[0])
        cp.start()
        cp.wait()


def ffn(n1, inv1, vec, vm, cot, win, wout, dp=0):
    T, D = n1.shape
    FF = win.shape[0]
    J = FF // COLS
    nz = dp // 2
    hb = pl.BlockSpec(memory_space=pl.ANY)
    S = pltpu.SemaphoreType.DMA
    ws, us, ch = (FF, D), (FF // D, D, D), (J, T, COLS)
    gs = (2, 2, dp, D // dp, D) if dp else us
    part_sums = [a for g in (EARLY, EARLY + 1) for a in reduce_shapes(nz, D, D // dp // 2, g)[:3]] if dp else [us]
    outs = [((T, D), f32), ((T, D), bf), ((4, 8, D), f32), ((T, D), bf), (ws, bf)] + [(a, bf) for a in part_sums]
    scratch = [(ws, bf), (gs, bf), (ws, bf), (gs, bf), (ch, bf), (ch, bf), ((T, D), bf), ((T, D), f32), ((T, D), f32), ((T, D), bf), ((D, T), bf)]
    scratch += [(n1.shape, f32), (inv1.shape, f32), (vm.shape, f32), ((T, D), bf), ((T, D), bf)]
    sems = [pltpu.VMEM(part_sums[0], bf)] * 2 + [S((NG, 2 * nz + 7)), S((NG, 2 * nz + 7))] + gather_sems(dp) if dp else []
    remote = dict(collective_id=3, has_side_effects=True) if dp else {}
    return pl.pallas_call(
        partial(ffn_kernel, nz, D // vec.shape[0]),
        out_shape=[jax.ShapeDtypeStruct(a, t) for a, t in outs],
        in_specs=[VM] + [hb] * (5 + len(wout)), out_specs=[VM] * 3 + [hb] * 2 + ([hb, VM, VM] * 2 if dp else [hb]),
        scratch_shapes=[pltpu.VMEM(a, t) for a, t in scratch] + [S((J,)), S((J,)), S((7,)), pltpu.VMEM((8, D), f32)] + sems,
        name="ffn",
        compiler_params=pltpu.CompilerParams(vmem_limit_bytes=ALLV, **remote),
    )(vec, n1, inv1, vm, cot, win, *wout)


def mix_back_kernel(ns, loc, gattn, qow, ctxb, ctx, den, qp, qf, right, fbm, tok, gqo, gq, gst, gkt, tr):
    tr[...] = gattn[...].T
    weight_grad(tr, ctxb, gqo.at[1])
    mix_back_query(gattn, qow.at[1], qp, qf, right, ctx, den, fbm, gst, gkt, gq, ns, loc)
    weight_grad_pairs(gq, tok, gqo.at[0])


LATE = 11
TAIL_ORDER = (
    "wu1.2", "mq", "s.0", "gq", "wi0.0", "wo", "wu1.3", "wu0.2", "wi1.0", "wi0.1", "qo.0", "tq",
    "s.1", "wi1.1", "qo.1", "s.2", "mk", "wu0.3", "gkv", "kv.0", "wi1.2", "qo.2", "kv.1", "wi0.2",
    "wi1.3", "wu0.4", "qo.3", "kv.2", "wi1.4", "wu1.4", "wi0.3", "kv.3", "wu0.5", "qo.4", "wu1.5", "wi0.4",
    "wi1.5", "wi0.5", "wu0.6", "wu1.6", "kv.4", "qo.5", "wi1.6", "tk", "kv.5", "wi0.6", "kv.6", "qo.6",
)


def tail_kernel(ns, loc, nz, *refs):
    (gattn, ctxb, sums, rf), refs = refs[:4], refs[4:]
    (gwin, gr1, *part_sums), refs = refs[:8], refs[8:]
    late, refs = refs[:LATE], refs[LATE:]
    tg, fins, sout, refs = refs[0], refs[1:5], refs[5], refs[6:]
    there, lsem, refs = refs[:LATE], refs[LATE], refs[LATE + 1:]
    (gkv, gqo, *own, gq, gk, gv, tr, gst, gkt, sto, kto), refs = refs[:12], refs[12:]
    (sb, srec, krec, ss, sr), refs = refs[:5], refs[5:]
    scratch, refs = [refs[g * 7:(g + 1) * 7] for g in range(NG)], refs[7 * NG:]
    rsend, rrecv, osem, sfirst, ssecond, qsend, qrecv, ssrc, fbm = refs
    qow, qp, qf, right, ctx, den, tok, kp, vp, kf, kvw = there
    P_ = gq.shape[0]
    n = ns * P_ // 4

    def load(i):
        return pltpu.make_async_copy(late[i], there[i], lsem.at[i])
    grl = pltpu.make_async_copy(gr1, tg, lsem.at[LATE])
    early = [pltpu.make_async_copy(part_sums[i], scratch[EARLY + i // 3][i % 3], lsem.at[LATE + 1 + i]) for i in range(6)]
    for cp in early: cp.start()
    for i in range(LATE): load(i).start()
    grl.start()
    R = Reduce(nz, (gkv, gqo, gwin, None), (None, None, *own, None, None), scratch, (rsend, rrecv), osem, fins, gkv.shape[3])
    Q = SmallSum(nz, ssrc, sout, sfirst, ssecond, (qsend, qrecv))
    S = StateSum(gst, gkt, sto, kto, sb, srec, krec, (ss, sr))
    entry_barrier(S.peers + Q.dpeer)
    ssrc[...] = jnp.zeros_like(ssrc)
    for i in range(4):
        ssrc[i:i + 1, :] = jnp.sum(sums[i], 0, keepdims=True)
    Q.t0()
    fbm[...] = feature_pull(rf[...])
    wait_for = iter(range(LATE))

    def need(n):
        for _ in range(n): load(next(wait_for)).wait()

    def output_grad():
        tr[...] = gattn[...].T
        weight_grad_units(tr, ctxb, gqo.at[1])

    def mix_query():
        need(7)
        gkt[...] = jnp.zeros_like(gkt)
        mix_back_query(gattn, qow.at[1], qp, qf, right, ctx, den, fbm, Flat(gst, P_), FlatRow(gkt, P_, n), gq, ns, loc)

    def query_token():
        grl.wait()
        token_grad_query(gq, qow.at[0], tg)

    def mix_key():
        need(4)
        mix_back_key(kp, vp, kf, Flat(sto, P_), FlatRow(kto, P_, n), fbm, gk, gv, ns, loc)

    def key_grads():
        weight_grad_pairs_units(gk, tok, gkv.at[0])
        weight_grad_pairs_units(gv, tok, gkv.at[1])
        Q.t1()
    compute = {
        "wo": output_grad, "mq": mix_query, "gq": lambda: weight_grad_pairs_units(gq, tok, gqo.at[0]), "tq": query_token, "mk": mix_key,
        "gkv": key_grads, "tk": lambda: token_grad_keys(gk, gv, kvw.at[0], kvw.at[1], tg),
    }

    def stage(g, i):
        if g >= EARLY and i == 2:
            for cp in early[(g - EARLY) * 3:(g - EARLY) * 3 + 3]: cp.wait()
        R.stage(g, i)
    run_order(TAIL_ORDER, compute, stage, S.stage)
    Q.t2()
    S.finish()
    Q.finish()
    R.finish()


def tail(ns, loc, dp, gattn, ctxb, sums, rf, gwin, gr1, part_sums, late):
    T, D = gattn.shape
    nz = dp // 2
    qf = late[2]
    P_, M = qf.shape[0], qf.shape[2] // 2
    part, ff = D // dp, gwin.shape[0]
    rows = (part // 2, part // 2, ff // dp // 4, part)
    shp = grad_shapes(dp, D, rows[0], rows[2], rows[3])
    n = ns * P_ // 4
    S = pltpu.SemaphoreType.DMA
    pm = pltpu.VMEM((P_, T, 128), bf)
    scratch = [pltpu.VMEM(a.shape, a.dtype) for a in late] + [S((LATE + 7,))]
    scratch += [pltpu.VMEM(shp[0], bf), pltpu.VMEM(shp[1], bf)] + [pltpu.VMEM((nz, 2, 2, rows[0], D), bf)] * 2
    scratch += [pm, pm, pm, pltpu.VMEM((D, T), bf), pltpu.VMEM((4, n, 128, M), f32), pltpu.VMEM((4, 8, 2 * M), f32)]
    scratch += [pltpu.VMEM((4, n, 128, M), bf), pltpu.VMEM((4, 8, 2 * M), f32)] + state_scratch(n, M, bf)
    scratch += [pltpu.VMEM(a, bf) for g in range(NG) for a in reduce_shapes(nz, D, rows[0], g)] + [S((NG, 2 * nz + 7)), S((NG, 2 * nz + 7)), S((NG, nz))] + small_scratch(dp, D) + [pltpu.VMEM((2 * M, 4 * HEAD), bf)]
    hb = pl.BlockSpec(memory_space=pl.ANY)
    return pl.pallas_call(
        partial(tail_kernel, ns, loc, nz),
        out_shape=[jax.ShapeDtypeStruct((T, D), f32)] + [jax.ShapeDtypeStruct((2, 2, r, D), bf) for r in rows] + [jax.ShapeDtypeStruct((8, D), f32)],
        in_specs=[VM] * 4 + [hb] * (8 + LATE), out_specs=[VM] * 6,
        scratch_shapes=scratch,
        name="tail",
        compiler_params=pltpu.CompilerParams(collective_id=2, has_side_effects=True, vmem_limit_bytes=ALLV),
    )(gattn, ctxb, sums, rf, gwin.reshape(shp[2]), gr1, *part_sums, *late)


def last_kernel(ns, loc, kp, vp, kf, gst, gkt, fbm, gr1, gq, kvw, qow, tok, gkv, tg, gk, gv):
    mix_back_key(kp, vp, kf, gst, gkt, fbm, gk, gv, ns, loc)
    weight_grad_pairs(gk, tok, gkv.at[0])
    weight_grad_pairs(gv, tok, gkv.at[1])
    token_grad(gr1, gq, gk, gv, qow.at[0], kvw.at[0], kvw.at[1], tg)


def shards(tokens, lengths, random_features, w_query, w_key, w_value, w_output, w_in, w_out, ln1_gain, ln1_bias, ln2_gain, ln2_bias, cotangent):
    ns, loc, D = tokens.shape
    T = ns * loc
    dp, parts = lax.axis_size("dp"), lax.axis_size("seq")
    part = w_query.shape[1]
    FF = w_out.shape[0]
    M = random_features.shape[1]
    P_ = D // 128
    fast = parts == 4 and dp == 8 and part % 32 == 0 and D == part * dp and part <= 128 and ns * P_ % 4 == 0 and ns * P_ <= 32 and FF == 4 * D
    pos = lax.axis_index("seq") * loc + jnp.arange(loc, dtype=jnp.int32)
    valid = (pos[None, :] < lengths[:, None]).astype(f32).reshape(T, 1)
    vm = jnp.broadcast_to(valid, (T, 128))
    tok, cot = tokens.reshape(T, D), cotangent.reshape(T, D)
    vloc = jnp.stack([ln1_gain, ln1_bias, ln2_gain, ln2_bias]).astype(f32)
    pm, pf, stt, ktt = (P_, T, 128), (P_, T, 2 * M), (ns, P_, 128, M), (ns, P_, 8, 2 * M)
    if fast:
        vloc = jnp.pad(vloc, ((0, 4), (0, 128 - part)))
        packed = pack(w_query, w_key, w_value, w_output, w_in, w_out)
        kvw, qow, win, wz, vec, *kept = head(ns, loc, dp, packed, vloc, tok, random_features, vm)
        wout = wz, packed[3]
        kp, vp, qp, kf, qf, ctx, den, ctxb, right, n1, inv1 = kept
    else:
        vec = jnp.pad(lax.all_gather(vloc, "dp", axis=1, tiled=True), ((0, 4), (0, 0)))[None]
        def full(w):
            return lax.all_gather(w, "dp", axis=1, tiled=True).T
        kvw, qow = jnp.stack([full(w_key), full(w_value)]), jnp.stack([full(w_query), full(w_output)])
        win = full(w_in)
        wout = (jnp.transpose(full(w_out).reshape(D, FF // D, D), (1, 0, 2)),)
    kvw, qow, win = kvw.reshape(2, D, D), qow.reshape(2, D, D), win.reshape(FF, D)
    if not fast:
        wf, fbm = feature_matrix(random_features), feature_pull(random_features)
        kp, vp, qp, kf, qf, st, kt = call(
            partial(key_query_kernel, ns, loc), (tok, kvw, qow, wf, vm),
            [(pm, bf)] * 3 + [(pf, bf)] * 2 + [(stt, f32), (ktt, f32)], name="key_query")
        st, kt = lax.psum((st, kt), "seq")
        ctx, den, ctxb, right, n1, inv1 = call(
            partial(mix_kernel, ns, loc), (tok, qow, qf, st, kt),
            [(pm, f32), (pm, f32), ((T, D), bf), ((ns, P_, 256, 2 * M), bf), ((T, D), f32), ((T, 128), f32)],
            [pltpu.VMEM((T, D), f32)], name="mix")
    gr1, gattn, sums, out, gwin, *gwout = ffn(n1, inv1, vec, vm, cot, win, wout, dp if fast else 0)
    if fast:
        tg, kvg, qog, wig, wug, small = tail(ns, loc, dp, gattn, ctxb, sums, random_features, gwin, gr1, gwout, (qow, qp, qf, right, ctx, den, tok, kp, vp, kf, kvw))
        wk_g, wv_g, wq_g, wo_g = kvg[0].reshape(part, D).T, kvg[1].reshape(part, D).T, qog[0].reshape(part, D).T, qog[1].reshape(part, D).T
        wi_g = wig.reshape(FF // dp, D).T
        wu_g = jnp.transpose(wug.reshape(FF // D, part, D), (0, 2, 1)).reshape(FF, part)
        grads = (wq_g, wk_g, wv_g, wo_g, wi_g, wu_g)
    else:
        gqo, gq, gst, gkt = call(
            partial(mix_back_kernel, ns, loc), (gattn, qow, ctxb, ctx, den, qp, qf, right, fbm, tok),
            [((2, D, D), bf), (pm, bf), (stt, f32), (ktt, f32)], [pltpu.VMEM((D, T), bf)], name="mix_back")
        gst, gkt = lax.psum((gst, gkt), "seq")
        gkv, tg = call(
            partial(last_kernel, ns, loc), (kp, vp, kf, gst, gkt, fbm, gr1, gq, kvw, qow, tok),
            [((2, D, D), bf), ((T, D), f32)], [pltpu.VMEM(pm, bf), pltpu.VMEM(pm, bf)], name="last")
        small = lax.psum(jnp.sum(sums, 1), ("seq", "dp"))
        whole = (gqo[0].T, gkv[0].T, gkv[1].T, gqo[1].T, gwin.T, jnp.transpose(gwout[0], (0, 2, 1)).reshape(FF, D))
        grads = tuple(lax.psum(lax.psum_scatter(g, "dp", scatter_dimension=1, tiled=True), "seq") for g in whole)
    small = lax.dynamic_slice_in_dim(small, lax.axis_index("dp") * part, part, 1)
    return (out.reshape(tokens.shape), tg.reshape(tokens.shape), *(g.astype(f32) for g in grads), small[2], small[3], small[0], small[1])


def solution(mesh):
    rows, cols, vecs = P("dp", "seq", None), P(None, "dp"), P("dp")
    return jax.shard_map(
        shards,
        mesh=mesh,
        in_specs=(rows, vecs, P(), *([cols] * 6), *([vecs] * 4), rows),
        out_specs=(rows, rows, *([cols] * 6), *([vecs] * 4)),
        check_vma=False,
    )
```

```python
import functools
from functools import partial

import jax
import jax.numpy as jnp
from jax import lax
from jax.experimental import pallas as pl
from jax.experimental.pallas import tpu as pltpu
from jax.sharding import PartitionSpec as P

MESH = pl.DeviceIdType.MESH
bf, f32 = jnp.bfloat16, jnp.float32
HEAD = 64
EPS = 1e-12


def coords():
    s, d = lax.axis_index("seq"), lax.axis_index("dp")
    return s // 2, s % 2, d // 2, d % 2

def dev(y, x, z, c):
    return (y * 2 + x, z * 2 + c)

def entry_barrier(peers):
    sem = pltpu.get_barrier_semaphore()
    for p in peers:
        pl.semaphore_signal(sem, inc=1, device_id=p, device_id_type=MESH)
    pl.semaphore_wait(sem, len(peers))

GROUPS = ((0, 0), (1, 0), (2, 0), (2, 1), (3, 0), (3, 1))
NAMES = ("kv", "qo", "wi0", "wi1", "wu0", "wu1")
ZFIRST = (2,)
EARLY = 4
NG = len(GROUPS)

def some(g, r):
    return pl.ds(GROUPS[g][1] * r, r)
def piece(g, ref, d, y, x, r):
    i = GROUPS[g][0]
    if i < 2:  return ref.at[y, d, x]
    if i == 2: return ref.at[d, y, x, some(g, r)]
    return ref.at[y, x, d, some(g, r)]
def lpiece(g, ref, y, x, r):
    return ref.at[y, x, some(g, r)]
def local_rows(g, ref, r):
    return ref.at[:, :, some(g, r)]
def shard(g, ref, d, r):
    i = GROUPS[g][0]
    if i < 2:  return ref.at[:, d]
    if i == 2: return ref.at[d, :, :, some(g, r)]
    return ref.at[:, :, d, some(g, r)]

class Gather:
    def __init__(self, nz, loc, out, sems, r):
        self.nz, self.sems, self.r = nz, sems, r
        self.loc, self.out = [loc[i] for i, _ in GROUPS], [out[i] for i, _ in GROUPS]
        y, x, z, c = self.pos = coords()
        dp = nz * 2
        self.ynb, self.xnb, self.sib = dev(1 - y, x, z, c), dev(y, 1 - x, z, c), dev(y, x, z, 1 - c)
        self.zpeer = [dev(y, x, (z + k) % nz, c) for k in range(1, nz)]
        self.me = z * 2 + c
        self.dpeer = [dev(y, x, (self.me + k) % dp // 2, (self.me + k) % 2) for k in range(1, dp)]
        self.started = []
        half = loc[3].shape[-1] // 2
        self.H = (pl.ds(0, half), pl.ds(half, half))

    def _rc(self, src, dst, ssem, rsem, to):
        return pltpu.make_async_remote_copy(src_ref=src, dst_ref=dst, send_sem=ssem, recv_sem=rsem, device_id=to, device_id_type=MESH)

    def _go(self, *a):
        cp = self._rc(*a)
        cp.start()
        self.started.append(cp)

    def _recv(self, dst, ssem, rsem, to):
        self._rc(dst, dst, ssem, rsem, to).wait_recv()

    def _local(self, g):
        return pltpu.make_async_copy(local_rows(g, self.loc[g], self.r), shard(g, self.out[g], self.me, self.r), self.sems[10].at[g])

    def _own(self, g):
        ss, sr = self.sems[8:10]
        self._go(local_rows(g, self.loc[g], self.r), shard(g, self.out[g], self.me, self.r), ss.at[g, 0], sr.at[g, 0], self.sib)
        self._local(g).start()

    def _vlocal(self, vloc, vout):
        return pltpu.make_async_copy(vloc, vout.at[self.me], self.sems[10].at[NG])

    def start(self, wz, vloc, vout):
        zs, zr, vs, vr = *self.sems[:2], *self.sems[11:13]
        y, x, z, c = self.pos
        for g in range(EARLY):
            for k in range(1, self.nz):
                self._go(lpiece(g, self.loc[g], y, x, self.r), piece(g, self.out[g], self.me, y, x, self.r), zs.at[g, k-1], zr.at[g, k-1], self.zpeer[k-1])
            self._own(g)
        for k in range(1, self.nz):
            self._go(self.loc[EARLY].at[y, x], wz.at[k - 1], zs.at[EARLY, k-1], zr.at[EARLY, k-1], self.zpeer[k-1])
        for k in range(1, self.nz * 2):
            self._go(vloc, vout.at[self.me], vs.at[k - 1], vr.at[k - 1], self.dpeer[k - 1])
        self._vlocal(vloc, vout).start()

    def _wz_local(self, wz, g, k):
        y, x, z, c = self.pos
        return pltpu.make_async_copy(wz.at[k - 1, some(g, self.r)], piece(g, self.out[g], self._from(k, c), y, x, self.r), self.sems[0].at[g, k - 1])

    def relay(self, wz):
        xs, xr, ys, yr = self.sems[2:6]
        y, x, z, c = self.pos
        for g in range(EARLY, NG):
            for k in range(1, self.nz):
                p, src = piece(g, self.out[g], self._from(k, c), y, x, self.r), wz.at[k - 1, some(g, self.r)]
                self._go(src, p, xs.at[g, k-1], xr.at[g, k-1], self.xnb)
                self._go(src, p, ys.at[g, k-1], yr.at[g, k-1], self.ynb)
        for g in range(EARLY, NG):
            for k in range(1, self.nz): self._wz_local(wz, g, k).start()
            self._own(g)

    def stage(self, g, i):
        (None, self.st1, self.st2, self.st3, self.done)[i](g)

    def _from(self, k, c):
        return ((self.pos[2] + self.nz - k) % self.nz) * 2 + c

    def st1(self, g):
        zs, zr, xs, xr, ys, yr = self.sems[:6]
        y, x, z, c = self.pos
        for k in range(1, self.nz):
            p = piece(g, self.out[g], self._from(k, c), y, x, self.r)
            self._recv(p, zs.at[g, k-1], zr.at[g, k-1], self.zpeer[k-1])
            self._go(p, p, xs.at[g, k-1], xr.at[g, k-1], self.xnb)
            self._go(p, p, ys.at[g, k-1], yr.at[g, k-1], self.ynb)

    def st2(self, g):
        xs, xr, ys, yr, ds_, dr = self.sems[2:8]
        y, x, z, c = self.pos
        for k in range(1, self.nz):
            d = self._from(k, c)
            p = piece(g, self.out[g], d, y, 1 - x, self.r)
            self._recv(p, xs.at[g, k-1], xr.at[g, k-1], self.xnb)
            pa = p.at[:, self.H[0]]
            self._go(pa, pa, ds_.at[g, k-1, 0], dr.at[g, k-1, 0], self.ynb)
            p = piece(g, self.out[g], d, 1 - y, x, self.r)
            self._recv(p, ys.at[g, k-1], yr.at[g, k-1], self.ynb)
            pb = p.at[:, self.H[1]]
            self._go(pb, pb, ds_.at[g, k-1, 1], dr.at[g, k-1, 1], self.xnb)

    def st3(self, g):
        ds_, dr, ss, sr = self.sems[6:10]
        y, x, z, c = self.pos
        for k in range(1, self.nz):
            d = self._from(k, c)
            p = piece(g, self.out[g], d, 1 - y, 1 - x, self.r)
            pa, pb = p.at[:, self.H[0]], p.at[:, self.H[1]]
            self._recv(pa, ds_.at[g, k-1, 0], dr.at[g, k-1, 0], self.ynb)
            self._recv(pb, ds_.at[g, k-1, 1], dr.at[g, k-1, 1], self.xnb)
            sh = shard(g, self.out[g], d, self.r)
            self._go(sh, sh, ss.at[g, k], sr.at[g, k], self.sib)

    def done(self, g):
        ss, sr = self.sems[8:10]
        for k in range(self.nz):
            self._recv(shard(g, self.out[g], self._from(k, 1 - self.pos[3]), self.r), ss.at[g, k], sr.at[g, k], self.sib)
        self._local(g).wait()

    def end(self, wz, vloc, vout):
        zs, zr, vs, vr = *self.sems[:2], *self.sems[11:13]
        dp = self.nz * 2
        for k in range(1, self.nz):
            self._recv(wz.at[k - 1], zs.at[EARLY, k-1], zr.at[EARLY, k-1], self.zpeer[k-1])
        for k in range(1, dp):
            self._recv(vout.at[(self.me + dp - k) % dp], vs.at[k - 1], vr.at[k - 1], self.dpeer[k - 1])
        self._vlocal(vloc, vout).wait()
        self.finish()

    def finish(self):
        for cp in self.started:
            cp.wait_send()

def gather_sems(dp):
    nz = dp // 2
    n = nz - 1
    S = pltpu.SemaphoreType.DMA
    return [S((NG, n)) for _ in range(6)] + [S((NG, n, 2)), S((NG, n, 2)), S((NG, nz)), S((NG, nz)), S((NG + 1,)), S((dp - 1,)), S((dp - 1,))]

def pack(wq, wk, wv, wo, win, wout):
    D = wq.shape[0]
    sh = wq.shape[1]
    t = jnp.transpose
    kv = jnp.stack([t(wk), t(wv)]).reshape(2, 2, sh // 2, D)
    qo = jnp.stack([t(wq), t(wo)]).reshape(2, 2, sh // 2, D)
    wi = t(win).reshape(2, 2, win.shape[1] // 4, D)
    ff = wout.shape[0]
    wu = t(wout.reshape(ff // D, D, sh), (0, 2, 1)).reshape(2, 2, sh, D)
    return kv, qo, wi, wu


def nn(a, b): return lax.dot_general(a, b, (((1,), (0,)), ((), ())), preferred_element_type=f32)
def nt(a, b): return lax.dot_general(a, b, (((1,), (1,)), ((), ())), preferred_element_type=f32)
def tn(a, b): return lax.dot_general(a, b, (((0,), (0,)), ((), ())), preferred_element_type=f32)

def ds(i, n): return pl.ds(pl.multiple_of(i * n, n), n)

def mat(w):
    return w[...].reshape(-1, w.shape[-1])

def project(tok, w, dst):
    D = tok.shape[1]
    v = mat(w)
    for n in range(D // 256):
        o = nt(tok[...], v[n * 256:(n + 1) * 256, :]).astype(bf)
        dst[2 * n] = o[:, :128]
        dst[2 * n + 1] = o[:, 128:]

def features(x, wf):
    xf = x.astype(f32)
    sq = xf * xf
    hi = sq.astype(bf)
    lo = (sq - hi.astype(f32)).astype(bf)
    return jnp.exp(nn(jnp.concatenate([x, x, hi, lo], 1), wf[...]))

def pair_mask(m):
    r = lax.broadcasted_iota(jnp.int32, (128, 2 * m), 0) < HEAD
    c = lax.broadcasted_iota(jnp.int32, (128, 2 * m), 1) < m
    return (r == c)

def compact(st, m):
    return jnp.concatenate([st[:HEAD, :m], st[HEAD:, m:]], 0)

def key_side(kp, vp, wf, vm, kf, st, kt, nseq, loc):
    P_ = kp.shape[0]
    M = wf.shape[1] // 2
    def body(p, _):
        f = features(kp[p], wf) * jnp.concatenate([vm[...]] * (2 * M // 128), 1)
        fb = f.astype(bf)
        kf[p] = fb
        for b in range(nseq):
            rows = slice(b * loc, (b + 1) * loc)
            st[b, p] = compact(tn(vp[p, rows, :], fb[rows]), M)
            kt[b, p] = jnp.broadcast_to(jnp.sum(f[rows], 0, keepdims=True), (8, 2 * M))
        return 0
    lax.fori_loop(0, P_, body, 0)

def query_side(qp, wf, qf):
    def body(p, _):
        qf[p] = features(qp[p], wf).astype(bf)
        return 0
    lax.fori_loop(0, qp.shape[0], body, 0)

def build_right(st, kt, right, m):
    mask = pair_mask(m)
    nseq, P_ = right.shape[:2]
    for b in range(nseq):
        def body(p, _):
            c = st[b, p].astype(f32)
            s = jnp.where(mask, jnp.concatenate([c, c], 1), 0.0)
            t = jnp.where(mask, jnp.broadcast_to(kt[b, p][:1], (128, 2 * m)), 0.0)
            right[b, p] = jnp.concatenate([s, t], 0).astype(bf)
            return 0
        lax.fori_loop(0, P_, body, 0)

def mix_forward(qf, right, ctx, den, ctxb, nseq, loc):
    def body(p, _):
        for b in range(nseq):
            rows = slice(b * loc, (b + 1) * loc)
            o = nt(qf[p, rows, :], right[b, p])
            d = o[:, 128:]
            c = o[:, :128] / d
            ctx[p, rows, :] = c
            den[p, rows, :] = d
            ctxb[rows, ds(p, 128)] = c.astype(bf)
        return 0
    lax.fori_loop(0, qf.shape[0], body, 0)

def mean(a): return jnp.mean(a, -1, keepdims=True)

def attend_out(ctxb, wo, tok, n1, inv1, resid):
    T, D = tok.shape
    v = mat(wo)
    for n in range(D // 256):
        resid[:, n * 256:(n + 1) * 256] = nt(ctxb[...], v[n * 256:(n + 1) * 256, :])
    R = 64
    def body(i, _):
        r = ds(i, R)
        x = tok[r, :].astype(f32) + resid[r, :]
        cen = x - mean(x)
        inv = lax.rsqrt(mean(cen * cen) + EPS)
        n1[r, :] = cen * inv
        inv1[r, :] = jnp.broadcast_to(inv, (R, 128))
        return 0
    lax.fori_loop(0, T // R, body, 0)

def ffn_chunk(j, hlow, win, act, gp):
    C = act.shape[2]
    pre = nt(hlow[...], win[ds(j, C), :])
    cdf = 0.5 * (1.0 + lax.erf(pre * 0.7071067811865476))
    act[j] = (pre * cdf).astype(bf)
    gp[j] = (cdf + pre * (jnp.exp(-0.5 * pre * pre) * 0.3989422804014327)).astype(bf)

def out_columns(wout, j, C):
    per = wout.shape[-1] // C
    jj, cc = j // per, ds(lax.rem(j, per), C)
    if len(wout.shape) == 3:
        return wout[jj, :, cc]
    return wout[jj // 2, lax.rem(jj, 2), :, :, cc].reshape(-1, C)

def ffn_output(j, act, wout, acc, first):
    o = nt(act[j], out_columns(wout, j, act.shape[2]))
    if first: acc[...] = o
    else: acc[...] += o

def hidden_rows(n1, vec, hlow):
    R = 64
    def body(i, _):
        r = ds(i, R)
        hlow[r, :] = (n1[r, :] * vec[0:1, :] + vec[1:2, :]).astype(bf)
        return 0
    lax.fori_loop(0, n1.shape[0] // R, body, 0)

def fold8(a):
    return jnp.sum(a.reshape(a.shape[0] // 8, 8, a.shape[1]), 0)

def norm_pull(g, n, inv, gain):
    e = g * gain
    return inv * (e - mean(e) - n * mean(e * n))

def second_norm(acc, n1, vec, vm, cot, out, gr2, gffn, sums):
    T, D = acc.shape
    R = 64
    sums[0] = jnp.zeros((8, D), f32)
    sums[1] = jnp.zeros((8, D), f32)
    def body(i, _):
        r = ds(i, R)
        x = n1[r, :] * vec[0:1, :] + vec[1:2, :] + acc[r, :]
        cen = x - mean(x)
        inv = lax.rsqrt(mean(cen * cen) + EPS)
        n = cen * inv
        v = vm[r, :]
        vv = jnp.concatenate([v] * (D // 128), 1)
        out[r, :] = ((n * vec[2:3, :] + vec[3:4, :]) * vv).astype(bf)
        gy = cot[r, :].astype(f32) * vv
        sums[0] += fold8(gy * n)
        sums[1] += fold8(gy)
        g = norm_pull(gy, n, inv, vec[2:3, :])
        gr2[r, :] = g
        gffn[r, :] = g.astype(bf)
        return 0
    lax.fori_loop(0, T // R, body, 0)

def ffn_out_grad(j, gffn_t, act, gwout):
    C = act.shape[2]
    per = gwout.shape[-1] // C
    o = nn(gffn_t[...], act[j]).astype(bf)
    jj, cc = j // per, ds(lax.rem(j, per), C)
    if len(gwout.shape) == 3:
        gwout[jj, :, cc] = o
    else:
        gwout[jj // 2, lax.rem(jj, 2), :, :, cc] = o.reshape(gwout.shape[2], gwout.shape[3], C)

def ffn_backward(j, gffn, hlow, win, wout, gp, gwin, gh, first):
    C = gp.shape[2]
    ga = nn(gffn[...], out_columns(wout, j, C))
    gpre = (ga * gp[j].astype(f32)).astype(bf)
    gwin[ds(j, C), :] = tn(gpre, hlow[...]).astype(bf)
    o = nn(gpre, win[ds(j, C), :])
    if first: gh[...] = o
    else: gh[...] += o

def first_norm_back(gh, gr2, n1, inv1, vec, gr1, gattn, sums):
    T, D = gh.shape
    R = 64
    sums[2] = jnp.zeros((8, D), f32)
    sums[3] = jnp.zeros((8, D), f32)
    def body(i, _):
        r = ds(i, R)
        g = gr2[r, :] + gh[r, :]
        n = n1[r, :]
        sums[2] += fold8(g * n)
        sums[3] += fold8(g)
        o = norm_pull(g, n, inv1[r, :][:, :1], vec[0:1, :])
        gr1[r, :] = o
        gattn[r, :] = o.astype(bf)
        return 0
    lax.fori_loop(0, T // R, body, 0)

def put_units(dst, n, o):
    dp, _, a, _ = dst.shape
    for u in range(dp):
        i = n * dp + u
        dst[i // 2, i % 2] = o[u * a:(u + 1) * a].astype(bf)

def weight_grad_units(gt, x, dst):
    h = gt.shape[0] // 2
    for n in range(2):
        put_units(dst, n, nn(gt[n * h:(n + 1) * h, :], x[...]))

def weight_grad_pairs_units(gp_, x, dst):
    h = gp_.shape[0] // 2
    for n in range(2):
        g = jnp.concatenate([gp_[n * h + i] for i in range(h)], 1)
        put_units(dst, n, tn(g, x[...]))

def weight_grad(gt, x, dst):
    D = x.shape[1]
    for n in range(D // 256):
        dst[n * 256:(n + 1) * 256, :] = nn(gt[n * 256:(n + 1) * 256, :], x[...]).astype(bf)

def weight_grad_pairs(gp_, x, dst):
    P_ = gp_.shape[0]
    for n in range(P_ // 2):
        g = jnp.concatenate([gp_[2 * n], gp_[2 * n + 1]], 1)
        dst[n * 256:(n + 1) * 256, :] = tn(g, x[...]).astype(bf)

def mix_back_query(gattn, wo, qp, qf, right, ctx, den, fbm, gst, gkt, gq, nseq, loc):
    M = qf.shape[2] // 2
    mask = pair_mask(M)
    def body(p, _):
        gc = nn(gattn[...], wo[:, ds(p, 128)]).astype(bf).astype(f32)
        gn = gc / den[p]
        t = -gn * ctx[p]
        g = jnp.concatenate([gn, t], 1).astype(bf)
        for b in range(nseq):
            rows = slice(b * loc, (b + 1) * loc)
            q = qf[p, rows, :]
            s = tn(g[rows], q)
            gst[b, p] = compact(s[:128], M)
            gkt[b, p] = jnp.broadcast_to(jnp.sum(jnp.where(mask, s[128:], 0.0), 0, keepdims=True), (8, 2 * M))
            pr = (nn(g[rows], right[b, p]) * q.astype(f32)).astype(bf)
            o = nn(pr, fbm[...])
            gq[p, rows, :] = (o[:, :128] - 0.125 * qp[p, rows, :].astype(f32) * o[:, 128:]).astype(bf)
        return 0
    lax.fori_loop(0, qf.shape[0], body, 0)

def mix_back_key(kp, vp, kf, gst, gkt, fbm, gk, gv, nseq, loc):
    M = kf.shape[2] // 2
    mask = pair_mask(M)
    def body(p, _):
        for b in range(nseq):
            rows = slice(b * loc, (b + 1) * loc)
            c = gst[b, p].astype(f32)
            s = jnp.where(mask, jnp.concatenate([c, c], 1), 0.0).astype(bf)
            k = kf[p, rows, :]
            pr = ((nn(vp[p, rows, :], s) + gkt[b, p][:1]) * k.astype(f32)).astype(bf)
            o = nn(pr, fbm[...])
            gk[p, rows, :] = (o[:, :128] - 0.125 * kp[p, rows, :].astype(f32) * o[:, 128:]).astype(bf)
            gv[p, rows, :] = nt(k, s).astype(bf)
        return 0
    lax.fori_loop(0, kf.shape[0], body, 0)

def join(g):
    return jnp.concatenate([g[i] for i in range(g.shape[0])], 1)

def token_grad(gr1, gq, gk, gv, wq, wk, wv, dst):
    D = gr1.shape[1]
    for n in range(D // 256):
        c = slice(n * 256, (n + 1) * 256)
        dst[:, c] = gr1[:, c] + (nn(join(gq), wq[:, c]) + nn(join(gk), wk[:, c]) + nn(join(gv), wv[:, c]))

def token_grad_query(gq, wq, dst):
    D = dst.shape[1]
    for n in range(D // 256):
        c = slice(n * 256, (n + 1) * 256)
        dst[:, c] += nn(join(gq), wq[:, c])

def token_grad_keys(gk, gv, wk, wv, dst):
    D = dst.shape[1]
    for n in range(D // 256):
        c = slice(n * 256, (n + 1) * 256)
        dst[:, c] += nn(join(gk), wk[:, c]) + nn(join(gv), wv[:, c])

def split_features(rf):
    w = rf * HEAD ** (-0.25)
    hi = w.astype(bf)
    lo = (w - hi.astype(f32)).astype(bf)
    z = jnp.zeros(rf.shape, bf)
    def bd(a): return jnp.concatenate([jnp.concatenate([a, z], 1), jnp.concatenate([z, a], 1)], 0)
    return hi, lo, bd

def feature_matrix(rf):
    hi, lo, bd = split_features(rf)
    s = bd(jnp.full(rf.shape, -0.0625, bf))
    return jnp.concatenate([bd(hi), bd(lo), s, s], 0)

def feature_pull(rf):
    hi, lo, bd = split_features(rf)
    return jnp.concatenate([bd(hi), bd(jnp.ones(rf.shape, bf))], 0).T


class Reduce:
    def __init__(self, nz, grads, own, scratch, sems, own_sem, fins, r):
        self.nz, self.own, self.own_sem, self.sem, self.r, self.sc = nz, own, own_sem, sems, r, scratch
        self.grads = [grads[i] for i, _ in GROUPS]
        if fins is not None:
            self.fins = [local_rows(g, fins[GROUPS[g][0]], r) for g in range(NG)]
            self.h = fins[0].shape[-1] // 2
        else:
            self.h = grads[3].shape[-1] // 2
        self.started = []
        y, x, z, c = self.pos = coords()
        self.ynb, self.xnb, self.sibdev = dev(1 - y, x, z, c), dev(y, 1 - x, z, c), dev(y, x, z, 1 - c)
        self.zpeer = [dev(y, x, (z + k) % nz, c) for k in range(1, nz)]
        self.A, self.B = pl.ds(0, self.h), pl.ds(self.h, self.h)

    def _cp(self, src, dst, g, i, to):
        s, r = self.sem
        return pltpu.make_async_remote_copy(src_ref=src, dst_ref=dst, send_sem=s.at[g, i], recv_sem=r.at[g, i], device_id=to, device_id_type=MESH)

    def _go(self, src, dst, g, i, to):
        cp = self._cp(src, dst, g, i, to)
        cp.start()
        self.started.append(cp)

    def _recv(self, dst, g, i, to):
        self._cp(dst, dst, g, i, to).wait_recv()

    def stage(self, g, i):
        late = g in ZFIRST
        (self.s0, self.z1 if late else self.s1, self.z2 if late else self.s2, self.z3 if late else self.s3, self.z4 if late else self.s4, self.s5, self.s6)[i](g)

    def s0(self, g):
        c = self.pos[3]
        sib = self.sc[g][0]
        for k in range(self.nz):
            self._go(shard(g, self.grads[g], k * 2 + 1 - c, self.r), sib.at[k], g, k, self.sibdev)
        if self.own[g] is not None:
            for k in range(self.nz):
                self._own(g, k).start()

    def _own(self, g, k):
        c = self.pos[3]
        return pltpu.make_async_copy(shard(g, self.grads[g], k * 2 + c, self.r), self.own[g].at[k], self.own_sem.at[g, k])

    def _pair(self, g):
        c = self.pos[3]
        sib, own, gr = self.sc[g][0], self.own[g], self.grads[g]
        for k in range(self.nz):
            self._recv(sib.at[k], g, k, self.sibdev)
            if own is not None:
                self._own(g, k).wait()
        def body(i, _):
            k, q = i // 4, lax.rem(i, 4)
            qy, qx = q // 2, lax.rem(q, 2)
            mine = piece(g, gr, k * 2 + c, qy, qx, self.r) if own is None else own.at[k, qy, qx]
            sib[k, qy, qx] = (sib[k, qy, qx].astype(f32) + mine[...].astype(f32)).astype(bf)
            return 0
        lax.fori_loop(0, self.nz * 4, body, 0)

    def s1(self, g):
        y, x, z, c = self.pos
        sib, a1, b1 = self.sc[g][:3]
        self._pair(g)
        self._go(sib.at[:, :, 1 - x, :, self.A], a1, g, self.nz, self.xnb)
        self._go(sib.at[:, 1 - y, :, :, self.B], b1, g, self.nz + 1, self.ynb)

    def recv1(self, g):
        a1, b1 = self.sc[g][1:3]
        self._recv(a1, g, self.nz, self.xnb)
        self._recv(b1, g, self.nz + 1, self.ynb)

    def s2(self, g):
        y, x, z, c = self.pos
        nz, h = self.nz, self.h
        sib, a1, b1, a2, b2 = self.sc[g][:5]
        if g < EARLY:
            self.recv1(g)
        def body(i, _):
            k, j = i // 2, lax.rem(i, 2)
            a1[k, j] = (a1[k, j].astype(f32) + sib[k, j, x, :, :h].astype(f32)).astype(bf)
            b1[k, j] = (b1[k, j].astype(f32) + sib[k, y, j, :, h:].astype(f32)).astype(bf)
            return 0
        lax.fori_loop(0, nz * 2, body, 0)
        self._go(a1.at[:, 1 - y], a2, g, nz + 2, self.ynb)
        self._go(b1.at[:, 1 - x], b2, g, nz + 3, self.xnb)

    def s3(self, g):
        y, x, z, c = self.pos
        nz, h = self.nz, self.h
        a1, b1, a2, b2, tot, zrec = self.sc[g][1:]
        self._recv(a2, g, nz + 2, self.ynb)
        self._recv(b2, g, nz + 3, self.xnb)
        def body(k, _):
            tot[k, :, :h] = (a1[k, y].astype(f32) + a2[k].astype(f32)).astype(bf)
            tot[k, :, h:] = (b1[k, x].astype(f32) + b2[k].astype(f32)).astype(bf)
            return 0
        lax.fori_loop(0, nz, body, 0)
        for k in range(1, nz):
            self._go(tot.at[(z + k) % nz], zrec.at[k - 1], g, nz + 3 + k, self.zpeer[k - 1])

    def s4(self, g):
        y, x, z, c = self.pos
        nz, fin = self.nz, self.fins[g]
        tot, zrec = self.sc[g][5:]
        for k in range(1, nz):
            self._recv(zrec.at[k - 1], g, nz + 3 + k, self.zpeer[k - 1])
        t = tot[z].astype(f32)
        for k in range(1, nz):
            t = t + zrec[k - 1].astype(f32)
        fin[y, x] = t.astype(bf)
        self._spread(g)

    def z1(self, g):
        z = self.pos[2]
        sib, zrec = self.sc[g][0], self.sc[g][6]
        self._pair(g)
        for k in range(1, self.nz):
            self._go(sib.at[(z + k) % self.nz], zrec.at[k - 1], g, self.nz + 3 + k, self.zpeer[k - 1])

    def z2(self, g):
        y, x, z, c = self.pos
        nz = self.nz
        sib, a1, b1, a2, b2, tot, zrec = self.sc[g]
        for k in range(1, nz):
            self._recv(zrec.at[k - 1], g, nz + 3 + k, self.zpeer[k - 1])
        def body(i, _):
            j, l = i // 2, lax.rem(i, 2)
            t = sib[z, j, l].astype(f32)
            for k in range(1, nz):
                t = t + zrec[k - 1, j, l].astype(f32)
            tot[j, l] = t.astype(bf)
            return 0
        lax.fori_loop(0, 4, body, 0)
        self._go(tot.at[:, 1 - x, :, self.A], a1, g, nz, self.xnb)
        self._go(tot.at[1 - y, :, :, self.B], b1, g, nz + 1, self.ynb)

    def z3(self, g):
        y, x, z, c = self.pos
        nz, h = self.nz, self.h
        sib, a1, b1, a2, b2, tot, zrec = self.sc[g]
        self._recv(a1, g, nz, self.xnb)
        self._recv(b1, g, nz + 1, self.ynb)
        for j in range(2):
            a1[j] = (a1[j].astype(f32) + tot[j, x, :, :h].astype(f32)).astype(bf)
            b1[j] = (b1[j].astype(f32) + tot[y, j, :, h:].astype(f32)).astype(bf)
        self._go(a1.at[1 - y], a2, g, nz + 2, self.ynb)
        self._go(b1.at[1 - x], b2, g, nz + 3, self.xnb)

    def z4(self, g):
        y, x, z, c = self.pos
        nz, h, fin = self.nz, self.h, self.fins[g]
        a1, b1, a2, b2 = self.sc[g][1:5]
        self._recv(a2, g, nz + 2, self.ynb)
        self._recv(b2, g, nz + 3, self.xnb)
        fin[y, x, :, :h] = (a1[y].astype(f32) + a2[...].astype(f32)).astype(bf)
        fin[y, x, :, h:] = (b1[x].astype(f32) + b2[...].astype(f32)).astype(bf)
        self._spread(g)

    def _spread(self, g):
        y, x, z, c = self.pos
        a, b = self.fins[g].at[y, x, :, self.A], self.fins[g].at[y, x, :, self.B]
        self._go(a, a, g, 2 * self.nz + 3, self.xnb)
        self._go(b, b, g, 2 * self.nz + 4, self.ynb)

    def s5(self, g):
        y, x, z, c = self.pos
        nz, fin = self.nz, self.fins[g]
        self._recv(fin.at[y, 1 - x, :, self.A], g, 2 * nz + 3, self.xnb)
        self._recv(fin.at[1 - y, x, :, self.B], g, 2 * nz + 4, self.ynb)
        a, b = fin.at[y, :, :, self.A], fin.at[:, x, :, self.B]
        self._go(a, a, g, 2 * nz + 5, self.ynb)
        self._go(b, b, g, 2 * nz + 6, self.xnb)

    def s6(self, g):
        y, x, z, c = self.pos
        nz, fin = self.nz, self.fins[g]
        self._recv(fin.at[1 - y, :, :, self.A], g, 2 * nz + 5, self.ynb)
        self._recv(fin.at[:, 1 - x, :, self.B], g, 2 * nz + 6, self.xnb)

    def finish(self):
        for cp in self.started:
            cp.wait_send()

def grad_shapes(dp, D, a, b, c_):
    return [(2, dp, 2, a, D), (2, dp, 2, a, D), (dp, 2, 2, b, D), (2, 2, dp, c_, D)]

def reduce_shapes(nz, D, r, g):
    h = D // 2
    if g in ZFIRST:
        return (nz, 2, 2, r, D), (2, r, h), (2, r, h), (r, h), (r, h), (2, 2, r, D), (nz - 1, 2, 2, r, D)
    return (nz, 2, 2, r, D), (nz, 2, r, h), (nz, 2, r, h), (nz, r, h), (nz, r, h), (nz, r, D), (nz - 1, r, D)

class SmallSum:
    def __init__(self, nz, src, dst, first, second, sems):
        self.dp, self.src, self.dst, self.first, self.second, self.sem = nz * 2, src, dst, first, second, sems
        y, x, z, c = coords()
        self.me, self.seq, dp = z * 2 + c, y * 2 + x, nz * 2
        self.dpeer = [dev(y, x, (self.me + k) % dp // 2, (self.me + k) % 2) for k in range(1, dp)]
        self.speer = [dev(y, 1 - x, z, c), dev(1 - y, x, z, c), dev(1 - y, 1 - x, z, c)]
        self.sid = [y * 2 + 1 - x, (1 - y) * 2 + x, (1 - y) * 2 + 1 - x]
        self.started = []

    def peers(self):
        return self.dpeer + self.speer

    def _cp(self, src, dst, i, to):
        s, r = self.sem
        return pltpu.make_async_remote_copy(src_ref=src, dst_ref=dst, send_sem=s.at[i], recv_sem=r.at[i], device_id=to, device_id_type=MESH)

    def _go(self, *a):
        cp = self._cp(*a)
        cp.start()
        self.started.append(cp)

    def t0(self):
        for k in range(1, self.dp):
            self._go(self.src, self.first.at[k - 1], k - 1, self.dpeer[k - 1])

    def t1(self):
        t = self.src[...]
        for k in range(1, self.dp):
            self._cp(self.first.at[k - 1], self.first.at[k - 1], k - 1, self.dpeer[k - 1]).wait_recv()
            t = t + self.first[k - 1]
        self.second[self.seq] = t
        for i in range(3):
            self._go(self.second.at[self.seq], self.second.at[self.seq], self.dp - 1 + i, self.speer[i])

    def t2(self):
        for i in range(3):
            self._cp(self.second.at[self.sid[i]], self.second.at[self.sid[i]], self.dp - 1 + i, self.speer[i]).wait_recv()
        self.dst[...] = (self.second[0] + self.second[1]) + (self.second[2] + self.second[3])

    def finish(self):
        for cp in self.started:
            cp.wait_send()

def small_scratch(dp, D):
    S = pltpu.SemaphoreType.DMA
    return [pltpu.VMEM((dp - 1, 8, D), f32), pltpu.VMEM((4, 8, D), f32), S((dp + 2,)), S((dp + 2,)), pltpu.VMEM((8, D), f32)]

class StateSum:
    def __init__(self, st, kt, sto, kto, sb, srec, krec, sems):
        self.st, self.kt, self.sto, self.kto, self.srec, self.krec, self.sem = st, kt, sto, kto, srec, krec, sems
        self.sb = st if sb is None else sb
        y, x, z, c = coords()
        self.peers = [dev(y, 1 - x, z, c), dev(1 - y, x, z, c), dev(1 - y, 1 - x, z, c)]
        self.sid = [y * 2 + 1 - x, (1 - y) * 2 + x, (1 - y) * 2 + 1 - x]
        self.me = y * 2 + x
        self.started = []

    def _cp(self, src, dst, i, k):
        s, r = self.sem
        return pltpu.make_async_remote_copy(src_ref=src, dst_ref=dst, send_sem=s.at[i, k], recv_sem=r.at[i, k], device_id=self.peers[k], device_id_type=MESH)

    def _go(self, *a):
        cp = self._cp(*a)
        cp.start()
        self.started.append(cp)

    def _recv(self, dst, i, k):
        self._cp(dst, dst, i, k).wait_recv()

    def start(self):
        if self.sb is not self.st:
            self.sb[...] = self.st[...].astype(self.sb.dtype)
        for k in range(3):
            self._go(self.sb.at[self.sid[k]], self.srec.at[k], 0, k)
            self._go(self.kt.at[self.sid[k]], self.krec.at[k], 1, k)

    def stage(self, i):
        (self.start, self.mid, self.end)[i]()

    def mid(self):
        me = self.me
        t, u = self.st[me], self.kt[me]
        for k in range(3):
            self._recv(self.srec.at[k], 0, k)
            self._recv(self.krec.at[k], 1, k)
            t = t + self.srec[k].astype(f32)
            u = u + self.krec[k]
        self.sto[me] = t.astype(self.sto.dtype)
        self.kto[me] = u
        for k in range(3):
            self._go(self.sto.at[me], self.sto.at[me], 2, k)
            self._go(self.kto.at[me], self.kto.at[me], 3, k)

    def end(self):
        for k in range(3):
            self._recv(self.sto.at[self.sid[k]], 2, k)
            self._recv(self.kto.at[self.sid[k]], 3, k)

    def finish(self):
        for cp in self.started:
            cp.wait_send()

class Flat:
    def __init__(self, ref, pairs):
        self.ref, self.pairs = ref, pairs

    def _at(self, i):
        f = i[0] * self.pairs + i[1]
        return (f // self.ref.shape[1], f % self.ref.shape[1])

    def __getitem__(self, i):
        return self.ref[self._at(i)]

    def __setitem__(self, i, v):
        self.ref[self._at(i)] = v

class FlatRow:
    def __init__(self, ref, pairs, n):
        self.ref, self.pairs, self.n = ref, pairs, n

    def _at(self, i):
        f = i[0] * self.pairs + i[1]
        return (f // self.n, pl.ds(f % self.n, 1), slice(None))

    def __getitem__(self, i):
        return self.ref[self._at(i)]

    def __setitem__(self, i, v):
        self.ref[self._at(i)] = v[:1]

def state_scratch(n, M, dtype):
    S = pltpu.SemaphoreType.DMA
    sb = [] if dtype == f32 else [pltpu.VMEM((4, n, 128, M), dtype)]
    return sb + [pltpu.VMEM((3, n, 128, M), dtype), pltpu.VMEM((3, 8, 2 * M), f32), S((4, 3)), S((4, 3))]

VM = pl.BlockSpec(memory_space=pltpu.VMEM)
ALLV = 67043328
COLS = 768


def call(body, ins, outs, scratch=(), name=None):
    return pl.pallas_call(
        body,
        out_shape=[jax.ShapeDtypeStruct(s, d) for s, d in outs],
        in_specs=[VM] * len(ins),
        out_specs=[VM] * len(outs),
        scratch_shapes=list(scratch),
        name=name,
        compiler_params=pltpu.CompilerParams(vmem_limit_bytes=ALLV),
    )(*ins)


def key_query_kernel(ns, loc, tok, kvw, qow, wf, vm, kp, vp, qp, kf, qf, st, kt):
    project(tok, kvw.at[0], kp)
    project(tok, kvw.at[1], vp)
    project(tok, qow.at[0], qp)
    key_side(kp, vp, wf, vm, kf, st, kt, ns, loc)
    query_side(qp, wf, qf)


def mix_kernel(ns, loc, tok, qow, qf, st, kt, ctx, den, ctxb, right, n1, inv1, resid):
    build_right(st, kt, right, qf.shape[2] // 2)
    mix_forward(qf, right, ctx, den, ctxb, ns, loc)
    attend_out(ctxb, qow.at[1], tok, n1, inv1, resid)


KEPT = 11
HEAD_ORDER = (
    "kv.1", "kv.2", "qo.1", "kv.3", "wi0.1", "kv.4", "qo.2", "pk", "wi1.1", "ks", "qo.3", "s.0",
    "wi0.2", "s.1", "wi0.3", "qo.4", "pq", "qs", "s.2", "wi1.2", "mx", "wi1.3", "wi0.4", "at",
    "wi1.4",
)


def run_order(order, compute, stage, state):
    for op in order:
        if op in compute:
            compute[op]()
        else:
            name, i = op.split(".")
            if name == "s":
                state(int(i))
            else:
                stage(NAMES.index(name), int(i))


def head_kernel(ns, loc, nz, *refs):
    local, (vloc, tok, rf, vm), refs = refs[:4], refs[4:8], refs[8:]
    whole, wz, vout, kept, refs = (*refs[:3], None), refs[3], refs[4], refs[5:5 + KEPT], refs[5 + KEPT:]
    sems, (kvs, qos, lsem), here, ksem, refs = refs[:13], refs[13:16], refs[16:16 + KEPT], refs[16 + KEPT], refs[17 + KEPT:]
    st, kt, sto, kto, sb, srec, krec, ss, sr, resid, wf = refs
    kp, vp, qp, kf, qf, ctx, den, ctxb, right, n1, inv1 = here
    P_, M = qf.shape[0], qf.shape[2] // 2
    n = ns * P_ // 4

    def keep(i):
        return pltpu.make_async_copy(here[i], kept[i], ksem.at[i])

    def load(i, dst):
        return pltpu.make_async_copy(whole[i], dst, lsem.at[i])
    G = Gather(nz, local, whole, sems, local[0].shape[2])
    S = StateSum(st, kt, sto, kto, sb, srec, krec, (ss, sr))
    entry_barrier([G.ynb, S.peers[0], S.peers[2]] + G.dpeer)
    G.start(wz, vloc, vout)
    wf[...] = feature_matrix(rf[...])

    def key_values():
        load(0, kvs).start()
        load(0, kvs).wait()
        project(tok, kvs.at[0], kp)
        project(tok, kvs.at[1], vp)
        for i in (0, 1): keep(i).start()

    def keys():
        kt[...] = jnp.zeros_like(kt)
        key_side(kp, vp, wf, vm, kf, Flat(st, P_), FlatRow(kt, P_, n), ns, loc)
        keep(3).start()

    def queries():
        load(1, qos).start()
        load(1, qos).wait()
        project(tok, qos.at[0], qp)
        keep(2).start()

    def query_features():
        query_side(qp, wf, qf)
        keep(4).start()

    def mix():
        build_right(Flat(sto, P_), FlatRow(kto, P_, n), right, M)
        mix_forward(qf, right, ctx, den, ctxb, ns, loc)
        for i in (5, 6, 7, 8): keep(i).start()

    def attend():
        attend_out(ctxb, qos.at[1], tok, n1, inv1, resid)
        for i in (9, 10): keep(i).start()
    run_order(HEAD_ORDER, {"pk": key_values, "ks": keys, "pq": queries, "qs": query_features, "mx": mix, "at": attend}, G.stage, S.stage)
    S.finish()
    G.end(wz, vloc, vout)
    for i in range(KEPT): keep(i).wait()


def head(ns, loc, dp, packed, vloc, tok, rf, vm):
    T, D = tok.shape
    nz = dp // 2
    M = rf.shape[1]
    P_ = D // 128
    shp = grad_shapes(dp, D, packed[0].shape[2], packed[2].shape[2], packed[3].shape[2])
    n = ns * P_ // 4
    pm, pf = (P_, T, 128), (P_, T, 2 * M)
    kept = [(pm, bf)] * 3 + [(pf, bf)] * 2 + [(pm, f32)] * 2 + [((T, D), bf), ((ns, P_, 256, 2 * M), bf), ((T, D), f32), ((T, 128), f32)]
    S = pltpu.SemaphoreType.DMA
    hb = pl.BlockSpec(memory_space=pl.ANY)
    scratch = gather_sems(dp) + [pltpu.VMEM(shp[0], bf), pltpu.VMEM(shp[1], bf), S((2,))] + [pltpu.VMEM(a, t) for a, t in kept] + [S((KEPT,))]
    scratch += [pltpu.VMEM((4, n, 128, M), f32), pltpu.VMEM((4, 8, 2 * M), f32), pltpu.VMEM((4, n, 128, M), bf), pltpu.VMEM((4, 8, 2 * M), f32)]
    scratch += state_scratch(n, M, bf) + [pltpu.VMEM((T, D), f32), pltpu.VMEM((8 * HEAD, 2 * M), bf)]
    return pl.pallas_call(
        partial(head_kernel, ns, loc, nz),
        out_shape=[jax.ShapeDtypeStruct(a, bf) for a in shp[:3]] + [jax.ShapeDtypeStruct((nz - 1, packed[3].shape[2], D), bf), jax.ShapeDtypeStruct((dp,) + vloc.shape, f32)] + [jax.ShapeDtypeStruct(a, t) for a, t in kept],
        in_specs=[hb] * 5 + [VM] * 3, out_specs=[hb] * (5 + KEPT),
        scratch_shapes=scratch,
        name="head",
        compiler_params=pltpu.CompilerParams(collective_id=1, has_side_effects=True, vmem_limit_bytes=ALLV),
    )(*packed, vloc, tok, rf, vm)


def ffn_kernel(nz, part, *refs):
    (shards_, *given, win), wout, refs = refs[:6], refs[6:8 if nz else 7], refs[8 if nz else 7:]
    (gr1, gattn, sums, outh, gwin), refs = refs[:5], refs[5:]
    gwout, refs = refs[:6 if nz else 1], refs[6 if nz else 1:]
    (wi, wu, gwi, gwu, act, gp, hlow, acc, gr2, gffn, tr, n1, inv1, vm, cot, out, lsem, ssem, gsem), sems = refs[:19], refs[19:]
    vec, sems = sems[0], sems[1:]
    sibs, sems = (sems[:2], sems[2:]) if nz else ((), sems)
    J, _, C = act.shape

    def rows(j): return ds(j, C)
    def load(j):
        return pltpu.make_async_copy(win.at[rows(j)], wi.at[rows(j)], lsem.at[j])
    def store(j):
        return pltpu.make_async_copy(gwi.at[rows(j)], gwin.at[rows(j)], ssem.at[j])
    def start_load(j, _):
        load(j).start()
        return 0
    def forward(j, _):
        load(j).wait()
        ffn_chunk(j, hlow, wi, act, gp)
        return 0
    def output(j, _):
        ffn_output(j, act, wu, acc, False)
        return 0
    def out_grad(j, _):
        ffn_out_grad(j, tr, act, gwu)
        return 0
    def backward(j, first):
        ffn_backward(j, gffn, hlow, wi, wu, gp, gwi, acc, first)
        store(j).start()
        return 0
    def some_backward(lo, hi):
        lax.fori_loop(lo, hi, lambda j, _: backward(j, False), 0)
    def end_store(j, _):
        store(j).wait()
        return 0
    here = [pltpu.make_async_copy(a, b, gsem.at[i]) for i, (a, b) in enumerate(zip(given, (n1, inv1, vm, cot)))]
    done_out = pltpu.make_async_copy(out, outh, gsem.at[4])

    def begin():
        for cp in here: cp.start()
        lax.fori_loop(0, J, start_load, 0)
        vec[...] = jnp.concatenate([shards_[d][:, :part] for d in range(shards_.shape[0])], 1)
        for cp in here: cp.wait()
        hidden_rows(n1, vec, hlow)
    if nz:
        wz, loc = wout
        r = loc.shape[2] // 2
        G = Gather(nz, (None, None, None, loc), (None, None, None, wu), sems[2:], r)
        entry_barrier([G.ynb, G.xnb, G.sib])
        G.relay(wz)
        begin()
        lax.fori_loop(0, J // 2, forward, 0)
        G.st2(EARLY)
        lax.fori_loop(J // 2, J - max(1, J // 6), forward, 0)
        G.st2(EARLY + 1)
        for g in (EARLY, EARLY + 1):
            for k in range(1, nz): G._wz_local(wz, g, k).wait()
        G.st3(EARLY)
        lax.fori_loop(J - max(1, J // 6), J, forward, 0)
        G.st3(EARLY + 1)
        G.done(EARLY)
        G.done(EARLY + 1)
    else:
        whole = pltpu.make_async_copy(wout[0], wu, ssem.at[0])
        whole.start()
        begin()
        lax.fori_loop(0, J, forward, 0)
        whole.wait()
    ffn_output(0, act, wu, acc, True)
    lax.fori_loop(1, J, output, 0)
    second_norm(acc, n1, vec, vm, cot, out, gr2, gffn, sums)
    done_out.start()
    tr[...] = gffn[...].T
    lax.fori_loop(0, J, out_grad, 0)
    if nz:
        sc = [()] * EARLY + [(sibs[0], *gwout[1:3]), (sibs[1], *gwout[4:])]
        kept = [pltpu.make_async_copy(sibs[i], gwout[3 * i], gsem.at[5 + i]) for i in range(2)]
        R = Reduce(nz, (None, None, None, gwu), (None,) * NG, sc, sems[:2], None, None, r)
        R.s0(EARLY)
        R.s0(EARLY + 1)
        backward(0, True)
        some_backward(1, J // 4)
        R.s1(EARLY)
        kept[0].start()
        some_backward(J // 4, J // 2)
        R.s1(EARLY + 1)
        kept[1].start()
        some_backward(J // 2, J)
    else:
        backward(0, True)
        some_backward(1, J)
    first_norm_back(acc, gr2, n1, inv1, vec, gr1, gattn, sums)
    if nz:
        for g in (EARLY, EARLY + 1): R.recv1(g)
        G.finish()
        R.finish()
        for cp in kept: cp.wait()
    done_out.wait()
    lax.fori_loop(0, J, end_store, 0)
    if not nz:
        cp = pltpu.make_async_copy(gwu, gwout[0], lsem.at[0])
        cp.start()
        cp.wait()


def ffn(n1, inv1, vec, vm, cot, win, wout, dp=0):
    T, D = n1.shape
    FF = win.shape[0]
    J = FF // COLS
    nz = dp // 2
    hb = pl.BlockSpec(memory_space=pl.ANY)
    S = pltpu.SemaphoreType.DMA
    ws, us, ch = (FF, D), (FF // D, D, D), (J, T, COLS)
    gs = (2, 2, dp, D // dp, D) if dp else us
    part_sums = [a for g in (EARLY, EARLY + 1) for a in reduce_shapes(nz, D, D // dp // 2, g)[:3]] if dp else [us]
    outs = [((T, D), f32), ((T, D), bf), ((4, 8, D), f32), ((T, D), bf), (ws, bf)] + [(a, bf) for a in part_sums]
    scratch = [(ws, bf), (gs, bf), (ws, bf), (gs, bf), (ch, bf), (ch, bf), ((T, D), bf), ((T, D), f32), ((T, D), f32), ((T, D), bf), ((D, T), bf)]
    scratch += [(n1.shape, f32), (inv1.shape, f32), (vm.shape, f32), ((T, D), bf), ((T, D), bf)]
    sems = [pltpu.VMEM(part_sums[0], bf)] * 2 + [S((NG, 2 * nz + 7)), S((NG, 2 * nz + 7))] + gather_sems(dp) if dp else []
    remote = dict(collective_id=3, has_side_effects=True) if dp else {}
    return pl.pallas_call(
        partial(ffn_kernel, nz, D // vec.shape[0]),
        out_shape=[jax.ShapeDtypeStruct(a, t) for a, t in outs],
        in_specs=[VM] + [hb] * (5 + len(wout)), out_specs=[VM] * 3 + [hb] * 2 + ([hb, VM, VM] * 2 if dp else [hb]),
        scratch_shapes=[pltpu.VMEM(a, t) for a, t in scratch] + [S((J,)), S((J,)), S((7,)), pltpu.VMEM((8, D), f32)] + sems,
        name="ffn",
        compiler_params=pltpu.CompilerParams(vmem_limit_bytes=ALLV, **remote),
    )(vec, n1, inv1, vm, cot, win, *wout)


def mix_back_kernel(ns, loc, gattn, qow, ctxb, ctx, den, qp, qf, right, fbm, tok, gqo, gq, gst, gkt, tr):
    tr[...] = gattn[...].T
    weight_grad(tr, ctxb, gqo.at[1])
    mix_back_query(gattn, qow.at[1], qp, qf, right, ctx, den, fbm, gst, gkt, gq, ns, loc)
    weight_grad_pairs(gq, tok, gqo.at[0])


LATE = 11
TAIL_ORDER = (
    "wu1.2", "mq", "s.0", "gq", "wi0.0", "wo", "wu1.3", "wu0.2", "wi1.0", "wi0.1", "qo.0", "tq",
    "s.1", "wi1.1", "qo.1", "s.2", "mk", "wu0.3", "gkv", "kv.0", "wi1.2", "qo.2", "kv.1", "wi0.2",
    "wi1.3", "wu0.4", "qo.3", "kv.2", "wi1.4", "wu1.4", "wi0.3", "kv.3", "wu0.5", "qo.4", "wu1.5", "wi0.4",
    "wi1.5", "wi0.5", "wu0.6", "wu1.6", "kv.4", "qo.5", "wi1.6", "tk", "kv.5", "wi0.6", "kv.6", "qo.6",
)


def tail_kernel(ns, loc, nz, *refs):
    (gattn, ctxb, sums, rf), refs = refs[:4], refs[4:]
    (gwin, gr1, *part_sums), refs = refs[:8], refs[8:]
    late, refs = refs[:LATE], refs[LATE:]
    tg, fins, sout, refs = refs[0], refs[1:5], refs[5], refs[6:]
    there, lsem, refs = refs[:LATE], refs[LATE], refs[LATE + 1:]
    (gkv, gqo, *own, gq, gk, gv, tr, gst, gkt, sto, kto), refs = refs[:12], refs[12:]
    (sb, srec, krec, ss, sr), refs = refs[:5], refs[5:]
    scratch, refs = [refs[g * 7:(g + 1) * 7] for g in range(NG)], refs[7 * NG:]
    rsend, rrecv, osem, sfirst, ssecond, qsend, qrecv, ssrc, fbm = refs
    qow, qp, qf, right, ctx, den, tok, kp, vp, kf, kvw = there
    P_ = gq.shape[0]
    n = ns * P_ // 4

    def load(i):
        return pltpu.make_async_copy(late[i], there[i], lsem.at[i])
    grl = pltpu.make_async_copy(gr1, tg, lsem.at[LATE])
    early = [pltpu.make_async_copy(part_sums[i], scratch[EARLY + i // 3][i % 3], lsem.at[LATE + 1 + i]) for i in range(6)]
    for cp in early: cp.start()
    for i in range(LATE): load(i).start()
    grl.start()
    R = Reduce(nz, (gkv, gqo, gwin, None), (None, None, *own, None, None), scratch, (rsend, rrecv), osem, fins, gkv.shape[3])
    Q = SmallSum(nz, ssrc, sout, sfirst, ssecond, (qsend, qrecv))
    S = StateSum(gst, gkt, sto, kto, sb, srec, krec, (ss, sr))
    entry_barrier(S.peers + Q.dpeer)
    ssrc[...] = jnp.zeros_like(ssrc)
    for i in range(4):
        ssrc[i:i + 1, :] = jnp.sum(sums[i], 0, keepdims=True)
    Q.t0()
    fbm[...] = feature_pull(rf[...])
    wait_for = iter(range(LATE))

    def need(n):
        for _ in range(n): load(next(wait_for)).wait()

    def output_grad():
        tr[...] = gattn[...].T
        weight_grad_units(tr, ctxb, gqo.at[1])

    def mix_query():
        need(7)
        gkt[...] = jnp.zeros_like(gkt)
        mix_back_query(gattn, qow.at[1], qp, qf, right, ctx, den, fbm, Flat(gst, P_), FlatRow(gkt, P_, n), gq, ns, loc)

    def query_token():
        grl.wait()
        token_grad_query(gq, qow.at[0], tg)

    def mix_key():
        need(4)
        mix_back_key(kp, vp, kf, Flat(sto, P_), FlatRow(kto, P_, n), fbm, gk, gv, ns, loc)

    def key_grads():
        weight_grad_pairs_units(gk, tok, gkv.at[0])
        weight_grad_pairs_units(gv, tok, gkv.at[1])
        Q.t1()
    compute = {
        "wo": output_grad, "mq": mix_query, "gq": lambda: weight_grad_pairs_units(gq, tok, gqo.at[0]), "tq": query_token, "mk": mix_key,
        "gkv": key_grads, "tk": lambda: token_grad_keys(gk, gv, kvw.at[0], kvw.at[1], tg),
    }

    def stage(g, i):
        if g >= EARLY and i == 2:
            for cp in early[(g - EARLY) * 3:(g - EARLY) * 3 + 3]: cp.wait()
        R.stage(g, i)
    run_order(TAIL_ORDER, compute, stage, S.stage)
    Q.t2()
    S.finish()
    Q.finish()
    R.finish()


def tail(ns, loc, dp, gattn, ctxb, sums, rf, gwin, gr1, part_sums, late):
    T, D = gattn.shape
    nz = dp // 2
    qf = late[2]
    P_, M = qf.shape[0], qf.shape[2] // 2
    part, ff = D // dp, gwin.shape[0]
    rows = (part // 2, part // 2, ff // dp // 4, part)
    shp = grad_shapes(dp, D, rows[0], rows[2], rows[3])
    n = ns * P_ // 4
    S = pltpu.SemaphoreType.DMA
    pm = pltpu.VMEM((P_, T, 128), bf)
    scratch = [pltpu.VMEM(a.shape, a.dtype) for a in late] + [S((LATE + 7,))]
    scratch += [pltpu.VMEM(shp[0], bf), pltpu.VMEM(shp[1], bf)] + [pltpu.VMEM((nz, 2, 2, rows[0], D), bf)] * 2
    scratch += [pm, pm, pm, pltpu.VMEM((D, T), bf), pltpu.VMEM((4, n, 128, M), f32), pltpu.VMEM((4, 8, 2 * M), f32)]
    scratch += [pltpu.VMEM((4, n, 128, M), bf), pltpu.VMEM((4, 8, 2 * M), f32)] + state_scratch(n, M, bf)
    scratch += [pltpu.VMEM(a, bf) for g in range(NG) for a in reduce_shapes(nz, D, rows[0], g)] + [S((NG, 2 * nz + 7)), S((NG, 2 * nz + 7)), S((NG, nz))] + small_scratch(dp, D) + [pltpu.VMEM((2 * M, 4 * HEAD), bf)]
    hb = pl.BlockSpec(memory_space=pl.ANY)
    return pl.pallas_call(
        partial(tail_kernel, ns, loc, nz),
        out_shape=[jax.ShapeDtypeStruct((T, D), f32)] + [jax.ShapeDtypeStruct((2, 2, r, D), bf) for r in rows] + [jax.ShapeDtypeStruct((8, D), f32)],
        in_specs=[VM] * 4 + [hb] * (8 + LATE), out_specs=[VM] * 6,
        scratch_shapes=scratch,
        name="tail",
        compiler_params=pltpu.CompilerParams(collective_id=2, has_side_effects=True, vmem_limit_bytes=ALLV),
    )(gattn, ctxb, sums, rf, gwin.reshape(shp[2]), gr1, *part_sums, *late)


def last_kernel(ns, loc, kp, vp, kf, gst, gkt, fbm, gr1, gq, kvw, qow, tok, gkv, tg, gk, gv):
    mix_back_key(kp, vp, kf, gst, gkt, fbm, gk, gv, ns, loc)
    weight_grad_pairs(gk, tok, gkv.at[0])
    weight_grad_pairs(gv, tok, gkv.at[1])
    token_grad(gr1, gq, gk, gv, qow.at[0], kvw.at[0], kvw.at[1], tg)


def shards(tokens, lengths, random_features, w_query, w_key, w_value, w_output, w_in, w_out, ln1_gain, ln1_bias, ln2_gain, ln2_bias, cotangent):
    ns, loc, D = tokens.shape
    T = ns * loc
    dp, parts = lax.axis_size("dp"), lax.axis_size("seq")
    part = w_query.shape[1]
    FF = w_out.shape[0]
    M = random_features.shape[1]
    P_ = D // 128
    fast = parts == 4 and dp == 8 and part % 32 == 0 and D == part * dp and part <= 128 and ns * P_ % 4 == 0 and ns * P_ <= 32 and FF == 4 * D
    pos = lax.axis_index("seq") * loc + jnp.arange(loc, dtype=jnp.int32)
    valid = (pos[None, :] < lengths[:, None]).astype(f32).reshape(T, 1)
    vm = jnp.broadcast_to(valid, (T, 128))
    tok, cot = tokens.reshape(T, D), cotangent.reshape(T, D)
    vloc = jnp.stack([ln1_gain, ln1_bias, ln2_gain, ln2_bias]).astype(f32)
    pm, pf, stt, ktt = (P_, T, 128), (P_, T, 2 * M), (ns, P_, 128, M), (ns, P_, 8, 2 * M)
    if fast:
        vloc = jnp.pad(vloc, ((0, 4), (0, 128 - part)))
        packed = pack(w_query, w_key, w_value, w_output, w_in, w_out)
        kvw, qow, win, wz, vec, *kept = head(ns, loc, dp, packed, vloc, tok, random_features, vm)
        wout = wz, packed[3]
        kp, vp, qp, kf, qf, ctx, den, ctxb, right, n1, inv1 = kept
    else:
        vec = jnp.pad(lax.all_gather(vloc, "dp", axis=1, tiled=True), ((0, 4), (0, 0)))[None]
        def full(w):
            return lax.all_gather(w, "dp", axis=1, tiled=True).T
        kvw, qow = jnp.stack([full(w_key), full(w_value)]), jnp.stack([full(w_query), full(w_output)])
        win = full(w_in)
        wout = (jnp.transpose(full(w_out).reshape(D, FF // D, D), (1, 0, 2)),)
    kvw, qow, win = kvw.reshape(2, D, D), qow.reshape(2, D, D), win.reshape(FF, D)
    if not fast:
        wf, fbm = feature_matrix(random_features), feature_pull(random_features)
        kp, vp, qp, kf, qf, st, kt = call(
            partial(key_query_kernel, ns, loc), (tok, kvw, qow, wf, vm),
            [(pm, bf)] * 3 + [(pf, bf)] * 2 + [(stt, f32), (ktt, f32)], name="key_query")
        st, kt = lax.psum((st, kt), "seq")
        ctx, den, ctxb, right, n1, inv1 = call(
            partial(mix_kernel, ns, loc), (tok, qow, qf, st, kt),
            [(pm, f32), (pm, f32), ((T, D), bf), ((ns, P_, 256, 2 * M), bf), ((T, D), f32), ((T, 128), f32)],
            [pltpu.VMEM((T, D), f32)], name="mix")
    gr1, gattn, sums, out, gwin, *gwout = ffn(n1, inv1, vec, vm, cot, win, wout, dp if fast else 0)
    if fast:
        tg, kvg, qog, wig, wug, small = tail(ns, loc, dp, gattn, ctxb, sums, random_features, gwin, gr1, gwout, (qow, qp, qf, right, ctx, den, tok, kp, vp, kf, kvw))
        wk_g, wv_g, wq_g, wo_g = kvg[0].reshape(part, D).T, kvg[1].reshape(part, D).T, qog[0].reshape(part, D).T, qog[1].reshape(part, D).T
        wi_g = wig.reshape(FF // dp, D).T
        wu_g = jnp.transpose(wug.reshape(FF // D, part, D), (0, 2, 1)).reshape(FF, part)
        grads = (wq_g, wk_g, wv_g, wo_g, wi_g, wu_g)
    else:
        gqo, gq, gst, gkt = call(
            partial(mix_back_kernel, ns, loc), (gattn, qow, ctxb, ctx, den, qp, qf, right, fbm, tok),
            [((2, D, D), bf), (pm, bf), (stt, f32), (ktt, f32)], [pltpu.VMEM((D, T), bf)], name="mix_back")
        gst, gkt = lax.psum((gst, gkt), "seq")
        gkv, tg = call(
            partial(last_kernel, ns, loc), (kp, vp, kf, gst, gkt, fbm, gr1, gq, kvw, qow, tok),
            [((2, D, D), bf), ((T, D), f32)], [pltpu.VMEM(pm, bf), pltpu.VMEM(pm, bf)], name="last")
        small = lax.psum(jnp.sum(sums, 1), ("seq", "dp"))
        whole = (gqo[0].T, gkv[0].T, gkv[1].T, gqo[1].T, gwin.T, jnp.transpose(gwout[0], (0, 2, 1)).reshape(FF, D))
        grads = tuple(lax.psum(lax.psum_scatter(g, "dp", scatter_dimension=1, tiled=True), "seq") for g in whole)
    small = lax.dynamic_slice_in_dim(small, lax.axis_index("dp") * part, part, 1)
    return (out.reshape(tokens.shape), tg.reshape(tokens.shape), *(g.astype(f32) for g in grads), small[2], small[3], small[0], small[1])


def solution(mesh):
    rows, cols, vecs = P("dp", "seq", None), P(None, "dp"), P("dp")
    return jax.shard_map(
        shards,
        mesh=mesh,
        in_specs=(rows, vecs, P(), *([cols] * 6), *([vecs] * 4), rows),
        out_specs=(rows, rows, *([cols] * 6), *([vecs] * 4)),
        check_vma=False,
    )
```
